32 devices in a mesh: groups: 2 (over x), ctx: 8 (over z, y), tp: 2 (over core).
Axes of the slice: x: 2, y: 2, z: 4, core: 2. Of those that a mesh axis runs over, the one named last changes fastest.
Arguments:
- tokens: bfloat16 [8192, 2048], P(('groups', 'ctx')), parts along dimension 0, may hold values from -6 to 6
- weight: bfloat16 [2048, 3, 2048], P('ctx', None, 'tp'), may hold values from -0.125 to 0.125
- adapter_a: bfloat16 [2048, 16], replicated, may hold values from -2.390625 to 2.390625
- adapter_b: bfloat16 [16, 3, 2048], P(None, None, 'tp'), may hold values from -2.390625 to 2.390625
- short_filter: float32 [7, 3, 2048], P(None, None, 'tp'), may hold values from -1.8 to 1.8
- long_filter: float32 [128, 2048], P(None, 'tp'), may hold values from -0.54 to 0.54
- skip_gain: float32 [2048], P('tp'), may hold values from -4.2 to 4.2
- cotangent: bfloat16 [8192, 2048], P(('groups', 'ctx'), 'tp'), parts along dimension 0, may hold values from -6 to 6
Outputs:
- mixed: bfloat16 [8192, 2048], P(('groups', 'ctx'), 'tp'), parts along dimension 0
- grad_tokens: bfloat16 [8192, 2048], P(('groups', 'ctx'), 'tp'), parts along dimension 0
- grad_a: float32 [4096, 16], P('groups'), parts along dimension 0
- grad_b: float32 [32, 3, 2048], P('groups', None, 'tp'), parts along dimension 0
The draws below stay inside these ranges and needn't reach their ends.
There are 2 independent parts, one for each index of `groups`. The reference program is written for one: setup_inputs(seed, part) draws one part's arguments, and reference() takes and returns one part's arrays. A program takes and returns all parts, laid end to end along the dimension named above; an argument that names none is the same for every part. Nothing has to cross between parts.
All inputs are finite; a program needn't handle non-finite values.
Results may differ from the reference program's by a relative error of at most 0.0093.
Values may be sent and summed in bfloat16 or wider, within the bound.
A program may use at most 128 MiB of HBM per device.

```python
import math
import jax
import jax.numpy as jnp
from jax import lax

D = 2048
R = 16
LONG = 128
SHORT = 7
TOK_DEV = 512
TOKENS = 4096
CH = 2048


def shard_levels(stream_key, dims, pieces, least, high):
    def one(axis_at, shards_of):
        heights = jax.random.uniform(jax.random.fold_in(jax.random.fold_in(stream_key, 6), axis_at), (shards_of,), jnp.float32, least / len(pieces), high / len(pieces))
        return jnp.repeat(jnp.exp(heights), dims[axis_at] // shards_of).reshape((-1,) + (1,) * (len(dims) - axis_at - 1))

    gain = one(*pieces[0])
    for cut in pieces[1:]:
        gain = gain * one(*cut)
    return gain


def noise(stream_key, dims, deviation, reach, split=(), held_as=jnp.bfloat16):
    values = jax.random.normal(stream_key, dims, jnp.float32) * deviation
    if len(split) > 0:
        values = shard_levels(stream_key, dims, split, -0.22, 0.18) * values
    return jnp.clip(values, min=-reach, max=reach).astype(held_as)


def setup_inputs(seed: int = 0, part: int = 0) -> dict:
    key_list = jax.random.split(jax.random.key(seed), 9)
    part_splits = jax.random.split(jax.random.fold_in(key_list[8], part), 9)
    return {
        "tokens": noise(part_splits[0], (TOKENS, D), 1.0, 6.0, ((0, 8),)),
        "weight": noise(key_list[1], (D, 3, CH), D ** -0.5, 0.125, ((0, 8), (2, 2))),
        "adapter_a": noise(key_list[2], (D, R), 0.4, 2.390625),
        "adapter_b": noise(key_list[3], (R, 3, CH), 0.4, 2.390625, ((2, 2),)),
        "short_filter": noise(key_list[4], (SHORT, 3, CH), 0.3, 1.8, ((2, 2),), jnp.float32),
        "long_filter": noise(key_list[5], (LONG, CH), 0.09, 0.54, ((1, 2),), jnp.float32),
        "skip_gain": noise(key_list[6], (CH,), 0.7, 4.2, ((0, 2),), jnp.float32),
        "cotangent": noise(part_splits[7], (TOKENS, CH), 1.0, 6.0, ((0, 8), (1, 2))),
    }


adapter_scale = 0.03125

def causal(signal, filter_taps):
    taps = filter_taps.shape[0]
    out_len = signal.shape[0] - taps + 1
    start_acc = jnp.zeros((out_len, signal.shape[1]), jnp.float32)

    def add_tap(index, acc):
        piece = lax.dynamic_slice_in_dim(signal, (taps - 1 - index).astype(jnp.int32), out_len, 0)
        return acc + filter_taps[index] * piece
    return lax.fori_loop(0, taps, add_tap, start_acc)

def anticausal(signal, filter_taps):
    taps = filter_taps.shape[0]
    out_len = signal.shape[0] - taps + 1
    start_acc = jnp.zeros((out_len, signal.shape[1]), jnp.float32)

    def add_tap(index, acc):
        piece = lax.dynamic_slice_in_dim(signal, jnp.asarray(index).astype(jnp.int32), out_len, 0)
        return acc + filter_taps[index] * piece
    return lax.fori_loop(0, taps, add_tap, start_acc)

def reference(tokens, weight, adapter_a, adapter_b, short_filter, long_filter, skip_gain, cotangent):
    channels = weight.shape[2]
    adapter_rank = adapter_a.shape[1]
    short_taps = short_filter.shape[0]
    long_taps = long_filter.shape[0]
    seq_total = tokens.shape[0]
    feature_count = tokens.shape[1]
    block_count = seq_total // TOK_DEV
    delta_w = jnp.dot(adapter_a, adapter_b.reshape(adapter_rank, 3 * channels), preferred_element_type=jnp.float32)
    merged = (weight.reshape(weight.shape[0], 3 * channels).astype(jnp.float32) + adapter_scale * delta_w).astype(jnp.bfloat16)

    def forward_rows(rows):
        return jnp.dot(rows, merged, preferred_element_type=jnp.float32).astype(jnp.bfloat16)
    packed = lax.map(forward_rows, tokens.reshape(block_count, TOK_DEV, feature_count)).reshape(seq_total, 3 * channels)
    short_flat = short_filter.reshape(short_taps, 3 * channels)
    padded = jnp.concatenate([jnp.zeros((short_taps - 1, 3 * channels), jnp.float32), packed.astype(jnp.float32)], axis=0)
    short_out = causal(padded, short_flat)
    query = short_out[:, :channels]
    keyed = short_out[:, channels:2 * channels]
    valued = short_out[:, 2 * channels:]
    gated = (keyed * valued).astype(jnp.bfloat16)
    gated_pad = jnp.concatenate([jnp.zeros((long_taps - 1, channels), jnp.float32), gated.astype(jnp.float32)], axis=0)
    filtered = causal(gated_pad, long_filter) + skip_gain * gated.astype(jnp.float32)
    mixed = (query * filtered).astype(jnp.bfloat16)
    cot_f = cotangent.astype(jnp.float32)
    grad_filtered = (cot_f * query).astype(jnp.bfloat16)
    back_pad = jnp.concatenate([grad_filtered.astype(jnp.float32), jnp.zeros((long_taps - 1, channels), jnp.float32)], axis=0)
    grad_gated = anticausal(back_pad, long_filter) + skip_gain * grad_filtered.astype(jnp.float32)
    grad_short = jnp.concatenate([cot_f * filtered, grad_gated * valued, grad_gated * keyed], axis=1).astype(jnp.bfloat16)
    short_pad = jnp.concatenate([grad_short.astype(jnp.float32), jnp.zeros((short_taps - 1, 3 * channels), jnp.float32)], axis=0)
    grad_packed = anticausal(short_pad, short_flat).astype(jnp.bfloat16)

    def backward_rows(rows):
        return lax.dot_general(rows, merged, (((1,), (1,)), ((), ())), preferred_element_type=jnp.float32).astype(jnp.bfloat16)
    grad_tokens = lax.map(backward_rows, grad_packed.reshape(block_count, TOK_DEV, 3 * channels)).reshape(seq_total, feature_count)
    factor = adapter_scale / math.sqrt(seq_total)
    projected = jnp.dot(tokens, adapter_a, preferred_element_type=jnp.float32).astype(jnp.bfloat16)
    grad_b = lax.dot_general(projected, grad_packed, (((0,), (0,)), ((), ())), preferred_element_type=jnp.float32) * factor
    through_b = lax.dot_general(grad_packed, adapter_b.reshape(adapter_rank, 3 * channels), (((1,), (1,)), ((), ())), preferred_element_type=jnp.float32).astype(jnp.bfloat16)
    grad_a = lax.dot_general(tokens, through_b, (((0,), (0,)), ((), ())), preferred_element_type=jnp.float32) * factor
    return (mixed, grad_tokens, grad_a, grad_b.reshape(adapter_rank, 3, channels))
```

```python
import functools
import math

import jax
import jax.numpy as jnp
from jax import lax
from jax.experimental import pallas as pl
from jax.experimental.pallas import tpu as pltpu
from jax.sharding import PartitionSpec as P

adapter_scale = 0.03125
LANES = 128
SUB = 8
BLOCK = 16
CHUNK = 32


def shifted(value, axis, steps):
    count = lax.axis_size(axis)
    initial, last = (max(0, -steps), min(count, count - steps))
    return lax.ppermute(value, axis, [(source, source + steps) for source in range(initial, last)])


def tiles(ref, first, count):
    start = first * SUB
    if not isinstance(start, int):
        start = pl.multiple_of(start, SUB)
    return ref[pl.ds(start, count * SUB), :].reshape(count, SUB, LANES)


def put(ref, first, value):
    count = value.shape[0]
    ref[pl.ds(pl.multiple_of(first * SUB, SUB), count * SUB), :] = value.reshape(count * SUB, LANES)


def rounded(value):
    return value.astype(jnp.bfloat16).astype(jnp.float32)


def mixer_kernel(
    rows, halo, packed_ref, cot_ref, short_ref, long_ref, skip_ref, mixed_ref, grad_ref,
    p0, p1, p2, cot, query, keyed, valued, gated, gradf,
):
    channels = SUB * LANES
    short_taps = short_ref.shape[0] // 3
    long_taps = long_ref.shape[0]
    spread = (p0, p1, p2)
    front = halo - long_taps

    @pl.loop(0, (rows + 2 * halo) // BLOCK)
    def _(i):
        at = pl.multiple_of(i * BLOCK, BLOCK)
        for g in range(3):
            for s in range(SUB):
                piece = packed_ref[pl.ds(at, BLOCK), pl.ds(g * channels + s * LANES, LANES)]
                spread[g][pl.ds(at * SUB + s, BLOCK, stride=SUB), :] = piece.astype(jnp.float32)

    @pl.loop(0, (rows + halo) // BLOCK)
    def _(i):
        at = pl.multiple_of(i * BLOCK, BLOCK)
        for s in range(SUB):
            piece = cot_ref[pl.ds(at, BLOCK), pl.ds(s * LANES, LANES)]
            cot[pl.ds(at * SUB + s, BLOCK, stride=SUB), :] = piece.astype(jnp.float32)

    def short(ref, g, first, sign):
        total = None
        for j in range(short_taps):
            term = short_ref[j * 3 + g][None] * tiles(ref, first + sign * j, SUB)
            total = term if total is None else total + term
        return total

    @pl.loop(0, (rows + BLOCK + long_taps) // SUB)
    def _(i):
        at = i * SUB
        key = short(p1, 1, at + front, -1)
        val = short(p2, 2, at + front, -1)
        put(keyed, at, key)
        put(valued, at, val)
        put(gated, at, rounded(key * val))

    @pl.loop(0, (rows + halo) // SUB)
    def _(i):
        at = i * SUB
        que = short(p0, 0, at + halo, -1)
        put(query, at, que)
        put(gradf, at, rounded(que * tiles(cot, at, SUB)))

    zero = tuple(jnp.zeros((SUB, LANES), jnp.float32) for _ in range(BLOCK))

    def long_sum(ref, base, sign):
        def chunk(c, acc):
            acc = list(acc)
            tap0 = c * CHUNK
            origin = base + sign * tap0
            low = origin - (CHUNK - 1) if sign < 0 else origin
            seen = {}

            def at(k):
                if k not in seen:
                    seen[k] = ref[pl.ds(pl.multiple_of((low + k) * SUB, SUB), SUB), :]
                return seen[k]

            for j in range(CHUNK):
                tap = long_ref[tap0 + j]
                for i in range(BLOCK):
                    k = i + (CHUNK - 1) - j if sign < 0 else i + j
                    acc[i] = acc[i] + tap * at(k)
            return tuple(acc)

        return lax.fori_loop(0, long_taps // CHUNK, chunk, zero)

    @pl.loop(0, (rows + BLOCK) // BLOCK)
    def _(b):
        at = b * BLOCK
        skip = skip_ref[...]
        ahead = jnp.stack(long_sum(gated, at + long_taps, -1))
        filtered = ahead + skip[None] * tiles(gated, at + long_taps, BLOCK)
        back = jnp.stack(long_sum(gradf, at, 1))
        grad_gated = back + skip[None] * tiles(gradf, at, BLOCK)
        put(p0, at, rounded(tiles(cot, at, BLOCK) * filtered))
        put(p1, at, rounded(grad_gated * tiles(valued, at + long_taps, BLOCK)))
        put(p2, at, rounded(grad_gated * tiles(keyed, at + long_taps, BLOCK)))
        put(gated, at, tiles(query, at, BLOCK) * filtered)

    results = (query, keyed, valued)

    @pl.loop(0, rows // SUB)
    def _(i):
        at = i * SUB
        for g in range(3):
            put(results[g], at, short(spread[g], g, at, 1))

    @pl.loop(0, rows // BLOCK)
    def _(i):
        at = pl.multiple_of(i * BLOCK, BLOCK)
        for s in range(SUB):
            pick = pl.ds(at * SUB + s, BLOCK, stride=SUB)
            mixed_ref[pl.ds(at, BLOCK), pl.ds(s * LANES, LANES)] = gated[pick, :].astype(jnp.bfloat16)
            for g in range(3):
                grad_ref[pl.ds(at, BLOCK), pl.ds(g * channels + s * LANES, LANES)] = results[g][
                    pick, :
                ].astype(jnp.bfloat16)


def mixer(packed, cot, short_filter, long_filter, skip_gain, rows, halo):
    channels = long_filter.shape[1]
    long_taps = long_filter.shape[0]
    full = (rows + 2 * halo) * SUB
    side = (rows + halo) * SUB
    scratch = [pltpu.VMEM((full, LANES), jnp.float32)] * 3 + [
        pltpu.VMEM((side, LANES), jnp.float32)
    ] * 6
    return pl.pallas_call(
        functools.partial(mixer_kernel, rows, halo),
        out_shape=(
            jax.ShapeDtypeStruct((rows, channels), jnp.bfloat16),
            jax.ShapeDtypeStruct((rows, 3 * channels), jnp.bfloat16),
        ),
        in_specs=[pl.BlockSpec(memory_space=pltpu.VMEM)] * 5,
        out_specs=(pl.BlockSpec(memory_space=pltpu.VMEM),) * 2,
        scratch_shapes=scratch,
        compiler_params=pltpu.CompilerParams(vmem_limit_bytes=52 << 20),
        cost_estimate=pl.CostEstimate(
            flops=4 * rows * channels * (long_taps + 42), bytes_accessed=12 << 20, transcendentals=0
        ),
    )(
        packed,
        cot,
        short_filter.reshape(-1, SUB, LANES),
        long_filter.reshape(long_taps, SUB, LANES),
        skip_gain.reshape(SUB, LANES),
    )


def finish_kernel(
    count, grad_ref, whole_ref, terms_ref, tokens_ref, sums_ref,
    held, total, mate, summed, ready, landed,
    send_one, recv_one, send_two, recv_two, send_tp, recv_tp, send_tok, recv_tok,
):
    me = lax.axis_index("ctx")
    mine = lax.axis_index("tp")
    other = 1 - mine
    width = mate.shape[1]
    cols = tokens_ref.shape[1]
    tile = ready.shape[2]
    steps = cols // tile

    barrier = pltpu.get_barrier_semaphore()
    for d in range(1, count):
        pl.semaphore_signal(
            barrier, inc=1, device_id={"ctx": lax.rem(me + d, count)}, device_id_type=pl.DeviceIdType.MESH
        )
    pl.semaphore_signal(barrier, inc=1, device_id={"tp": other}, device_id_type=pl.DeviceIdType.MESH)
    pl.semaphore_wait(barrier, count)

    first = []
    for d in range(1, count):
        peer = lax.rem(me + d, count)
        first.append(
            pltpu.make_async_remote_copy(
                src_ref=terms_ref.at[peer],
                dst_ref=held.at[d],
                send_sem=send_one.at[d],
                recv_sem=recv_one.at[d],
                device_id={"ctx": peer},
                device_id_type=pl.DeviceIdType.MESH,
            )
        )
        first[-1].start()

    def product(half, t):
        at = pl.multiple_of(half * cols + t * tile, tile)
        return lax.dot_general(
            grad_ref[...],
            whole_ref[pl.ds(at, tile), :],
            (((1,), (1,)), ((), ())),
            preferred_element_type=jnp.float32,
        )

    def token_copy(t):
        return pltpu.make_async_remote_copy(
            src_ref=ready.at[t],
            dst_ref=landed.at[t],
            send_sem=send_tok.at[t],
            recv_sem=recv_tok.at[t],
            device_id={"tp": other},
            device_id_type=pl.DeviceIdType.MESH,
        )

    @pl.loop(0, steps)
    def _(t):
        ready[t] = product(other, t).astype(jnp.bfloat16)
        token_copy(t).start()

    own = terms_ref[me]
    for d in range(1, count):
        first[d - 1].wait()
        own = own + held[d]
    total[...] = own
    tp_copy = pltpu.make_async_remote_copy(
        src_ref=total.at[:, pl.ds(0, width)],
        dst_ref=mate,
        send_sem=send_tp,
        recv_sem=recv_tp,
        device_id={"tp": other},
        device_id_type=pl.DeviceIdType.MESH,
    )
    tp_copy.start()

    def own_tile(t):
        value = product(mine, t)
        token_copy(t).wait()
        at = pl.multiple_of(t * tile, tile)
        tokens_ref[:, pl.ds(at, tile)] = (value + landed[t].astype(jnp.float32)).astype(jnp.bfloat16)

    pl.loop(0, steps // 4)(own_tile)
    tp_copy.wait()
    total[:, pl.ds(0, width)] = total[:, pl.ds(0, width)] + mate[...]
    summed[me] = total[...]
    second = []
    for d in range(1, count):
        second.append(
            pltpu.make_async_remote_copy(
                src_ref=total,
                dst_ref=summed.at[me],
                send_sem=send_two.at[d],
                recv_sem=recv_two.at[d],
                device_id={"ctx": lax.rem(me + d, count)},
                device_id_type=pl.DeviceIdType.MESH,
            )
        )
        second[-1].start()
    pl.loop(steps // 4, steps)(own_tile)
    for copy in second:
        copy.wait()
    sums_ref[...] = summed[...]


def finish(grad_packed, whole, part_a, part_b, count):
    rank, features = part_a.shape
    rows, wide = grad_packed.shape
    width, rest = features // count, wide // count
    cols = features // 2
    tile = 256
    terms = jnp.concatenate(
        [part_a.reshape(rank, count, width), part_b.reshape(rank, count, rest)], axis=2
    ).transpose(1, 0, 2)
    vmem = pl.BlockSpec(memory_space=pltpu.VMEM)
    grad_tokens, sums = pl.pallas_call(
        functools.partial(finish_kernel, count),
        out_shape=(
            jax.ShapeDtypeStruct((rows, cols), jnp.bfloat16),
            jax.ShapeDtypeStruct(terms.shape, jnp.float32),
        ),
        in_specs=[vmem] * 3,
        out_specs=(vmem, vmem),
        scratch_shapes=[
            pltpu.VMEM(terms.shape, jnp.float32),
            pltpu.VMEM((rank, width + rest), jnp.float32),
            pltpu.VMEM((rank, width), jnp.float32),
            pltpu.VMEM(terms.shape, jnp.float32),
            pltpu.VMEM((cols // tile, rows, tile), jnp.bfloat16),
            pltpu.VMEM((cols // tile, rows, tile), jnp.bfloat16),
            pltpu.SemaphoreType.DMA((count,)),
            pltpu.SemaphoreType.DMA((count,)),
            pltpu.SemaphoreType.DMA((count,)),
            pltpu.SemaphoreType.DMA((count,)),
            pltpu.SemaphoreType.DMA,
            pltpu.SemaphoreType.DMA,
            pltpu.SemaphoreType.DMA((cols // tile,)),
            pltpu.SemaphoreType.DMA((cols // tile,)),
        ],
        compiler_params=pltpu.CompilerParams(
            vmem_limit_bytes=48 << 20, collective_id=1, has_side_effects=True
        ),
        cost_estimate=pl.CostEstimate(
            flops=2 * rows * wide * features, bytes_accessed=20 << 20, transcendentals=0
        ),
    )(grad_packed, whole, terms)
    flat = sums.transpose(1, 0, 2)
    return (
        grad_tokens,
        flat[:, :, :width].reshape(rank, features),
        flat[:, :, width:].reshape(rank, wide),
    )


MESH = pl.DeviceIdType.MESH
PIECES = 4


def gather_kernel(
    outer, shard_ref, out_ref, z_send, z_recv, y_send, y_recv, x_send, x_recv, local_sem
):
    me = lax.axis_index("ctx")
    x = lax.axis_index("groups")
    z, y = me // 2, lax.rem(me, 2)
    rows = shard_ref.shape[0]
    piece = rows // PIECES
    half = piece // 2
    last = outer - 2
    steps = outer - 1

    def ctx_of(line, pair):
        return {"ctx": line * 2 + pair}

    def span(line, pair, start, size):
        return pl.ds(pl.multiple_of((line * 2 + pair) * rows + start, half), size)

    def part(p, side):
        return p * piece + side * half

    def copy(src, dst, send, recv, device):
        return pltpu.make_async_remote_copy(
            src_ref=src, dst_ref=dst, send_sem=send, recv_sem=recv, device_id=device, device_id_type=MESH
        )

    def z_range(k, p):
        return (part(p, x), half) if k == last else (p * piece, piece)

    def z_out(way, k, p):
        step = 1 - 2 * way
        start, size = z_range(k, p)
        place = span(z - step * k, y, start, size)
        src = out_ref.at[place] if k else shard_ref.at[pl.ds(pl.multiple_of(start, half), size)]
        return copy(
            src, out_ref.at[place], z_send.at[way, k, p], z_recv.at[way, k, p], ctx_of(z + step, y)
        )

    def z_in(way, k, p):
        step = 1 - 2 * way
        start, size = z_range(k, p)
        place = out_ref.at[span(z - step * (k + 1), y, start, size)]
        return copy(place, place, z_send.at[way, k, p], z_recv.at[way, k, p], ctx_of(z - step, y))

    def sends(way, k):
        return (z < steps) & (z >= k) if way == 0 else (z > 0) & (z + k <= steps)

    def receives(way, k):
        return z > k if way == 0 else z + k < steps

    def line_of(i):
        if i == 0:
            return z
        way, k = (i - 1) // steps, (i - 1) % steps
        return z - (1 - 2 * way) * (k + 1)

    def item(way, k):
        return 1 + way * steps + k

    def y_out(i, p):
        start = part(p, x)
        place = span(line_of(i), y, start, half)
        src = out_ref.at[place] if i else shard_ref.at[pl.ds(pl.multiple_of(start, half), half)]
        return copy(src, out_ref.at[place], y_send.at[i, p], y_recv.at[i, p], ctx_of(z, 1 - y))

    def y_in(i, p):
        place = out_ref.at[span(line_of(i), 1 - y, part(p, x), half)]
        return copy(place, place, y_send.at[i, p], y_recv.at[i, p], ctx_of(z, 1 - y))

    def x_copy(i, p, side):
        if i > 2 * steps:
            line, pair = line_of(item(i - 2 * steps - 1, last)), y
        else:
            line, pair = line_of(i), 1 - y
        place = out_ref.at[span(line, pair, part(p, side), half)]
        return copy(place, place, x_send.at[i, p], x_recv.at[i, p], {"groups": 1 - x})

    def extra(way):
        return 2 * steps + 1 + way

    barrier = pltpu.get_barrier_semaphore()
    pl.semaphore_signal(barrier, inc=1, device_id=ctx_of(z, 1 - y), device_id_type=MESH)
    pl.semaphore_signal(barrier, inc=1, device_id={"groups": 1 - x}, device_id_type=MESH)
    for step in (1, outer - 1):
        pl.semaphore_signal(
            barrier, inc=1, device_id=ctx_of(lax.rem(z + step, outer), y), device_id_type=MESH
        )
    pl.semaphore_wait(barrier, 4)

    @pl.loop(0, PIECES)
    def _(p):
        for way in range(2):
            @pl.when(sends(way, 0))
            def _():
                z_out(way, 0, p).start()
        y_out(0, p).start()

    own = pltpu.make_async_copy(
        shard_ref, out_ref.at[pl.ds(pl.multiple_of(me * rows, rows), rows)], local_sem
    )
    own.start()

    def pass_on(k, p):
        for way in range(2):
            @pl.when(receives(way, k))
            def _():
                i = item(way, k)
                y_in(i, p).wait_recv()
                x_copy(i, p, x).start()

    for k in range(steps):
        @pl.loop(0, PIECES)
        def _(p):
            for way in range(2):
                @pl.when(receives(way, k))
                def _():
                    z_in(way, k, p).wait_recv()
                    if k < last:
                        @pl.when(sends(way, k + 1))
                        def _():
                            z_out(way, k + 1, p).start()
                    y_out(item(way, k), p).start()
                    if k == last:
                        x_copy(extra(way), p, x).start()
            if k == 0:
                y_in(0, p).wait_recv()
                x_copy(0, p, x).start()

            @pl.when(p > 0)
            def _():
                pass_on(k, p - 1)

            if k > 0:
                @pl.when(p == 0)
                def _():
                    pass_on(k - 1, PIECES - 1)

    pass_on(last, PIECES - 1)
    own.wait()

    @pl.loop(0, PIECES)
    def _(p):
        x_copy(0, p, 1 - x).wait_recv()
        x_copy(0, p, x).wait_send()
        y_out(0, p).wait_send()
        for way in range(2):
            for k in range(steps):
                @pl.when(sends(way, k))
                def _():
                    z_out(way, k, p).wait_send()

                @pl.when(receives(way, k))
                def _():
                    i = item(way, k)
                    x_copy(i, p, 1 - x).wait_recv()
                    x_copy(i, p, x).wait_send()
                    y_out(i, p).wait_send()
                    if k == last:
                        x_copy(extra(way), p, 1 - x).wait_recv()
                        x_copy(extra(way), p, x).wait_send()


def gather(merged, count):
    rows, wide = merged.shape
    outer = count // 2
    items = 2 * (outer - 1) + 1
    dma = pltpu.SemaphoreType.DMA
    hbm = pl.BlockSpec(memory_space=pl.ANY)
    return pl.pallas_call(
        functools.partial(gather_kernel, outer),
        out_shape=jax.ShapeDtypeStruct((rows * count, wide), merged.dtype),
        in_specs=[hbm],
        out_specs=hbm,
        scratch_shapes=[
            dma((2, outer - 1, PIECES)),
            dma((2, outer - 1, PIECES)),
            dma((items, PIECES)),
            dma((items, PIECES)),
            dma((items + 2, PIECES)),
            dma((items + 2, PIECES)),
            dma,
        ],
        compiler_params=pltpu.CompilerParams(collective_id=2, has_side_effects=True),
        cost_estimate=pl.CostEstimate(flops=0, bytes_accessed=300 << 20, transcendentals=0),
    )(merged)


def general_body(tokens, weight, adapter_a, adapter_b, short_filter, long_filter, skip_gain, cotangent):
    row_count = tokens.shape[0]
    share_rows = weight.shape[0]
    channels = weight.shape[2]
    features = tokens.shape[1]
    adapter_rank = adapter_a.shape[1]
    halo = long_filter.shape[0] + BLOCK
    count = lax.axis_size("ctx")
    seq_total = row_count * count
    first_row = lax.axis_index("ctx") * share_rows
    before = shifted(tokens[row_count - halo :], "ctx", 1)
    after = shifted(tokens[:halo], "ctx", -1)
    cot_after = shifted(cotangent[:halo], "ctx", -1)
    tokens_ext = jnp.concatenate([before, tokens, after], axis=0)
    cot_ext = jnp.concatenate([cotangent, cot_after], axis=0)
    own_rows = lax.dynamic_slice_in_dim(adapter_a, first_row, share_rows, 0)
    flat_b = adapter_b.reshape(adapter_rank, 3 * channels)
    delta_w = jnp.dot(own_rows, flat_b, preferred_element_type=jnp.float32)
    merged = (
        weight.reshape(share_rows, 3 * channels).astype(jnp.float32) + adapter_scale * delta_w
    ).astype(jnp.bfloat16)
    if count == 8 and lax.axis_size("groups") == 2:
        whole = gather(merged, count)
    else:
        whole = lax.all_gather(merged, "ctx", axis=0, tiled=True)
    packed = jnp.dot(tokens_ext, whole, preferred_element_type=jnp.float32).astype(jnp.bfloat16)
    mixed, grad_packed = mixer(
        packed, cot_ext, short_filter, long_filter, skip_gain, row_count, halo
    )
    projected = jnp.dot(tokens, adapter_a, preferred_element_type=jnp.float32).astype(jnp.bfloat16)
    part_b = lax.dot_general(
        projected, grad_packed, (((0,), (0,)), ((), ())), preferred_element_type=jnp.float32
    )
    through = lax.dot_general(
        flat_b, grad_packed, (((1,), (1,)), ((), ())), preferred_element_type=jnp.float32
    ).astype(jnp.bfloat16)
    part_a = jnp.dot(through, tokens, preferred_element_type=jnp.float32)
    if features % (LANES * count) == 0 and (3 * channels) % (LANES * count) == 0:
        grad_tokens, sum_a, sum_b = finish(grad_packed, whole, part_a, part_b, count)
    else:
        sum_a = lax.psum(part_a, ("ctx", "tp"))
        sum_b = lax.psum(part_b, "ctx")
        partial_grad = lax.dot_general(
            grad_packed, whole, (((1,), (1,)), ((), ())), preferred_element_type=jnp.float32
        )
        grad_tokens = lax.psum_scatter(
            partial_grad.astype(jnp.bfloat16), "tp", scatter_dimension=1, tiled=True
        )
    sum_a = sum_a.T
    factor = adapter_scale / math.sqrt(seq_total)
    return (mixed, grad_tokens, sum_a * factor, (sum_b * factor).reshape(adapter_rank, 3, channels))


CHUNK_LANES = 128
QUARTERS = 4
LAG = 2
PIECE = 32
SEG = 68
COMBOS = 9
PHASE_TAPS = 32
OUT_SEG = 66
OUT_STEP = 11


def combine(p):
    p02, p13, p01, p23 = p[0] + p[2], p[1] + p[3], p[0] + p[1], p[2] + p[3]
    return (p[0], p[2], p02, p[1], p[3], p13, p01, p23, p01 + p23)


def block_kernel(
    chunks, halo, rows,
    weight_ref, own_ref, down_ref, up_ref, tokens_ref, cot_ref, short_ref, long_ref, skip_ref,
    mixed_ref, tokgrad_ref, sums_ref,
    whole, pk0, pk1, pk2, cot, keyed, valued, gated, query, gradf, gs0, gs1, gs2, mix,
    comb, taps, sub, gp, acc, proj, through, terms, held, total, mate, summed, ready, landed,
    sent, r0, r1, r2, send_one, recv_one, send_two, recv_two, send_tp, recv_tp, send_tok, recv_tok,
):
    me = lax.axis_index("ctx")
    x = lax.axis_index("groups")
    mine = lax.axis_index("tp")
    other = 1 - mine
    z, y = me // 2, lax.rem(me, 2)
    count = chunks
    lines = count // 2
    subs = chunks * QUARTERS
    lanes = CHUNK_LANES
    f32, bf16 = jnp.float32, jnp.bfloat16
    pk = (pk0, pk1, pk2)
    long_taps = long_ref.shape[0]
    short_taps = short_ref.shape[0] // 3
    channels = chunks * lanes

    barrier = pltpu.get_barrier_semaphore()
    for d in range(1, count):
        pl.semaphore_signal(
            barrier, inc=1, device_id={"ctx": lax.rem(me + d, count)}, device_id_type=MESH
        )
    pl.semaphore_signal(barrier, inc=1, device_id={"tp": other}, device_id_type=MESH)
    pl.semaphore_signal(barrier, inc=1, device_id={"groups": 1 - x}, device_id_type=MESH)

    def merge(c):
        delta = jnp.dot(own_ref[...], up_ref[c], preferred_element_type=f32)
        for g in range(3):
            at = pl.ds(pl.multiple_of(g * channels + c * lanes, lanes), lanes)
            value = weight_ref[:, at].astype(f32) + adapter_scale * delta[:, g * lanes : (g + 1) * lanes]
            whole[c, z, y, :, :, :, pl.ds(g * lanes, lanes)] = value.astype(bf16).reshape(
                QUARTERS, 2, PIECE, lanes
            )

    def send(ref, sub_at, recv, device):
        pltpu.make_async_remote_copy(
            src_ref=ref, dst_ref=ref, send_sem=sent.at[sub_at], recv_sem=recv.at[sub_at],
            device_id=device, device_id_type=MESH,
        ).start()

    def arrived(ref, sub_at, recv):
        pltpu.make_async_remote_copy(
            src_ref=ref, dst_ref=ref, send_sem=sent.at[sub_at], recv_sem=recv.at[sub_at],
            device_id={"tp": other}, device_id_type=MESH,
        ).wait_recv()

    def line(d):
        return lax.rem(z + d, lines)

    to_x = {"groups": 1 - x}
    to_y = {"ctx": z * 2 + 1 - y}

    def stage0(c, q):
        n = c * QUARTERS + q
        for d in range(1, lines):
            ref = whole.at[c, z, y, q] if q == 3 else whole.at[c, z, y, q, x]
            send(ref, n, r0, {"ctx": line(d) * 2 + y})

    def stage1(c, q):
        n = c * QUARTERS + q
        if q == 3:
            arrived(whole.at[0, 0, 0, pl.ds(0, lines - 1)], n, r0)
        else:
            arrived(whole.at[0, 0, 0, pl.ds(0, lines - 1), 0], n, r0)
        if q != 3:
            for d in range(1, lines):
                send(whole.at[c, line(d), y, q, x], n, r1, to_x)
        send(whole.at[c, :, y, q, x], n, r1, to_y)

    def stage2(c, q):
        n = c * QUARTERS + q
        arrived(whole.at[pl.ds(0, lines if q == 3 else 2 * lines - 1), 0, 0, 0, 0], n, r1)
        if q in (0, 3):
            send(whole.at[c, :, 1 - y, q, x], n, r2, to_x)
        else:
            half = PIECE // 2
            send(whole.at[c, :, 1 - y, q, x, pl.ds(0, half)], n, r2, to_x)
            send(whole.at[c, :, y, q, 1 - x, pl.ds(half, half)], n, r2, to_y)

    def slot(base, off):
        for stage, back in ((stage0, 0), (stage2, 2 * LAG), (stage1, LAG)):
            at = off - back
            if at < 0:
                continue
            c, q = base + at // QUARTERS, at % QUARTERS
            if isinstance(base, int):
                stage(c, q)
            else:
                pl.when(c < chunks)(functools.partial(stage, c, q))

    merge(0)
    pl.semaphore_wait(barrier, count + 1)

    first_slots = 3 * LAG + QUARTERS - 1
    body_rows = pl.ds(halo, rows)
    for n in range(first_slots):
        slot(0, n)
        if n + 1 < chunks:
            merge(n + 1)
        if n == first_slots - 2:
            proj[...] = lax.dot_general(
                down_ref[...], tokens_ref[body_rows, :], (((1,), (1,)), ((), ())),
                preferred_element_type=f32,
            ).astype(bf16)
            through[...] = jnp.zeros_like(through)
        if n == first_slots - 1:
            acc[...] = jnp.zeros_like(acc)
            for ref in pk:
                ref[pl.ds(rows + 2 * halo, BLOCK), :] = jnp.zeros((BLOCK, lanes), f32)

    def spread(row, count_rows):
        return jnp.broadcast_to(row, (count_rows, lanes))

    def chunk_step(c):
        cols = pl.ds(pl.multiple_of(c * lanes, lanes), lanes)

        slot(c, first_slots)
        for q in range(QUARTERS):
            arrived(whole.at[pl.ds(0, lines), 0, 0, 0, 0], c * QUARTERS + q, r2)
        ext = tokens_ref.shape[0]
        part = ext // 2

        @pl.loop(0, 2)
        def _(r):
            at = pl.ds(pl.multiple_of(r * part, 16), part)
            value = jnp.dot(
                tokens_ref[at, :], whole[c].reshape(-1, 3 * lanes), preferred_element_type=f32
            )
            for g in range(3):
                pk[g][at, :] = rounded(value[:, g * lanes : (g + 1) * lanes])

        slot(c, first_slots + 1)

        @pl.loop(0, long_taps // SUB)
        def _(k):
            piece = long_ref[pl.ds(pl.multiple_of(k * SUB, SUB), SUB), cols]
            for h in range(2):
                p = [spread(piece[4 * h + i : 4 * h + i + 1], SUB) for i in range(4)]
                at = pl.ds(pl.multiple_of((2 * k + h) * SUB, SUB), SUB)
                for e, value in enumerate(combine(p)):
                    taps[e, at, :] = value

        @pl.loop(0, cot.shape[0] // BLOCK)
        def _(i):
            here = pl.ds(pl.multiple_of(i * BLOCK, BLOCK), BLOCK)
            cot[here, :] = cot_ref[here, cols].astype(f32)

        def short(ref, g, first, sign, size, stride):
            seen = {}

            def at(k):
                if k not in seen:
                    seen[k] = ref[pl.ds(first + k, SUB, stride=stride), :]
                return seen[k]

            result = [None] * size
            for j in range(short_taps):
                tap = spread(short_ref[j * 3 + g : j * 3 + g + 1, cols], SUB)
                for i in range(size):
                    term = tap * at(i + sign * j)
                    result[i] = term if j == 0 else result[i] + term
            return result

        wide = gated.shape[0] // SUB
        step = 12

        @pl.loop(0, wide // step)
        def _(b):
            key = short(pk1, 1, b * step + halo - long_taps, -1, step, wide)
            val = short(pk2, 2, b * step + halo - long_taps, -1, step, wide)
            for i in range(step):
                here = pl.ds(b * step + i, SUB, stride=wide)
                keyed[here, :] = key[i]
                valued[here, :] = val[i]
                gated[here, :] = rounded(key[i] * val[i])

        @pl.loop(0, wide // step)
        def _(b):
            que = short(pk0, 0, b * step + halo, -1, step, wide)
            for i in range(step):
                here = pl.ds(b * step + i, SUB, stride=wide)
                query[here, :] = que[i]
                gradf[here, :] = rounded(que[i] * cot[here, :])

        span = PHASE_TAPS + SEG // 4

        @pl.loop(0, span)
        def _(k):
            at = pl.ds(pl.multiple_of(k * SUB, SUB), SUB)
            ahead = [gated[pl.ds(4 * k + i, SUB, stride=SEG), :] for i in range(4)]
            last = long_taps + SEG - 1
            back = [gradf[pl.ds(last - 4 * k - i, SUB, stride=SEG), :] for i in range(4)]
            for e, value in enumerate(combine(ahead) + combine(back)):
                comb[e, at, :] = value

        slot(c, first_slots + 2)

        outs = SEG // 4 + 1

        @pl.loop(0, 2 * COMBOS)
        def _(e):
            te = lax.rem(e, COMBOS)
            sums = [None] * outs
            seen = {}
            for k in range(PHASE_TAPS):
                weight = taps[te, k * SUB : (k + 1) * SUB, :]
                for n in range(outs):
                    at = n + PHASE_TAPS - 1 - k
                    if at not in seen:
                        seen[at] = comb[e, at * SUB : (at + 1) * SUB, :]
                    term = weight * seen[at]
                    sums[n] = term if sums[n] is None else sums[n] + term
            for n in range(outs):
                sub[e, n * SUB : (n + 1) * SUB, :] = sums[n]

        slot(c, first_slots + 3)
        skip = spread(skip_ref[:, cols], SUB)

        @pl.loop(0, SEG // 4)
        def _(n):
            before = pl.ds(pl.multiple_of(n * SUB, SUB), SUB)
            now = pl.ds(pl.multiple_of((n + 1) * SUB, SUB), SUB)

            def outputs(first):
                def pair(e):
                    v0, v1, v2 = (sub[first + e + i, now, :] for i in range(3))
                    return v0 + sub[first + e + 1, before, :], v2 - v0 - v1

                a_e, a_o = pair(0)
                b_e, b_o = pair(3)
                c_e, c_o = pair(6)
                b_was = (
                    sub[first + 5, before, :] - sub[first + 3, before, :] - sub[first + 4, before, :]
                )
                return (a_e + b_was, c_e - a_e - b_e, a_o + b_e, c_o - a_o - b_o)

            for i, value in enumerate(outputs(0)):
                here = pl.ds(4 * n + i, SUB, stride=SEG)
                filtered = value + skip * gated[pl.ds(long_taps + 4 * n + i, SUB, stride=SEG), :]
                gs0[here, :] = rounded(cot[here, :] * filtered)
                mix[here, :] = query[here, :] * filtered
            for i, value in enumerate(outputs(COMBOS)):
                first = SEG - 1 - 4 * n - i
                here = pl.ds(first, SUB, stride=SEG)
                there = pl.ds(long_taps + first, SUB, stride=SEG)
                grad_gated = value + skip * gradf[here, :]
                gs1[here, :] = rounded(grad_gated * valued[there, :])
                gs2[here, :] = rounded(grad_gated * keyed[there, :])

        done = (query, keyed, valued)

        @pl.loop(0, OUT_SEG // OUT_STEP)
        def _(b):
            for g, ref in enumerate((gs0, gs1, gs2)):
                value = short(ref, g, b * OUT_STEP, 1, OUT_STEP, OUT_SEG)
                for i in range(OUT_STEP):
                    done[g][pl.ds(b * OUT_STEP + i, SUB, stride=OUT_SEG), :] = value[i]

        @pl.loop(0, rows // BLOCK)
        def _(i):
            here = pl.ds(pl.multiple_of(i * BLOCK, BLOCK), BLOCK)
            mixed_ref[here, cols] = mix[here, :].astype(bf16)
            for g in range(3):
                gp[here, pl.ds(g * lanes, lanes)] = done[g][here, :].astype(bf16)

        terms[c, :, pl.ds(terms.shape[2] - 3 * lanes, 3 * lanes)] = jnp.dot(
            proj[...], gp[...], preferred_element_type=f32
        )
        through[...] += lax.dot_general(
            up_ref[c], gp[...], (((1,), (1,)), ((), ())), preferred_element_type=f32
        )

        @pl.loop(0, lines)
        def _(k):
            for pair in range(2):
                block = whole[c, k, pair].reshape(-1, 3 * lanes)
                wide = block.shape[0]
                at = pl.ds(pl.multiple_of((k * 2 + pair) * wide, wide), wide)
                acc[:, at] += lax.dot_general(
                    gp[...], block, (((1,), (1,)), ((), ())), preferred_element_type=f32
                )

    pl.loop(0, chunks)(chunk_step)

    cols = tokgrad_ref.shape[1]
    tile = ready.shape[2]
    steps = cols // tile
    width = mate.shape[1]

    def token_copy(t):
        return pltpu.make_async_remote_copy(
            src_ref=ready.at[t], dst_ref=landed.at[t], send_sem=send_tok.at[t],
            recv_sem=recv_tok.at[t], device_id={"tp": other}, device_id_type=MESH,
        )

    @pl.loop(0, steps)
    def _(t):
        at = pl.multiple_of(other * cols + t * tile, tile)
        ready[t] = acc[:, pl.ds(at, tile)].astype(bf16)
        token_copy(t).start()

    part_a = jnp.dot(through[...].astype(bf16), tokens_ref[body_rows, :], preferred_element_type=f32)
    for d in range(count):
        terms[d, :, pl.ds(0, width)] = part_a[:, d * width : (d + 1) * width]

    first = []
    for d in range(1, count):
        peer = lax.rem(me + d, count)
        first.append(
            pltpu.make_async_remote_copy(
                src_ref=terms.at[peer], dst_ref=held.at[d], send_sem=send_one.at[d],
                recv_sem=recv_one.at[d], device_id={"ctx": peer}, device_id_type=MESH,
            )
        )
        first[-1].start()
    own = terms[me]
    for d in range(1, count):
        first[d - 1].wait()
        own = own + held[d]
    total[...] = own
    tp_copy = pltpu.make_async_remote_copy(
        src_ref=total.at[:, pl.ds(0, width)], dst_ref=mate, send_sem=send_tp, recv_sem=recv_tp,
        device_id={"tp": other}, device_id_type=MESH,
    )
    tp_copy.start()
    tp_copy.wait()
    total[:, pl.ds(0, width)] = total[:, pl.ds(0, width)] + mate[...]
    summed[me] = total[...]
    second = []
    for d in range(1, count):
        second.append(
            pltpu.make_async_remote_copy(
                src_ref=total, dst_ref=summed.at[me], send_sem=send_two.at[d],
                recv_sem=recv_two.at[d], device_id={"ctx": lax.rem(me + d, count)},
                device_id_type=MESH,
            )
        )
        second[-1].start()

    @pl.loop(0, steps)
    def _(t):
        token_copy(t).wait()
        at = pl.multiple_of(t * tile, tile)
        from_at = pl.multiple_of(mine * cols + t * tile, tile)
        tokgrad_ref[:, pl.ds(at, tile)] = (
            acc[:, pl.ds(from_at, tile)] + landed[t].astype(f32)
        ).astype(bf16)

    @pl.loop(0, subs)
    def _(n):
        ref = whole.at[pl.ds(0, 7), 0, 0, 0]
        pltpu.make_async_remote_copy(
            src_ref=ref, dst_ref=ref, send_sem=sent.at[n], recv_sem=r0.at[n],
            device_id={"tp": other}, device_id_type=MESH,
        ).wait_send()

    for copy in second:
        copy.wait()
    sums_ref[...] = summed[...]


def block(weight, own_rows, adapter_a, adapter_b, tokens_ext, cot_ext, short, long, skip, rows, halo, count):
    rank = adapter_a.shape[1]
    features = tokens_ext.shape[1]
    channels = long.shape[1]
    chunks = channels // CHUNK_LANES
    lanes = CHUNK_LANES
    width = features // count
    cols = features // 2
    tile = 256
    up = adapter_b.reshape(rank, 3, chunks, lanes).transpose(2, 0, 1, 3).reshape(chunks, rank, 3 * lanes)
    vmem = pl.BlockSpec(memory_space=pltpu.VMEM)
    f32, bf16 = jnp.float32, jnp.bfloat16
    seg_rows = SUB * SEG
    reach = seg_rows + long.shape[0]
    plain = lambda n: pltpu.VMEM((n, lanes), f32)
    dma = pltpu.SemaphoreType.DMA
    subs = chunks * QUARTERS
    terms = (count, rank, width + 3 * lanes)
    scratch = [
        pltpu.VMEM((chunks, count // 2, 2, QUARTERS, 2, PIECE, 3 * lanes), bf16),
        plain(rows + 2 * halo + BLOCK), plain(rows + 2 * halo + BLOCK), plain(rows + 2 * halo + BLOCK),
        plain(reach), plain(reach), plain(reach), plain(reach), plain(reach), plain(reach),
        plain(seg_rows), plain(seg_rows), plain(seg_rows), plain(seg_rows),
        pltpu.VMEM((2 * COMBOS, (PHASE_TAPS + SEG // 4) * SUB, lanes), f32),
        pltpu.VMEM((COMBOS, PHASE_TAPS * SUB, lanes), f32),
        pltpu.VMEM((2 * COMBOS, (SEG // 4 + 1) * SUB, lanes), f32),
        pltpu.VMEM((rows, 3 * lanes), bf16),
        pltpu.VMEM((rows, features), f32),
        pltpu.VMEM((rank, rows), bf16),
        pltpu.VMEM((rank, rows), f32),
        pltpu.VMEM(terms, f32),
        pltpu.VMEM(terms, f32),
        pltpu.VMEM(terms[1:], f32),
        pltpu.VMEM((rank, width), f32),
        pltpu.VMEM(terms, f32),
        pltpu.VMEM((cols // tile, rows, tile), bf16),
        pltpu.VMEM((cols // tile, rows, tile), bf16),
        dma((subs,)), dma((subs,)), dma((subs,)), dma((subs,)),
        dma((count,)), dma((count,)), dma((count,)), dma((count,)),
        dma, dma, dma((cols // tile,)), dma((cols // tile,)),
    ]
    mixed, grad_tokens, sums = pl.pallas_call(
        functools.partial(block_kernel, chunks, halo, rows),
        out_shape=(
            jax.ShapeDtypeStruct((rows, channels), bf16),
            jax.ShapeDtypeStruct((rows, cols), bf16),
            jax.ShapeDtypeStruct(terms, f32),
        ),
        in_specs=[vmem] * 9,
        out_specs=(vmem,) * 3,
        scratch_shapes=scratch,
        compiler_params=pltpu.CompilerParams(
            vmem_limit_bytes=58 << 20, collective_id=3, has_side_effects=True
        ),
        cost_estimate=pl.CostEstimate(
            flops=8 * rows * 3 * channels * features, bytes_accessed=20 << 20, transcendentals=0
        ),
    )(weight, own_rows, adapter_a.T, up, tokens_ext, cot_ext, short, long, skip)
    sum_a = sums[:, :, :width].transpose(1, 0, 2).reshape(rank, features)
    sum_b = sums[:, :, width:].reshape(chunks, rank, 3, lanes).transpose(1, 2, 0, 3)
    return mixed, grad_tokens, sum_a, sum_b.reshape(rank, 3 * channels)


def body(tokens, weight, adapter_a, adapter_b, short_filter, long_filter, skip_gain, cotangent):
    rows, features = tokens.shape
    share = weight.shape[0]
    channels = weight.shape[2]
    rank = adapter_a.shape[1]
    count = lax.axis_size("ctx")
    fits = (
        count == 8
        and lax.axis_size("groups") == 2
        and rows == SUB * (SEG - 4)
        and long_filter.shape[0] == 4 * PHASE_TAPS
        and short_filter.shape[0] <= BLOCK
        and channels == count * CHUNK_LANES
        and share == 2 * QUARTERS * PIECE
        and features == share * count
    )
    if not fits:
        return general_body(
            tokens, weight, adapter_a, adapter_b, short_filter, long_filter, skip_gain, cotangent
        )
    halo = long_filter.shape[0] + BLOCK
    before = shifted(tokens[rows - halo :], "ctx", 1)
    after = shifted(tokens[:halo], "ctx", -1)
    cot_after = shifted(cotangent[:halo], "ctx", -1)
    tokens_ext = jnp.concatenate([before, tokens, after], axis=0)
    rest = jnp.zeros((SUB * SEG + long_filter.shape[0] - rows - halo, channels), cotangent.dtype)
    cot_ext = jnp.concatenate([cotangent, cot_after, rest], axis=0)
    own_rows = lax.dynamic_slice_in_dim(adapter_a, lax.axis_index("ctx") * share, share, 0)
    mixed, grad_tokens, sum_a, sum_b = block(
        weight.reshape(share, 3 * channels), own_rows, adapter_a, adapter_b, tokens_ext, cot_ext,
        short_filter.reshape(-1, channels), long_filter, skip_gain.reshape(1, channels),
        rows, halo, count,
    )
    factor = adapter_scale / math.sqrt(rows * count)
    return (mixed, grad_tokens, sum_a.T * factor, (sum_b * factor).reshape(rank, 3, channels))


def solution(mesh):
    return jax.shard_map(
        body,
        mesh=mesh,
        in_specs=(
            P(("groups", "ctx"), None),
            P("ctx", None, "tp"),
            P(),
            P(None, None, "tp"),
            P(None, None, "tp"),
            P(None, "tp"),
            P("tp"),
            P(("groups", "ctx"), "tp"),
        ),
        out_specs=(
            P(("groups", "ctx"), "tp"),
            P(("groups", "ctx"), "tp"),
            P("groups", None),
            P("groups", None, "tp"),
        ),
        check_vma=False,
    )
```

```python
import functools
import math

import jax
import jax.numpy as jnp
from jax import lax
from jax.experimental import pallas as pl
from jax.experimental.pallas import tpu as pltpu
from jax.sharding import PartitionSpec as P

adapter_scale = 0.03125
LANES = 128
SUB = 8
BLOCK = 16
CHUNK = 32


def shifted(value, axis, steps):
    count = lax.axis_size(axis)
    initial, last = (max(0, -steps), min(count, count - steps))
    return lax.ppermute(value, axis, [(source, source + steps) for source in range(initial, last)])


def tiles(ref, first, count):
    start = first * SUB
    if not isinstance(start, int):
        start = pl.multiple_of(start, SUB)
    return ref[pl.ds(start, count * SUB), :].reshape(count, SUB, LANES)


def put(ref, first, value):
    count = value.shape[0]
    ref[pl.ds(pl.multiple_of(first * SUB, SUB), count * SUB), :] = value.reshape(count * SUB, LANES)


def rounded(value):
    return value.astype(jnp.bfloat16).astype(jnp.float32)


def mixer_kernel(
    rows, halo, packed_ref, cot_ref, short_ref, long_ref, skip_ref, mixed_ref, grad_ref,
    p0, p1, p2, cot, query, keyed, valued, gated, gradf,
):
    channels = SUB * LANES
    short_taps = short_ref.shape[0] // 3
    long_taps = long_ref.shape[0]
    spread = (p0, p1, p2)
    front = halo - long_taps

    @pl.loop(0, (rows + 2 * halo) // BLOCK)
    def _(i):
        at = pl.multiple_of(i * BLOCK, BLOCK)
        for g in range(3):
            for s in range(SUB):
                piece = packed_ref[pl.ds(at, BLOCK), pl.ds(g * channels + s * LANES, LANES)]
                spread[g][pl.ds(at * SUB + s, BLOCK, stride=SUB), :] = piece.astype(jnp.float32)

    @pl.loop(0, (rows + halo) // BLOCK)
    def _(i):
        at = pl.multiple_of(i * BLOCK, BLOCK)
        for s in range(SUB):
            piece = cot_ref[pl.ds(at, BLOCK), pl.ds(s * LANES, LANES)]
            cot[pl.ds(at * SUB + s, BLOCK, stride=SUB), :] = piece.astype(jnp.float32)

    def short(ref, g, first, sign):
        total = None
        for j in range(short_taps):
            term = short_ref[j * 3 + g][None] * tiles(ref, first + sign * j, SUB)
            total = term if total is None else total + term
        return total

    @pl.loop(0, (rows + BLOCK + long_taps) // SUB)
    def _(i):
        at = i * SUB
        key = short(p1, 1, at + front, -1)
        val = short(p2, 2, at + front, -1)
        put(keyed, at, key)
        put(valued, at, val)
        put(gated, at, rounded(key * val))

    @pl.loop(0, (rows + halo) // SUB)
    def _(i):
        at = i * SUB
        que = short(p0, 0, at + halo, -1)
        put(query, at, que)
        put(gradf, at, rounded(que * tiles(cot, at, SUB)))

    zero = tuple(jnp.zeros((SUB, LANES), jnp.float32) for _ in range(BLOCK))

    def long_sum(ref, base, sign):
        def chunk(c, acc):
            acc = list(acc)
            tap0 = c * CHUNK
            origin = base + sign * tap0
            low = origin - (CHUNK - 1) if sign < 0 else origin
            seen = {}

            def at(k):
                if k not in seen:
                    seen[k] = ref[pl.ds(pl.multiple_of((low + k) * SUB, SUB), SUB), :]
                return seen[k]

            for j in range(CHUNK):
                tap = long_ref[tap0 + j]
                for i in range(BLOCK):
                    k = i + (CHUNK - 1) - j if sign < 0 else i + j
                    acc[i] = acc[i] + tap * at(k)
            return tuple(acc)

        return lax.fori_loop(0, long_taps // CHUNK, chunk, zero)

    @pl.loop(0, (rows + BLOCK) // BLOCK)
    def _(b):
        at = b * BLOCK
        skip = skip_ref[...]
        ahead = jnp.stack(long_sum(gated, at + long_taps, -1))
        filtered = ahead + skip[None] * tiles(gated, at + long_taps, BLOCK)
        back = jnp.stack(long_sum(gradf, at, 1))
        grad_gated = back + skip[None] * tiles(gradf, at, BLOCK)
        put(p0, at, rounded(tiles(cot, at, BLOCK) * filtered))
        put(p1, at, rounded(grad_gated * tiles(valued, at + long_taps, BLOCK)))
        put(p2, at, rounded(grad_gated * tiles(keyed, at + long_taps, BLOCK)))
        put(gated, at, tiles(query, at, BLOCK) * filtered)

    results = (query, keyed, valued)

    @pl.loop(0, rows // SUB)
    def _(i):
        at = i * SUB
        for g in range(3):
            put(results[g], at, short(spread[g], g, at, 1))

    @pl.loop(0, rows // BLOCK)
    def _(i):
        at = pl.multiple_of(i * BLOCK, BLOCK)
        for s in range(SUB):
            pick = pl.ds(at * SUB + s, BLOCK, stride=SUB)
            mixed_ref[pl.ds(at, BLOCK), pl.ds(s * LANES, LANES)] = gated[pick, :].astype(jnp.bfloat16)
            for g in range(3):
                grad_ref[pl.ds(at, BLOCK), pl.ds(g * channels + s * LANES, LANES)] = results[g][
                    pick, :
                ].astype(jnp.bfloat16)


def mixer(packed, cot, short_filter, long_filter, skip_gain, rows, halo):
    channels = long_filter.shape[1]
    long_taps = long_filter.shape[0]
    full = (rows + 2 * halo) * SUB
    side = (rows + halo) * SUB
    scratch = [pltpu.VMEM((full, LANES), jnp.float32)] * 3 + [
        pltpu.VMEM((side, LANES), jnp.float32)
    ] * 6
    return pl.pallas_call(
        functools.partial(mixer_kernel, rows, halo),
        out_shape=(
            jax.ShapeDtypeStruct((rows, channels), jnp.bfloat16),
            jax.ShapeDtypeStruct((rows, 3 * channels), jnp.bfloat16),
        ),
        in_specs=[pl.BlockSpec(memory_space=pltpu.VMEM)] * 5,
        out_specs=(pl.BlockSpec(memory_space=pltpu.VMEM),) * 2,
        scratch_shapes=scratch,
        compiler_params=pltpu.CompilerParams(vmem_limit_bytes=52 << 20),
        cost_estimate=pl.CostEstimate(
            flops=4 * rows * channels * (long_taps + 42), bytes_accessed=12 << 20, transcendentals=0
        ),
    )(
        packed,
        cot,
        short_filter.reshape(-1, SUB, LANES),
        long_filter.reshape(long_taps, SUB, LANES),
        skip_gain.reshape(SUB, LANES),
    )


def finish_kernel(
    count, grad_ref, whole_ref, terms_ref, tokens_ref, sums_ref,
    held, total, mate, summed, ready, landed,
    send_one, recv_one, send_two, recv_two, send_tp, recv_tp, send_tok, recv_tok,
):
    me = lax.axis_index("ctx")
    mine = lax.axis_index("tp")
    other = 1 - mine
    width = mate.shape[1]
    cols = tokens_ref.shape[1]
    tile = ready.shape[2]
    steps = cols // tile

    barrier = pltpu.get_barrier_semaphore()
    for d in range(1, count):
        pl.semaphore_signal(
            barrier, inc=1, device_id={"ctx": lax.rem(me + d, count)}, device_id_type=pl.DeviceIdType.MESH
        )
    pl.semaphore_signal(barrier, inc=1, device_id={"tp": other}, device_id_type=pl.DeviceIdType.MESH)
    pl.semaphore_wait(barrier, count)

    first = []
    for d in range(1, count):
        peer = lax.rem(me + d, count)
        first.append(
            pltpu.make_async_remote_copy(
                src_ref=terms_ref.at[peer],
                dst_ref=held.at[d],
                send_sem=send_one.at[d],
                recv_sem=recv_one.at[d],
                device_id={"ctx": peer},
                device_id_type=pl.DeviceIdType.MESH,
            )
        )
        first[-1].start()

    def product(half, t):
        at = pl.multiple_of(half * cols + t * tile, tile)
        return lax.dot_general(
            grad_ref[...],
            whole_ref[pl.ds(at, tile), :],
            (((1,), (1,)), ((), ())),
            preferred_element_type=jnp.float32,
        )

    def token_copy(t):
        return pltpu.make_async_remote_copy(
            src_ref=ready.at[t],
            dst_ref=landed.at[t],
            send_sem=send_tok.at[t],
            recv_sem=recv_tok.at[t],
            device_id={"tp": other},
            device_id_type=pl.DeviceIdType.MESH,
        )

    @pl.loop(0, steps)
    def _(t):
        ready[t] = product(other, t).astype(jnp.bfloat16)
        token_copy(t).start()

    own = terms_ref[me]
    for d in range(1, count):
        first[d - 1].wait()
        own = own + held[d]
    total[...] = own
    tp_copy = pltpu.make_async_remote_copy(
        src_ref=total.at[:, pl.ds(0, width)],
        dst_ref=mate,
        send_sem=send_tp,
        recv_sem=recv_tp,
        device_id={"tp": other},
        device_id_type=pl.DeviceIdType.MESH,
    )
    tp_copy.start()

    def own_tile(t):
        value = product(mine, t)
        token_copy(t).wait()
        at = pl.multiple_of(t * tile, tile)
        tokens_ref[:, pl.ds(at, tile)] = (value + landed[t].astype(jnp.float32)).astype(jnp.bfloat16)

    pl.loop(0, steps // 4)(own_tile)
    tp_copy.wait()
    total[:, pl.ds(0, width)] = total[:, pl.ds(0, width)] + mate[...]
    summed[me] = total[...]
    second = []
    for d in range(1, count):
        second.append(
            pltpu.make_async_remote_copy(
                src_ref=total,
                dst_ref=summed.at[me],
                send_sem=send_two.at[d],
                recv_sem=recv_two.at[d],
                device_id={"ctx": lax.rem(me + d, count)},
                device_id_type=pl.DeviceIdType.MESH,
            )
        )
        second[-1].start()
    pl.loop(steps // 4, steps)(own_tile)
    for copy in second:
        copy.wait()
    sums_ref[...] = summed[...]


def finish(grad_packed, whole, part_a, part_b, count):
    rank, features = part_a.shape
    rows, wide = grad_packed.shape
    width, rest = features // count, wide // count
    cols = features // 2
    tile = 256
    terms = jnp.concatenate(
        [part_a.reshape(rank, count, width), part_b.reshape(rank, count, rest)], axis=2
    ).transpose(1, 0, 2)
    vmem = pl.BlockSpec(memory_space=pltpu.VMEM)
    grad_tokens, sums = pl.pallas_call(
        functools.partial(finish_kernel, count),
        out_shape=(
            jax.ShapeDtypeStruct((rows, cols), jnp.bfloat16),
            jax.ShapeDtypeStruct(terms.shape, jnp.float32),
        ),
        in_specs=[vmem] * 3,
        out_specs=(vmem, vmem),
        scratch_shapes=[
            pltpu.VMEM(terms.shape, jnp.float32),
            pltpu.VMEM((rank, width + rest), jnp.float32),
            pltpu.VMEM((rank, width), jnp.float32),
            pltpu.VMEM(terms.shape, jnp.float32),
            pltpu.VMEM((cols // tile, rows, tile), jnp.bfloat16),
            pltpu.VMEM((cols // tile, rows, tile), jnp.bfloat16),
            pltpu.SemaphoreType.DMA((count,)),
            pltpu.SemaphoreType.DMA((count,)),
            pltpu.SemaphoreType.DMA((count,)),
            pltpu.SemaphoreType.DMA((count,)),
            pltpu.SemaphoreType.DMA,
            pltpu.SemaphoreType.DMA,
            pltpu.SemaphoreType.DMA((cols // tile,)),
            pltpu.SemaphoreType.DMA((cols // tile,)),
        ],
        compiler_params=pltpu.CompilerParams(
            vmem_limit_bytes=48 << 20, collective_id=1, has_side_effects=True
        ),
        cost_estimate=pl.CostEstimate(
            flops=2 * rows * wide * features, bytes_accessed=20 << 20, transcendentals=0
        ),
    )(grad_packed, whole, terms)
    flat = sums.transpose(1, 0, 2)
    return (
        grad_tokens,
        flat[:, :, :width].reshape(rank, features),
        flat[:, :, width:].reshape(rank, wide),
    )


MESH = pl.DeviceIdType.MESH
PIECES = 4


def gather_kernel(
    outer, shard_ref, out_ref, z_send, z_recv, y_send, y_recv, x_send, x_recv, local_sem
):
    me = lax.axis_index("ctx")
    x = lax.axis_index("groups")
    z, y = me // 2, lax.rem(me, 2)
    rows = shard_ref.shape[0]
    piece = rows // PIECES
    half = piece // 2
    last = outer - 2
    steps = outer - 1

    def ctx_of(line, pair):
        return {"ctx": line * 2 + pair}

    def span(line, pair, start, size):
        return pl.ds(pl.multiple_of((line * 2 + pair) * rows + start, half), size)

    def part(p, side):
        return p * piece + side * half

    def copy(src, dst, send, recv, device):
        return pltpu.make_async_remote_copy(
            src_ref=src, dst_ref=dst, send_sem=send, recv_sem=recv, device_id=device, device_id_type=MESH
        )

    def z_range(k, p):
        return (part(p, x), half) if k == last else (p * piece, piece)

    def z_out(way, k, p):
        step = 1 - 2 * way
        start, size = z_range(k, p)
        place = span(z - step * k, y, start, size)
        src = out_ref.at[place] if k else shard_ref.at[pl.ds(pl.multiple_of(start, half), size)]
        return copy(
            src, out_ref.at[place], z_send.at[way, k, p], z_recv.at[way, k, p], ctx_of(z + step, y)
        )

    def z_in(way, k, p):
        step = 1 - 2 * way
        start, size = z_range(k, p)
        place = out_ref.at[span(z - step * (k + 1), y, start, size)]
        return copy(place, place, z_send.at[way, k, p], z_recv.at[way, k, p], ctx_of(z - step, y))

    def sends(way, k):
        return (z < steps) & (z >= k) if way == 0 else (z > 0) & (z + k <= steps)

    def receives(way, k):
        return z > k if way == 0 else z + k < steps

    def line_of(i):
        if i == 0:
            return z
        way, k = (i - 1) // steps, (i - 1) % steps
        return z - (1 - 2 * way) * (k + 1)

    def item(way, k):
        return 1 + way * steps + k

    def y_out(i, p):
        start = part(p, x)
        place = span(line_of(i), y, start, half)
        src = out_ref.at[place] if i else shard_ref.at[pl.ds(pl.multiple_of(start, half), half)]
        return copy(src, out_ref.at[place], y_send.at[i, p], y_recv.at[i, p], ctx_of(z, 1 - y))

    def y_in(i, p):
        place = out_ref.at[span(line_of(i), 1 - y, part(p, x), half)]
        return copy(place, place, y_send.at[i, p], y_recv.at[i, p], ctx_of(z, 1 - y))

    def x_copy(i, p, side):
        if i > 2 * steps:
            line, pair = line_of(item(i - 2 * steps - 1, last)), y
        else:
            line, pair = line_of(i), 1 - y
        place = out_ref.at[span(line, pair, part(p, side), half)]
        return copy(place, place, x_send.at[i, p], x_recv.at[i, p], {"groups": 1 - x})

    def extra(way):
        return 2 * steps + 1 + way

    barrier = pltpu.get_barrier_semaphore()
    pl.semaphore_signal(barrier, inc=1, device_id=ctx_of(z, 1 - y), device_id_type=MESH)
    pl.semaphore_signal(barrier, inc=1, device_id={"groups": 1 - x}, device_id_type=MESH)
    for step in (1, outer - 1):
        pl.semaphore_signal(
            barrier, inc=1, device_id=ctx_of(lax.rem(z + step, outer), y), device_id_type=MESH
        )
    pl.semaphore_wait(barrier, 4)

    @pl.loop(0, PIECES)
    def _(p):
        for way in range(2):
            @pl.when(sends(way, 0))
            def _():
                z_out(way, 0, p).start()
        y_out(0, p).start()

    own = pltpu.make_async_copy(
        shard_ref, out_ref.at[pl.ds(pl.multiple_of(me * rows, rows), rows)], local_sem
    )
    own.start()

    def pass_on(k, p):
        for way in range(2):
            @pl.when(receives(way, k))
            def _():
                i = item(way, k)
                y_in(i, p).wait_recv()
                x_copy(i, p, x).start()

    for k in range(steps):
        @pl.loop(0, PIECES)
        def _(p):
            for way in range(2):
                @pl.when(receives(way, k))
                def _():
                    z_in(way, k, p).wait_recv()
                    if k < last:
                        @pl.when(sends(way, k + 1))
                        def _():
                            z_out(way, k + 1, p).start()
                    y_out(item(way, k), p).start()
                    if k == last:
                        x_copy(extra(way), p, x).start()
            if k == 0:
                y_in(0, p).wait_recv()
                x_copy(0, p, x).start()

            @pl.when(p > 0)
            def _():
                pass_on(k, p - 1)

            if k > 0:
                @pl.when(p == 0)
                def _():
                    pass_on(k - 1, PIECES - 1)

    pass_on(last, PIECES - 1)
    own.wait()

    @pl.loop(0, PIECES)
    def _(p):
        x_copy(0, p, 1 - x).wait_recv()
        x_copy(0, p, x).wait_send()
        y_out(0, p).wait_send()
        for way in range(2):
            for k in range(steps):
                @pl.when(sends(way, k))
                def _():
                    z_out(way, k, p).wait_send()

                @pl.when(receives(way, k))
                def _():
                    i = item(way, k)
                    x_copy(i, p, 1 - x).wait_recv()
                    x_copy(i, p, x).wait_send()
                    y_out(i, p).wait_send()
                    if k == last:
                        x_copy(extra(way), p, 1 - x).wait_recv()
                        x_copy(extra(way), p, x).wait_send()


def gather(merged, count):
    rows, wide = merged.shape
    outer = count // 2
    items = 2 * (outer - 1) + 1
    dma = pltpu.SemaphoreType.DMA
    hbm = pl.BlockSpec(memory_space=pl.ANY)
    return pl.pallas_call(
        functools.partial(gather_kernel, outer),
        out_shape=jax.ShapeDtypeStruct((rows * count, wide), merged.dtype),
        in_specs=[hbm],
        out_specs=hbm,
        scratch_shapes=[
            dma((2, outer - 1, PIECES)),
            dma((2, outer - 1, PIECES)),
            dma((items, PIECES)),
            dma((items, PIECES)),
            dma((items + 2, PIECES)),
            dma((items + 2, PIECES)),
            dma,
        ],
        compiler_params=pltpu.CompilerParams(collective_id=2, has_side_effects=True),
        cost_estimate=pl.CostEstimate(flops=0, bytes_accessed=300 << 20, transcendentals=0),
    )(merged)


def general_body(tokens, weight, adapter_a, adapter_b, short_filter, long_filter, skip_gain, cotangent):
    row_count = tokens.shape[0]
    share_rows = weight.shape[0]
    channels = weight.shape[2]
    features = tokens.shape[1]
    adapter_rank = adapter_a.shape[1]
    halo = long_filter.shape[0] + BLOCK
    count = lax.axis_size("ctx")
    seq_total = row_count * count
    first_row = lax.axis_index("ctx") * share_rows
    before = shifted(tokens[row_count - halo :], "ctx", 1)
    after = shifted(tokens[:halo], "ctx", -1)
    cot_after = shifted(cotangent[:halo], "ctx", -1)
    tokens_ext = jnp.concatenate([before, tokens, after], axis=0)
    cot_ext = jnp.concatenate([cotangent, cot_after], axis=0)
    own_rows = lax.dynamic_slice_in_dim(adapter_a, first_row, share_rows, 0)
    flat_b = adapter_b.reshape(adapter_rank, 3 * channels)
    delta_w = jnp.dot(own_rows, flat_b, preferred_element_type=jnp.float32)
    merged = (
        weight.reshape(share_rows, 3 * channels).astype(jnp.float32) + adapter_scale * delta_w
    ).astype(jnp.bfloat16)
    if count == 8 and lax.axis_size("groups") == 2:
        whole = gather(merged, count)
    else:
        whole = lax.all_gather(merged, "ctx", axis=0, tiled=True)
    packed = jnp.dot(tokens_ext, whole, preferred_element_type=jnp.float32).astype(jnp.bfloat16)
    mixed, grad_packed = mixer(
        packed, cot_ext, short_filter, long_filter, skip_gain, row_count, halo
    )
    projected = jnp.dot(tokens, adapter_a, preferred_element_type=jnp.float32).astype(jnp.bfloat16)
    part_b = lax.dot_general(
        projected, grad_packed, (((0,), (0,)), ((), ())), preferred_element_type=jnp.float32
    )
    through = lax.dot_general(
        flat_b, grad_packed, (((1,), (1,)), ((), ())), preferred_element_type=jnp.float32
    ).astype(jnp.bfloat16)
    part_a = jnp.dot(through, tokens, preferred_element_type=jnp.float32)
    if features % (LANES * count) == 0 and (3 * channels) % (LANES * count) == 0:
        grad_tokens, sum_a, sum_b = finish(grad_packed, whole, part_a, part_b, count)
    else:
        sum_a = lax.psum(part_a, ("ctx", "tp"))
        sum_b = lax.psum(part_b, "ctx")
        partial_grad = lax.dot_general(
            grad_packed, whole, (((1,), (1,)), ((), ())), preferred_element_type=jnp.float32
        )
        grad_tokens = lax.psum_scatter(
            partial_grad.astype(jnp.bfloat16), "tp", scatter_dimension=1, tiled=True
        )
    sum_a = sum_a.T
    factor = adapter_scale / math.sqrt(seq_total)
    return (mixed, grad_tokens, sum_a * factor, (sum_b * factor).reshape(adapter_rank, 3, channels))


CHUNK_LANES = 128
QUARTERS = 4
LAG = 2
PIECE = 32
SEG = 68
COMBOS = 9
PHASE_TAPS = 32
OUT_SEG = 66
OUT_STEP = 11
EDGE = 16


def combine(p):
    p02, p13, p01, p23 = p[0] + p[2], p[1] + p[3], p[0] + p[1], p[2] + p[3]
    return (p[0], p[2], p02, p[1], p[3], p13, p01, p23, p01 + p23)


def block_kernel(
    chunks, rows,
    weight_ref, own_ref, down_ref, up_ref, tokens_hbm, cot_hbm, short_ref, long_ref, skip_ref,
    mixed_ref, tokgrad_ref, sums_ref,
    tokens_ref, cot_ref, hold_g, hold_f, edge_g, edge_f,
    whole, pk0, pk1, pk2, cot, keyed, valued, gated, query, gradf, gs0, gs1, gs2, mix,
    comb, taps, sub, gp, acc, proj, through, terms, held, total, mate, summed, ready, landed,
    load_sem, near_send, near_recv, edge_send, edge_recv,
    sent, r0, r1, r2, send_one, recv_one, send_two, recv_two, send_tp, recv_tp, send_tok, recv_tok,
):
    me = lax.axis_index("ctx")
    x = lax.axis_index("groups")
    mine = lax.axis_index("tp")
    other = 1 - mine
    z, y = me // 2, lax.rem(me, 2)
    count = chunks
    lines = count // 2
    subs = chunks * QUARTERS
    lanes = CHUNK_LANES
    f32, bf16 = jnp.float32, jnp.bfloat16
    pk = (pk0, pk1, pk2)
    long_taps = long_ref.shape[0]
    short_taps = short_ref.shape[0] // 3
    channels = chunks * lanes
    halo = EDGE
    has_next, has_last = me < count - 1, me > 0
    to_next = {"ctx": lax.rem(me + 1, count)}
    to_last = {"ctx": lax.rem(me + count - 1, count)}

    loads = (
        pltpu.make_async_copy(tokens_hbm, tokens_ref.at[pl.ds(halo, rows)], load_sem.at[0]),
        pltpu.make_async_copy(cot_hbm, cot_ref.at[pl.ds(0, rows)], load_sem.at[1]),
    )
    for copy in loads:
        copy.start()

    barrier = pltpu.get_barrier_semaphore()
    for d in range(1, count):
        pl.semaphore_signal(
            barrier, inc=1, device_id={"ctx": lax.rem(me + d, count)}, device_id_type=MESH
        )
    pl.semaphore_signal(barrier, inc=1, device_id={"tp": other}, device_id_type=MESH)
    pl.semaphore_signal(barrier, inc=1, device_id={"groups": 1 - x}, device_id_type=MESH)

    def merge(c):
        delta = jnp.dot(own_ref[...], up_ref[c], preferred_element_type=f32)
        for g in range(3):
            at = pl.ds(pl.multiple_of(g * channels + c * lanes, lanes), lanes)
            value = weight_ref[:, at].astype(f32) + adapter_scale * delta[:, g * lanes : (g + 1) * lanes]
            whole[c, z, y, :, :, :, pl.ds(g * lanes, lanes)] = value.astype(bf16).reshape(
                QUARTERS, 2, PIECE, lanes
            )

    def send(ref, sub_at, recv, device):
        pltpu.make_async_remote_copy(
            src_ref=ref, dst_ref=ref, send_sem=sent.at[sub_at], recv_sem=recv.at[sub_at],
            device_id=device, device_id_type=MESH,
        ).start()

    def arrived(ref, sub_at, recv):
        pltpu.make_async_remote_copy(
            src_ref=ref, dst_ref=ref, send_sem=sent.at[sub_at], recv_sem=recv.at[sub_at],
            device_id={"tp": other}, device_id_type=MESH,
        ).wait_recv()

    def line(d):
        return lax.rem(z + d, lines)

    to_x = {"groups": 1 - x}
    to_y = {"ctx": z * 2 + 1 - y}

    def stage0(c, q):
        n = c * QUARTERS + q
        for d in range(1, lines):
            ref = whole.at[c, z, y, q] if q == 3 else whole.at[c, z, y, q, x]
            send(ref, n, r0, {"ctx": line(d) * 2 + y})

    def stage1(c, q):
        n = c * QUARTERS + q
        if q == 3:
            arrived(whole.at[0, 0, 0, pl.ds(0, lines - 1)], n, r0)
        else:
            arrived(whole.at[0, 0, 0, pl.ds(0, lines - 1), 0], n, r0)
        if q != 3:
            for d in range(1, lines):
                send(whole.at[c, line(d), y, q, x], n, r1, to_x)
        send(whole.at[c, :, y, q, x], n, r1, to_y)

    def stage2(c, q):
        n = c * QUARTERS + q
        arrived(whole.at[pl.ds(0, lines if q == 3 else 2 * lines - 1), 0, 0, 0, 0], n, r1)
        if q in (0, 3):
            send(whole.at[c, :, 1 - y, q, x], n, r2, to_x)
        else:
            half = PIECE // 2
            send(whole.at[c, :, 1 - y, q, x, pl.ds(0, half)], n, r2, to_x)
            send(whole.at[c, :, y, q, 1 - x, pl.ds(half, half)], n, r2, to_y)

    def slot(base, off):
        for stage, back in ((stage0, 0), (stage2, 2 * LAG), (stage1, LAG)):
            at = off - back
            if at < 0:
                continue
            c, q = base + at // QUARTERS, at % QUARTERS
            if isinstance(base, int):
                stage(c, q)
            else:
                pl.when(c < chunks)(functools.partial(stage, c, q))

    def near(k):
        src, dst, device = (
            (tokens_hbm.at[pl.ds(rows - halo, halo)], tokens_ref.at[pl.ds(0, halo)], to_next),
            (tokens_hbm.at[pl.ds(0, halo)], tokens_ref.at[pl.ds(rows + halo, halo)], to_last),
            (cot_hbm.at[pl.ds(0, halo)], cot_ref.at[pl.ds(rows, halo)], to_last),
        )[k]
        return pltpu.make_async_remote_copy(
            src_ref=src, dst_ref=dst, send_sem=near_send.at[k], recv_sem=near_recv.at[k],
            device_id=device, device_id_type=MESH,
        )

    def edge(k, c):
        src, dst, device = ((hold_g, edge_g, to_next), (hold_f, edge_f, to_last))[k]
        return pltpu.make_async_remote_copy(
            src_ref=src.at[c], dst_ref=dst.at[c], send_sem=edge_send.at[k, c],
            recv_sem=edge_recv.at[k, c], device_id=device, device_id_type=MESH,
        )

    merge(0)
    pl.semaphore_wait(barrier, count + 1)

    first_slots = 3 * LAG + QUARTERS - 1
    body_rows = pl.ds(halo, rows)
    for n in range(first_slots):
        slot(0, n)
        if n + 1 < chunks:
            merge(n + 1)
        if n == 0:
            pl.when(has_next)(lambda: near(0).start())

            @pl.when(has_last)
            def _():
                near(1).start()
                near(2).start()

            @pl.when(jnp.logical_not(has_last))
            def _():
                tokens_ref[pl.ds(0, halo), :] = jnp.zeros((halo, tokens_ref.shape[1]), bf16)
                edge_g[...] = jnp.zeros_like(edge_g)

            @pl.when(jnp.logical_not(has_next))
            def _():
                tokens_ref[pl.ds(rows + halo, halo), :] = jnp.zeros((halo, tokens_ref.shape[1]), bf16)
                cot_ref[pl.ds(rows, halo), :] = jnp.zeros((halo, channels), bf16)
                edge_f[...] = jnp.zeros_like(edge_f)

            tail = cot_ref.shape[0] - rows - halo
            cot_ref[pl.ds(rows + halo, tail), :] = jnp.zeros((tail, channels), bf16)
            known = rows + halo
            for ref in (query, keyed, valued):
                ref[pl.ds(known, ref.shape[0] - known), :] = jnp.zeros((ref.shape[0] - known, lanes), f32)
            after = gated.shape[0] - known - long_taps
            gated[pl.ds(known + long_taps, after), :] = jnp.zeros((after, lanes), f32)
            after = gradf.shape[0] - rows - edge_f.shape[1]
            gradf[pl.ds(rows + edge_f.shape[1], after), :] = jnp.zeros((after, lanes), f32)
        if n == first_slots - 2:
            for copy in loads:
                copy.wait()
            proj[...] = lax.dot_general(
                down_ref[...], tokens_ref[body_rows, :], (((1,), (1,)), ((), ())),
                preferred_element_type=f32,
            ).astype(bf16)
            through[...] = jnp.zeros_like(through)
        if n == first_slots - 1:
            acc[...] = jnp.zeros_like(acc)

            @pl.when(has_last)
            def _():
                near(0).wait_recv()
                near(1).wait_send()
                near(2).wait_send()

            @pl.when(has_next)
            def _():
                near(0).wait_send()
                near(1).wait_recv()
                near(2).wait_recv()

    def spread(row, count_rows):
        return jnp.broadcast_to(row, (count_rows, lanes))

    def adapter_terms(c):
        terms[c, :, pl.ds(terms.shape[2] - 3 * lanes, 3 * lanes)] = jnp.dot(
            proj[...], gp[...], preferred_element_type=f32
        )
        through[...] += lax.dot_general(
            up_ref[c], gp[...], (((1,), (1,)), ((), ())), preferred_element_type=f32
        )

    def token_terms(c, k, pair):
        block = whole[c, k, pair].reshape(-1, 3 * lanes)
        wide = block.shape[0]
        start = (k * 2 + pair) * wide
        at = pl.ds(start if isinstance(start, int) else pl.multiple_of(start, wide), wide)
        value = acc[:, at] + lax.dot_general(
            gp[...], block, (((1,), (1,)), ((), ())), preferred_element_type=f32
        )
        acc[:, at] = value
        return value

    def token_copy(t):
        return pltpu.make_async_remote_copy(
            src_ref=ready.at[t], dst_ref=landed.at[t], send_sem=send_tok.at[t],
            recv_sem=recv_tok.at[t], device_id={"tp": other}, device_id_type=MESH,
        )

    def chunk_step(c):
        cols = pl.ds(pl.multiple_of(c * lanes, lanes), lanes)

        slot(c, first_slots)
        for q in range(QUARTERS):
            arrived(whole.at[pl.ds(0, lines), 0, 0, 0, 0], c * QUARTERS + q, r2)
        ext = tokens_ref.shape[0]
        part = ext // 2

        @pl.loop(0, 2)
        def _(r):
            at = pl.ds(pl.multiple_of(r * part, 16), part)
            value = jnp.dot(
                tokens_ref[at, :], whole[c].reshape(-1, 3 * lanes), preferred_element_type=f32
            )
            for g in range(3):
                pk[g][at, :] = rounded(value[:, g * lanes : (g + 1) * lanes])

        slot(c, first_slots + 1)

        @pl.loop(0, long_taps // SUB)
        def _(k):
            piece = long_ref[pl.ds(pl.multiple_of(k * SUB, SUB), SUB), cols]
            for h in range(2):
                p = [spread(piece[4 * h + i : 4 * h + i + 1], SUB) for i in range(4)]
                at = pl.ds(pl.multiple_of((2 * k + h) * SUB, SUB), SUB)
                for e, value in enumerate(combine(p)):
                    taps[e, at, :] = value

        @pl.loop(0, cot.shape[0] // BLOCK)
        def _(i):
            here = pl.ds(pl.multiple_of(i * BLOCK, BLOCK), BLOCK)
            cot[here, :] = cot_ref[here, cols].astype(f32)

        def short(ref, g, first, sign, size, stride):
            seen = {}

            def at(k):
                if k not in seen:
                    seen[k] = ref[pl.ds(first + k, SUB, stride=stride), :]
                return seen[k]

            result = [None] * size
            for j in range(short_taps):
                tap = spread(short_ref[j * 3 + g : j * 3 + g + 1, cols], SUB)
                for i in range(size):
                    term = tap * at(i + sign * j)
                    result[i] = term if j == 0 else result[i] + term
            return result

        @pl.loop(0, OUT_SEG // OUT_STEP)
        def _(b):
            at = b * OUT_STEP
            key = short(pk1, 1, at + halo, -1, OUT_STEP, OUT_SEG)
            val = short(pk2, 2, at + halo, -1, OUT_STEP, OUT_SEG)
            for i in range(OUT_STEP):
                here = pl.ds(at + i, SUB, stride=OUT_SEG)
                keyed[here, :] = key[i]
                valued[here, :] = val[i]
                gated[pl.ds(at + i + long_taps, SUB, stride=OUT_SEG), :] = rounded(key[i] * val[i])
            que = short(pk0, 0, at + halo, -1, OUT_STEP, OUT_SEG)
            for i in range(OUT_STEP):
                here = pl.ds(at + i, SUB, stride=OUT_SEG)
                query[here, :] = que[i]
                gradf[here, :] = rounded(que[i] * cot[here, :])

        hold_g[c] = gated[pl.ds(rows, long_taps), :].astype(bf16)
        hold_f[c] = gradf[pl.ds(0, edge_f.shape[1]), :].astype(bf16)
        pl.when(has_next)(lambda: edge(0, c).start())
        pl.when(has_last)(lambda: edge(1, c).start())

        slot(c, first_slots + 2)

        @pl.when(c > 0)
        def _():
            adapter_terms(c - 1)
            for k in range(lines):
                for pair in range(2):
                    token_terms(c - 1, k, pair)

        pl.when(has_last)(lambda: edge(0, c).wait_recv())
        pl.when(has_next)(lambda: edge(1, c).wait_recv())
        gated[pl.ds(0, long_taps), :] = edge_g[c].astype(f32)
        gradf[pl.ds(rows, edge_f.shape[1]), :] = edge_f[c].astype(f32)

        span = PHASE_TAPS + SEG // 4

        @pl.loop(0, span)
        def _(k):
            at = pl.ds(pl.multiple_of(k * SUB, SUB), SUB)
            ahead = [gated[pl.ds(4 * k + i, SUB, stride=SEG), :] for i in range(4)]
            last = long_taps + SEG - 1
            back = [gradf[pl.ds(last - 4 * k - i, SUB, stride=SEG), :] for i in range(4)]
            for e, value in enumerate(combine(ahead) + combine(back)):
                comb[e, at, :] = value

        slot(c, first_slots + 3)

        outs = SEG // 4 + 1

        @pl.loop(0, 2 * COMBOS)
        def _(e):
            te = lax.rem(e, COMBOS)
            sums = [None] * outs
            seen = {}
            for k in range(PHASE_TAPS):
                weight = taps[te, k * SUB : (k + 1) * SUB, :]
                for n in range(outs):
                    at = n + PHASE_TAPS - 1 - k
                    if at not in seen:
                        seen[at] = comb[e, at * SUB : (at + 1) * SUB, :]
                    term = weight * seen[at]
                    sums[n] = term if sums[n] is None else sums[n] + term
            for n in range(outs):
                sub[e, n * SUB : (n + 1) * SUB, :] = sums[n]

        skip = spread(skip_ref[:, cols], SUB)

        @pl.loop(0, SEG // 4)
        def _(n):
            before = pl.ds(pl.multiple_of(n * SUB, SUB), SUB)
            now = pl.ds(pl.multiple_of((n + 1) * SUB, SUB), SUB)

            def outputs(first):
                def pair(e):
                    v0, v1, v2 = (sub[first + e + i, now, :] for i in range(3))
                    return v0 + sub[first + e + 1, before, :], v2 - v0 - v1

                a_e, a_o = pair(0)
                b_e, b_o = pair(3)
                c_e, c_o = pair(6)
                b_was = (
                    sub[first + 5, before, :] - sub[first + 3, before, :] - sub[first + 4, before, :]
                )
                return (a_e + b_was, c_e - a_e - b_e, a_o + b_e, c_o - a_o - b_o)

            for i, value in enumerate(outputs(0)):
                here = pl.ds(4 * n + i, SUB, stride=SEG)
                filtered = value + skip * gated[pl.ds(long_taps + 4 * n + i, SUB, stride=SEG), :]
                gs0[here, :] = rounded(cot[here, :] * filtered)
                mix[here, :] = query[here, :] * filtered
            for i, value in enumerate(outputs(COMBOS)):
                first = SEG - 1 - 4 * n - i
                here = pl.ds(first, SUB, stride=SEG)
                grad_gated = value + skip * gradf[here, :]
                gs1[here, :] = rounded(grad_gated * valued[here, :])
                gs2[here, :] = rounded(grad_gated * keyed[here, :])

        done = (query, keyed, valued)

        @pl.loop(0, OUT_SEG // OUT_STEP)
        def _(b):
            for g, ref in enumerate((gs0, gs1, gs2)):
                value = short(ref, g, b * OUT_STEP, 1, OUT_STEP, OUT_SEG)
                for i in range(OUT_STEP):
                    done[g][pl.ds(b * OUT_STEP + i, SUB, stride=OUT_SEG), :] = value[i]

        @pl.loop(0, rows // BLOCK)
        def _(i):
            here = pl.ds(pl.multiple_of(i * BLOCK, BLOCK), BLOCK)
            mixed_ref[here, cols] = mix[here, :].astype(bf16)
            for g in range(3):
                gp[here, pl.ds(g * lanes, lanes)] = done[g][here, :].astype(bf16)

    pl.loop(0, chunks)(chunk_step)

    cols = tokgrad_ref.shape[1]
    tile = ready.shape[2]
    steps = cols // tile
    width = mate.shape[1]
    adapter_terms(chunks - 1)
    part_a = jnp.dot(through[...].astype(bf16), tokens_ref[body_rows, :], preferred_element_type=f32)
    for d in range(count):
        terms[d, :, pl.ds(0, width)] = part_a[:, d * width : (d + 1) * width]

    first = []
    for d in range(1, count):
        peer = lax.rem(me + d, count)
        first.append(
            pltpu.make_async_remote_copy(
                src_ref=terms.at[peer], dst_ref=held.at[d], send_sem=send_one.at[d],
                recv_sem=recv_one.at[d], device_id={"ctx": peer}, device_id_type=MESH,
            )
        )
        first[-1].start()
    half_lines = lines // 2
    for t in range(steps):
        value = token_terms(chunks - 1, other * half_lines + t // 2, t % 2)
        ready[t] = value.astype(bf16)
        token_copy(t).start()
    own = terms[me]
    for d in range(1, count):
        first[d - 1].wait()
        own = own + held[d]
    total[...] = own
    tp_copy = pltpu.make_async_remote_copy(
        src_ref=total.at[:, pl.ds(0, width)], dst_ref=mate, send_sem=send_tp, recv_sem=recv_tp,
        device_id={"tp": other}, device_id_type=MESH,
    )
    tp_copy.start()
    for t in range(steps):
        token_terms(chunks - 1, mine * half_lines + t // 2, t % 2)
    tp_copy.wait()
    total[:, pl.ds(0, width)] = total[:, pl.ds(0, width)] + mate[...]
    summed[me] = total[...]
    second = []
    for d in range(1, count):
        second.append(
            pltpu.make_async_remote_copy(
                src_ref=total, dst_ref=summed.at[me], send_sem=send_two.at[d],
                recv_sem=recv_two.at[d], device_id={"ctx": lax.rem(me + d, count)},
                device_id_type=MESH,
            )
        )
        second[-1].start()

    @pl.loop(0, steps)
    def _(t):
        token_copy(t).wait()
        at = pl.multiple_of(t * tile, tile)
        from_at = pl.multiple_of(mine * cols + t * tile, tile)
        tokgrad_ref[:, pl.ds(at, tile)] = (
            acc[:, pl.ds(from_at, tile)] + landed[t].astype(f32)
        ).astype(bf16)

    @pl.loop(0, subs)
    def _(n):
        ref = whole.at[pl.ds(0, 7), 0, 0, 0]
        pltpu.make_async_remote_copy(
            src_ref=ref, dst_ref=ref, send_sem=sent.at[n], recv_sem=r0.at[n],
            device_id={"tp": other}, device_id_type=MESH,
        ).wait_send()

    @pl.when(has_next)
    def _():
        for c in range(chunks):
            edge(0, c).wait_send()

    @pl.when(has_last)
    def _():
        for c in range(chunks):
            edge(1, c).wait_send()

    for copy in second:
        copy.wait()
    sums_ref[...] = summed[...]


def block(weight, own_rows, adapter_a, adapter_b, tokens, cotangent, short, long, skip, count):
    rank = adapter_a.shape[1]
    rows, features = tokens.shape
    channels = long.shape[1]
    chunks = channels // CHUNK_LANES
    lanes = CHUNK_LANES
    width = features // count
    cols = features // 2
    tile = 256
    up = adapter_b.reshape(rank, 3, chunks, lanes).transpose(2, 0, 1, 3).reshape(chunks, rank, 3 * lanes)
    vmem = pl.BlockSpec(memory_space=pltpu.VMEM)
    f32, bf16 = jnp.float32, jnp.bfloat16
    seg_rows = SUB * SEG
    reach = seg_rows + long.shape[0]
    plain = lambda n: pltpu.VMEM((n, lanes), f32)
    dma = pltpu.SemaphoreType.DMA
    subs = chunks * QUARTERS
    terms = (count, rank, width + 3 * lanes)
    reach_back = long.shape[0] + EDGE
    scratch = [
        pltpu.VMEM((rows + 2 * EDGE, features), bf16),
        pltpu.VMEM((seg_rows, channels), bf16),
        pltpu.VMEM((chunks, long.shape[0], lanes), bf16),
        pltpu.VMEM((chunks, reach_back, lanes), bf16),
        pltpu.VMEM((chunks, long.shape[0], lanes), bf16),
        pltpu.VMEM((chunks, reach_back, lanes), bf16),
        pltpu.VMEM((chunks, count // 2, 2, QUARTERS, 2, PIECE, 3 * lanes), bf16),
        plain(rows + 2 * EDGE), plain(rows + 2 * EDGE), plain(rows + 2 * EDGE),
        plain(seg_rows), plain(seg_rows), plain(seg_rows), plain(reach), plain(seg_rows), plain(reach),
        plain(seg_rows), plain(seg_rows), plain(seg_rows), plain(seg_rows),
        pltpu.VMEM((2 * COMBOS, (PHASE_TAPS + SEG // 4) * SUB, lanes), f32),
        pltpu.VMEM((COMBOS, PHASE_TAPS * SUB, lanes), f32),
        pltpu.VMEM((2 * COMBOS, (SEG // 4 + 1) * SUB, lanes), f32),
        pltpu.VMEM((rows, 3 * lanes), bf16),
        pltpu.VMEM((rows, features), f32),
        pltpu.VMEM((rank, rows), bf16),
        pltpu.VMEM((rank, rows), f32),
        pltpu.VMEM(terms, f32),
        pltpu.VMEM(terms, f32),
        pltpu.VMEM(terms[1:], f32),
        pltpu.VMEM((rank, width), f32),
        pltpu.VMEM(terms, f32),
        pltpu.VMEM((cols // tile, rows, tile), bf16),
        pltpu.VMEM((cols // tile, rows, tile), bf16),
        dma((2,)), dma((3,)), dma((3,)), dma((2, chunks)), dma((2, chunks)),
        dma((subs,)), dma((subs,)), dma((subs,)), dma((subs,)),
        dma((count,)), dma((count,)), dma((count,)), dma((count,)),
        dma, dma, dma((cols // tile,)), dma((cols // tile,)),
    ]
    mixed, grad_tokens, sums = pl.pallas_call(
        functools.partial(block_kernel, chunks, rows),
        out_shape=(
            jax.ShapeDtypeStruct((rows, channels), bf16),
            jax.ShapeDtypeStruct((rows, cols), bf16),
            jax.ShapeDtypeStruct(terms, f32),
        ),
        in_specs=[vmem] * 4 + [pl.BlockSpec(memory_space=pl.ANY)] * 2 + [vmem] * 3,
        out_specs=(vmem,) * 3,
        scratch_shapes=scratch,
        compiler_params=pltpu.CompilerParams(
            vmem_limit_bytes=58 << 20, collective_id=3, has_side_effects=True
        ),
        cost_estimate=pl.CostEstimate(
            flops=8 * rows * 3 * channels * features, bytes_accessed=20 << 20, transcendentals=0
        ),
    )(weight, own_rows, adapter_a.T, up, tokens, cotangent, short, long, skip)
    sum_a = sums[:, :, :width].transpose(1, 0, 2).reshape(rank, features)
    sum_b = sums[:, :, width:].reshape(chunks, rank, 3, lanes).transpose(1, 2, 0, 3)
    return mixed, grad_tokens, sum_a, sum_b.reshape(rank, 3 * channels)


def body(tokens, weight, adapter_a, adapter_b, short_filter, long_filter, skip_gain, cotangent):
    rows, features = tokens.shape
    share = weight.shape[0]
    channels = weight.shape[2]
    rank = adapter_a.shape[1]
    count = lax.axis_size("ctx")
    fits = (
        count == 8
        and lax.axis_size("groups") == 2
        and rows == SUB * (SEG - 4)
        and long_filter.shape[0] == 4 * PHASE_TAPS
        and short_filter.shape[0] <= BLOCK
        and channels == count * CHUNK_LANES
        and share == 2 * QUARTERS * PIECE
        and features == share * count
    )
    if not fits:
        return general_body(
            tokens, weight, adapter_a, adapter_b, short_filter, long_filter, skip_gain, cotangent
        )
    own_rows = lax.dynamic_slice_in_dim(adapter_a, lax.axis_index("ctx") * share, share, 0)
    mixed, grad_tokens, sum_a, sum_b = block(
        weight.reshape(share, 3 * channels), own_rows, adapter_a, adapter_b, tokens, cotangent,
        short_filter.reshape(-1, channels), long_filter, skip_gain.reshape(1, channels), count,
    )
    factor = adapter_scale / math.sqrt(rows * count)
    return (mixed, grad_tokens, sum_a.T * factor, (sum_b * factor).reshape(rank, 3, channels))


def solution(mesh):
    return jax.shard_map(
        body,
        mesh=mesh,
        in_specs=(
            P(("groups", "ctx"), None),
            P("ctx", None, "tp"),
            P(),
            P(None, None, "tp"),
            P(None, None, "tp"),
            P(None, "tp"),
            P("tp"),
            P(("groups", "ctx"), "tp"),
        ),
        out_specs=(
            P(("groups", "ctx"), "tp"),
            P(("groups", "ctx"), "tp"),
            P("groups", None),
            P("groups", None, "tp"),
        ),
        check_vma=False,
    )
```

```python
import functools
import math

import jax
import jax.numpy as jnp
from jax import lax
from jax.experimental import pallas as pl
from jax.experimental.pallas import tpu as pltpu
from jax.sharding import PartitionSpec as P

adapter_scale = 0.03125
LANES = 128
SUB = 8
BLOCK = 16
CHUNK = 32


def shifted(value, axis, steps):
    count = lax.axis_size(axis)
    initial, last = (max(0, -steps), min(count, count - steps))
    return lax.ppermute(value, axis, [(source, source + steps) for source in range(initial, last)])


def tiles(ref, first, count):
    start = first * SUB
    if not isinstance(start, int):
        start = pl.multiple_of(start, SUB)
    return ref[pl.ds(start, count * SUB), :].reshape(count, SUB, LANES)


def put(ref, first, value):
    count = value.shape[0]
    ref[pl.ds(pl.multiple_of(first * SUB, SUB), count * SUB), :] = value.reshape(count * SUB, LANES)


def rounded(value):
    return value.astype(jnp.bfloat16).astype(jnp.float32)


def mixer_kernel(
    rows, halo, packed_ref, cot_ref, short_ref, long_ref, skip_ref, mixed_ref, grad_ref,
    p0, p1, p2, cot, query, keyed, valued, gated, gradf,
):
    channels = SUB * LANES
    short_taps = short_ref.shape[0] // 3
    long_taps = long_ref.shape[0]
    spread = (p0, p1, p2)
    front = halo - long_taps

    @pl.loop(0, (rows + 2 * halo) // BLOCK)
    def _(i):
        at = pl.multiple_of(i * BLOCK, BLOCK)
        for g in range(3):
            for s in range(SUB):
                piece = packed_ref[pl.ds(at, BLOCK), pl.ds(g * channels + s * LANES, LANES)]
                spread[g][pl.ds(at * SUB + s, BLOCK, stride=SUB), :] = piece.astype(jnp.float32)

    @pl.loop(0, (rows + halo) // BLOCK)
    def _(i):
        at = pl.multiple_of(i * BLOCK, BLOCK)
        for s in range(SUB):
            piece = cot_ref[pl.ds(at, BLOCK), pl.ds(s * LANES, LANES)]
            cot[pl.ds(at * SUB + s, BLOCK, stride=SUB), :] = piece.astype(jnp.float32)

    def short(ref, g, first, sign):
        total = None
        for j in range(short_taps):
            term = short_ref[j * 3 + g][None] * tiles(ref, first + sign * j, SUB)
            total = term if total is None else total + term
        return total

    @pl.loop(0, (rows + BLOCK + long_taps) // SUB)
    def _(i):
        at = i * SUB
        key = short(p1, 1, at + front, -1)
        val = short(p2, 2, at + front, -1)
        put(keyed, at, key)
        put(valued, at, val)
        put(gated, at, rounded(key * val))

    @pl.loop(0, (rows + halo) // SUB)
    def _(i):
        at = i * SUB
        que = short(p0, 0, at + halo, -1)
        put(query, at, que)
        put(gradf, at, rounded(que * tiles(cot, at, SUB)))

    zero = tuple(jnp.zeros((SUB, LANES), jnp.float32) for _ in range(BLOCK))

    def long_sum(ref, base, sign):
        def chunk(c, acc):
            acc = list(acc)
            tap0 = c * CHUNK
            origin = base + sign * tap0
            low = origin - (CHUNK - 1) if sign < 0 else origin
            seen = {}

            def at(k):
                if k not in seen:
                    seen[k] = ref[pl.ds(pl.multiple_of((low + k) * SUB, SUB), SUB), :]
                return seen[k]

            for j in range(CHUNK):
                tap = long_ref[tap0 + j]
                for i in range(BLOCK):
                    k = i + (CHUNK - 1) - j if sign < 0 else i + j
                    acc[i] = acc[i] + tap * at(k)
            return tuple(acc)

        return lax.fori_loop(0, long_taps // CHUNK, chunk, zero)

    @pl.loop(0, (rows + BLOCK) // BLOCK)
    def _(b):
        at = b * BLOCK
        skip = skip_ref[...]
        ahead = jnp.stack(long_sum(gated, at + long_taps, -1))
        filtered = ahead + skip[None] * tiles(gated, at + long_taps, BLOCK)
        back = jnp.stack(long_sum(gradf, at, 1))
        grad_gated = back + skip[None] * tiles(gradf, at, BLOCK)
        put(p0, at, rounded(tiles(cot, at, BLOCK) * filtered))
        put(p1, at, rounded(grad_gated * tiles(valued, at + long_taps, BLOCK)))
        put(p2, at, rounded(grad_gated * tiles(keyed, at + long_taps, BLOCK)))
        put(gated, at, tiles(query, at, BLOCK) * filtered)

    results = (query, keyed, valued)

    @pl.loop(0, rows // SUB)
    def _(i):
        at = i * SUB
        for g in range(3):
            put(results[g], at, short(spread[g], g, at, 1))

    @pl.loop(0, rows // BLOCK)
    def _(i):
        at = pl.multiple_of(i * BLOCK, BLOCK)
        for s in range(SUB):
            pick = pl.ds(at * SUB + s, BLOCK, stride=SUB)
            mixed_ref[pl.ds(at, BLOCK), pl.ds(s * LANES, LANES)] = gated[pick, :].astype(jnp.bfloat16)
            for g in range(3):
                grad_ref[pl.ds(at, BLOCK), pl.ds(g * channels + s * LANES, LANES)] = results[g][
                    pick, :
                ].astype(jnp.bfloat16)


def mixer(packed, cot, short_filter, long_filter, skip_gain, rows, halo):
    channels = long_filter.shape[1]
    long_taps = long_filter.shape[0]
    full = (rows + 2 * halo) * SUB
    side = (rows + halo) * SUB
    scratch = [pltpu.VMEM((full, LANES), jnp.float32)] * 3 + [
        pltpu.VMEM((side, LANES), jnp.float32)
    ] * 6
    return pl.pallas_call(
        functools.partial(mixer_kernel, rows, halo),
        out_shape=(
            jax.ShapeDtypeStruct((rows, channels), jnp.bfloat16),
            jax.ShapeDtypeStruct((rows, 3 * channels), jnp.bfloat16),
        ),
        in_specs=[pl.BlockSpec(memory_space=pltpu.VMEM)] * 5,
        out_specs=(pl.BlockSpec(memory_space=pltpu.VMEM),) * 2,
        scratch_shapes=scratch,
        compiler_params=pltpu.CompilerParams(vmem_limit_bytes=52 << 20),
        cost_estimate=pl.CostEstimate(
            flops=4 * rows * channels * (long_taps + 42), bytes_accessed=12 << 20, transcendentals=0
        ),
    )(
        packed,
        cot,
        short_filter.reshape(-1, SUB, LANES),
        long_filter.reshape(long_taps, SUB, LANES),
        skip_gain.reshape(SUB, LANES),
    )


def finish_kernel(
    count, grad_ref, whole_ref, terms_ref, tokens_ref, sums_ref,
    held, total, mate, summed, ready, landed,
    send_one, recv_one, send_two, recv_two, send_tp, recv_tp, send_tok, recv_tok,
):
    me = lax.axis_index("ctx")
    mine = lax.axis_index("tp")
    other = 1 - mine
    width = mate.shape[1]
    cols = tokens_ref.shape[1]
    tile = ready.shape[2]
    steps = cols // tile

    barrier = pltpu.get_barrier_semaphore()
    for d in range(1, count):
        pl.semaphore_signal(
            barrier, inc=1, device_id={"ctx": lax.rem(me + d, count)}, device_id_type=pl.DeviceIdType.MESH
        )
    pl.semaphore_signal(barrier, inc=1, device_id={"tp": other}, device_id_type=pl.DeviceIdType.MESH)
    pl.semaphore_wait(barrier, count)

    first = []
    for d in range(1, count):
        peer = lax.rem(me + d, count)
        first.append(
            pltpu.make_async_remote_copy(
                src_ref=terms_ref.at[peer],
                dst_ref=held.at[d],
                send_sem=send_one.at[d],
                recv_sem=recv_one.at[d],
                device_id={"ctx": peer},
                device_id_type=pl.DeviceIdType.MESH,
            )
        )
        first[-1].start()

    def product(half, t):
        at = pl.multiple_of(half * cols + t * tile, tile)
        return lax.dot_general(
            grad_ref[...],
            whole_ref[pl.ds(at, tile), :],
            (((1,), (1,)), ((), ())),
            preferred_element_type=jnp.float32,
        )

    def token_copy(t):
        return pltpu.make_async_remote_copy(
            src_ref=ready.at[t],
            dst_ref=landed.at[t],
            send_sem=send_tok.at[t],
            recv_sem=recv_tok.at[t],
            device_id={"tp": other},
            device_id_type=pl.DeviceIdType.MESH,
        )

    @pl.loop(0, steps)
    def _(t):
        ready[t] = product(other, t).astype(jnp.bfloat16)
        token_copy(t).start()

    own = terms_ref[me]
    for d in range(1, count):
        first[d - 1].wait()
        own = own + held[d]
    total[...] = own
    tp_copy = pltpu.make_async_remote_copy(
        src_ref=total.at[:, pl.ds(0, width)],
        dst_ref=mate,
        send_sem=send_tp,
        recv_sem=recv_tp,
        device_id={"tp": other},
        device_id_type=pl.DeviceIdType.MESH,
    )
    tp_copy.start()

    def own_tile(t):
        value = product(mine, t)
        token_copy(t).wait()
        at = pl.multiple_of(t * tile, tile)
        tokens_ref[:, pl.ds(at, tile)] = (value + landed[t].astype(jnp.float32)).astype(jnp.bfloat16)

    pl.loop(0, steps // 4)(own_tile)
    tp_copy.wait()
    total[:, pl.ds(0, width)] = total[:, pl.ds(0, width)] + mate[...]
    summed[me] = total[...]
    second = []
    for d in range(1, count):
        second.append(
            pltpu.make_async_remote_copy(
                src_ref=total,
                dst_ref=summed.at[me],
                send_sem=send_two.at[d],
                recv_sem=recv_two.at[d],
                device_id={"ctx": lax.rem(me + d, count)},
                device_id_type=pl.DeviceIdType.MESH,
            )
        )
        second[-1].start()
    pl.loop(steps // 4, steps)(own_tile)
    for copy in second:
        copy.wait()
    sums_ref[...] = summed[...]


def finish(grad_packed, whole, part_a, part_b, count):
    rank, features = part_a.shape
    rows, wide = grad_packed.shape
    width, rest = features // count, wide // count
    cols = features // 2
    tile = 256
    terms = jnp.concatenate(
        [part_a.reshape(rank, count, width), part_b.reshape(rank, count, rest)], axis=2
    ).transpose(1, 0, 2)
    vmem = pl.BlockSpec(memory_space=pltpu.VMEM)
    grad_tokens, sums = pl.pallas_call(
        functools.partial(finish_kernel, count),
        out_shape=(
            jax.ShapeDtypeStruct((rows, cols), jnp.bfloat16),
            jax.ShapeDtypeStruct(terms.shape, jnp.float32),
        ),
        in_specs=[vmem] * 3,
        out_specs=(vmem, vmem),
        scratch_shapes=[
            pltpu.VMEM(terms.shape, jnp.float32),
            pltpu.VMEM((rank, width + rest), jnp.float32),
            pltpu.VMEM((rank, width), jnp.float32),
            pltpu.VMEM(terms.shape, jnp.float32),
            pltpu.VMEM((cols // tile, rows, tile), jnp.bfloat16),
            pltpu.VMEM((cols // tile, rows, tile), jnp.bfloat16),
            pltpu.SemaphoreType.DMA((count,)),
            pltpu.SemaphoreType.DMA((count,)),
            pltpu.SemaphoreType.DMA((count,)),
            pltpu.SemaphoreType.DMA((count,)),
            pltpu.SemaphoreType.DMA,
            pltpu.SemaphoreType.DMA,
            pltpu.SemaphoreType.DMA((cols // tile,)),
            pltpu.SemaphoreType.DMA((cols // tile,)),
        ],
        compiler_params=pltpu.CompilerParams(
            vmem_limit_bytes=48 << 20, collective_id=1, has_side_effects=True
        ),
        cost_estimate=pl.CostEstimate(
            flops=2 * rows * wide * features, bytes_accessed=20 << 20, transcendentals=0
        ),
    )(grad_packed, whole, terms)
    flat = sums.transpose(1, 0, 2)
    return (
        grad_tokens,
        flat[:, :, :width].reshape(rank, features),
        flat[:, :, width:].reshape(rank, wide),
    )


MESH = pl.DeviceIdType.MESH
PIECES = 4


def gather_kernel(
    outer, shard_ref, out_ref, z_send, z_recv, y_send, y_recv, x_send, x_recv, local_sem
):
    me = lax.axis_index("ctx")
    x = lax.axis_index("groups")
    z, y = me // 2, lax.rem(me, 2)
    rows = shard_ref.shape[0]
    piece = rows // PIECES
    half = piece // 2
    last = outer - 2
    steps = outer - 1

    def ctx_of(line, pair):
        return {"ctx": line * 2 + pair}

    def span(line, pair, start, size):
        return pl.ds(pl.multiple_of((line * 2 + pair) * rows + start, half), size)

    def part(p, side):
        return p * piece + side * half

    def copy(src, dst, send, recv, device):
        return pltpu.make_async_remote_copy(
            src_ref=src, dst_ref=dst, send_sem=send, recv_sem=recv, device_id=device, device_id_type=MESH
        )

    def z_range(k, p):
        return (part(p, x), half) if k == last else (p * piece, piece)

    def z_out(way, k, p):
        step = 1 - 2 * way
        start, size = z_range(k, p)
        place = span(z - step * k, y, start, size)
        src = out_ref.at[place] if k else shard_ref.at[pl.ds(pl.multiple_of(start, half), size)]
        return copy(
            src, out_ref.at[place], z_send.at[way, k, p], z_recv.at[way, k, p], ctx_of(z + step, y)
        )

    def z_in(way, k, p):
        step = 1 - 2 * way
        start, size = z_range(k, p)
        place = out_ref.at[span(z - step * (k + 1), y, start, size)]
        return copy(place, place, z_send.at[way, k, p], z_recv.at[way, k, p], ctx_of(z - step, y))

    def sends(way, k):
        return (z < steps) & (z >= k) if way == 0 else (z > 0) & (z + k <= steps)

    def receives(way, k):
        return z > k if way == 0 else z + k < steps

    def line_of(i):
        if i == 0:
            return z
        way, k = (i - 1) // steps, (i - 1) % steps
        return z - (1 - 2 * way) * (k + 1)

    def item(way, k):
        return 1 + way * steps + k

    def y_out(i, p):
        start = part(p, x)
        place = span(line_of(i), y, start, half)
        src = out_ref.at[place] if i else shard_ref.at[pl.ds(pl.multiple_of(start, half), half)]
        return copy(src, out_ref.at[place], y_send.at[i, p], y_recv.at[i, p], ctx_of(z, 1 - y))

    def y_in(i, p):
        place = out_ref.at[span(line_of(i), 1 - y, part(p, x), half)]
        return copy(place, place, y_send.at[i, p], y_recv.at[i, p], ctx_of(z, 1 - y))

    def x_copy(i, p, side):
        if i > 2 * steps:
            line, pair = line_of(item(i - 2 * steps - 1, last)), y
        else:
            line, pair = line_of(i), 1 - y
        place = out_ref.at[span(line, pair, part(p, side), half)]
        return copy(place, place, x_send.at[i, p], x_recv.at[i, p], {"groups": 1 - x})

    def extra(way):
        return 2 * steps + 1 + way

    barrier = pltpu.get_barrier_semaphore()
    pl.semaphore_signal(barrier, inc=1, device_id=ctx_of(z, 1 - y), device_id_type=MESH)
    pl.semaphore_signal(barrier, inc=1, device_id={"groups": 1 - x}, device_id_type=MESH)
    for step in (1, outer - 1):
        pl.semaphore_signal(
            barrier, inc=1, device_id=ctx_of(lax.rem(z + step, outer), y), device_id_type=MESH
        )
    pl.semaphore_wait(barrier, 4)

    @pl.loop(0, PIECES)
    def _(p):
        for way in range(2):
            @pl.when(sends(way, 0))
            def _():
                z_out(way, 0, p).start()
        y_out(0, p).start()

    own = pltpu.make_async_copy(
        shard_ref, out_ref.at[pl.ds(pl.multiple_of(me * rows, rows), rows)], local_sem
    )
    own.start()

    def pass_on(k, p):
        for way in range(2):
            @pl.when(receives(way, k))
            def _():
                i = item(way, k)
                y_in(i, p).wait_recv()
                x_copy(i, p, x).start()

    for k in range(steps):
        @pl.loop(0, PIECES)
        def _(p):
            for way in range(2):
                @pl.when(receives(way, k))
                def _():
                    z_in(way, k, p).wait_recv()
                    if k < last:
                        @pl.when(sends(way, k + 1))
                        def _():
                            z_out(way, k + 1, p).start()
                    y_out(item(way, k), p).start()
                    if k == last:
                        x_copy(extra(way), p, x).start()
            if k == 0:
                y_in(0, p).wait_recv()
                x_copy(0, p, x).start()

            @pl.when(p > 0)
            def _():
                pass_on(k, p - 1)

            if k > 0:
                @pl.when(p == 0)
                def _():
                    pass_on(k - 1, PIECES - 1)

    pass_on(last, PIECES - 1)
    own.wait()

    @pl.loop(0, PIECES)
    def _(p):
        x_copy(0, p, 1 - x).wait_recv()
        x_copy(0, p, x).wait_send()
        y_out(0, p).wait_send()
        for way in range(2):
            for k in range(steps):
                @pl.when(sends(way, k))
                def _():
                    z_out(way, k, p).wait_send()

                @pl.when(receives(way, k))
                def _():
                    i = item(way, k)
                    x_copy(i, p, 1 - x).wait_recv()
                    x_copy(i, p, x).wait_send()
                    y_out(i, p).wait_send()
                    if k == last:
                        x_copy(extra(way), p, 1 - x).wait_recv()
                        x_copy(extra(way), p, x).wait_send()


def gather(merged, count):
    rows, wide = merged.shape
    outer = count // 2
    items = 2 * (outer - 1) + 1
    dma = pltpu.SemaphoreType.DMA
    hbm = pl.BlockSpec(memory_space=pl.ANY)
    return pl.pallas_call(
        functools.partial(gather_kernel, outer),
        out_shape=jax.ShapeDtypeStruct((rows * count, wide), merged.dtype),
        in_specs=[hbm],
        out_specs=hbm,
        scratch_shapes=[
            dma((2, outer - 1, PIECES)),
            dma((2, outer - 1, PIECES)),
            dma((items, PIECES)),
            dma((items, PIECES)),
            dma((items + 2, PIECES)),
            dma((items + 2, PIECES)),
            dma,
        ],
        compiler_params=pltpu.CompilerParams(collective_id=2, has_side_effects=True),
        cost_estimate=pl.CostEstimate(flops=0, bytes_accessed=300 << 20, transcendentals=0),
    )(merged)


def general_body(tokens, weight, adapter_a, adapter_b, short_filter, long_filter, skip_gain, cotangent):
    row_count = tokens.shape[0]
    share_rows = weight.shape[0]
    channels = weight.shape[2]
    features = tokens.shape[1]
    adapter_rank = adapter_a.shape[1]
    halo = long_filter.shape[0] + BLOCK
    count = lax.axis_size("ctx")
    seq_total = row_count * count
    first_row = lax.axis_index("ctx") * share_rows
    before = shifted(tokens[row_count - halo :], "ctx", 1)
    after = shifted(tokens[:halo], "ctx", -1)
    cot_after = shifted(cotangent[:halo], "ctx", -1)
    tokens_ext = jnp.concatenate([before, tokens, after], axis=0)
    cot_ext = jnp.concatenate([cotangent, cot_after], axis=0)
    own_rows = lax.dynamic_slice_in_dim(adapter_a, first_row, share_rows, 0)
    flat_b = adapter_b.reshape(adapter_rank, 3 * channels)
    delta_w = jnp.dot(own_rows, flat_b, preferred_element_type=jnp.float32)
    merged = (
        weight.reshape(share_rows, 3 * channels).astype(jnp.float32) + adapter_scale * delta_w
    ).astype(jnp.bfloat16)
    if count == 8 and lax.axis_size("groups") == 2:
        whole = gather(merged, count)
    else:
        whole = lax.all_gather(merged, "ctx", axis=0, tiled=True)
    packed = jnp.dot(tokens_ext, whole, preferred_element_type=jnp.float32).astype(jnp.bfloat16)
    mixed, grad_packed = mixer(
        packed, cot_ext, short_filter, long_filter, skip_gain, row_count, halo
    )
    projected = jnp.dot(tokens, adapter_a, preferred_element_type=jnp.float32).astype(jnp.bfloat16)
    part_b = lax.dot_general(
        projected, grad_packed, (((0,), (0,)), ((), ())), preferred_element_type=jnp.float32
    )
    through = lax.dot_general(
        flat_b, grad_packed, (((1,), (1,)), ((), ())), preferred_element_type=jnp.float32
    ).astype(jnp.bfloat16)
    part_a = jnp.dot(through, tokens, preferred_element_type=jnp.float32)
    if features % (LANES * count) == 0 and (3 * channels) % (LANES * count) == 0:
        grad_tokens, sum_a, sum_b = finish(grad_packed, whole, part_a, part_b, count)
    else:
        sum_a = lax.psum(part_a, ("ctx", "tp"))
        sum_b = lax.psum(part_b, "ctx")
        partial_grad = lax.dot_general(
            grad_packed, whole, (((1,), (1,)), ((), ())), preferred_element_type=jnp.float32
        )
        grad_tokens = lax.psum_scatter(
            partial_grad.astype(jnp.bfloat16), "tp", scatter_dimension=1, tiled=True
        )
    sum_a = sum_a.T
    factor = adapter_scale / math.sqrt(seq_total)
    return (mixed, grad_tokens, sum_a * factor, (sum_b * factor).reshape(adapter_rank, 3, channels))


CHUNK_LANES = 128
QUARTERS = 4
LAGS = (2, 4, 6, 8)
WHOLE_Z = (1, 3)
HALF_Y = (2,)
PIECE = 32
SEG = 68
COMBOS = 9
PHASE_TAPS = 32
OUT_SEG = 66
OUT_STEP = 11
EDGE = 16


def combine(p):
    p02, p13, p01, p23 = p[0] + p[2], p[1] + p[3], p[0] + p[1], p[2] + p[3]
    return (p[0], p[2], p02, p[1], p[3], p13, p01, p23, p01 + p23)


def block_kernel(
    chunks, rows,
    weight_ref, down_ref, wide_ref, tokens_hbm, cot_hbm, short_ref, long_ref, skip_ref,
    mixed_ref, tokgrad_ref, sums_ref,
    up_ref, tokens_ref, cot_ref, hold_g, hold_f, edge_g, edge_f,
    whole, pk0, pk1, pk2, cot, keyed, valued, gated, query, gradf, gs0, gs1, gs2, mix,
    comb, taps, sub, gp, acc, proj, through, terms, held, total, mate, summed, ready, landed,
    load_sem, near_send, near_recv, edge_send, edge_recv,
    sent, came, send_one, recv_one, send_two, recv_two, send_tp, recv_tp, send_tok, recv_tok,
):
    me = lax.axis_index("ctx")
    x = lax.axis_index("groups")
    mine = lax.axis_index("tp")
    other = 1 - mine
    z, y = me // 2, lax.rem(me, 2)
    count = chunks
    lines = count // 2
    subs = chunks * QUARTERS
    lanes = CHUNK_LANES
    f32, bf16 = jnp.float32, jnp.bfloat16
    pk = (pk0, pk1, pk2)
    long_taps = long_ref.shape[0]
    short_taps = short_ref.shape[0] // 3
    channels = chunks * lanes
    halo = EDGE
    has_next, has_last = me < count - 1, me > 0
    to_next = {"ctx": lax.rem(me + 1, count)}
    to_last = {"ctx": lax.rem(me + count - 1, count)}

    loads = (
        pltpu.make_async_copy(tokens_hbm, tokens_ref.at[pl.ds(halo, rows)], load_sem.at[0]),
        pltpu.make_async_copy(cot_hbm, cot_ref.at[pl.ds(0, rows)], load_sem.at[1]),
    )
    for copy in loads:
        copy.start()

    barrier = pltpu.get_barrier_semaphore()
    for d in range(1, count):
        pl.semaphore_signal(
            barrier, inc=1, device_id={"ctx": lax.rem(me + d, count)}, device_id_type=MESH
        )
    pl.semaphore_signal(barrier, inc=1, device_id={"tp": other}, device_id_type=MESH)
    pl.semaphore_signal(barrier, inc=1, device_id={"groups": 1 - x}, device_id_type=MESH)

    def merge(c):
        own = pl.ds(pl.multiple_of(me * weight_ref.shape[1], weight_ref.shape[1]), weight_ref.shape[1])
        delta = lax.dot_general(
            down_ref[:, own], up_ref[c], (((0,), (0,)), ((), ())), preferred_element_type=f32
        )
        for g in range(3):
            value = weight_ref[g, :, c * lanes : (c + 1) * lanes].astype(f32) + adapter_scale * delta[:, g * lanes : (g + 1) * lanes]
            whole[c, z, y, :, :, :, pl.ds(g * lanes, lanes)] = value.astype(bf16).reshape(
                QUARTERS, 2, PIECE, lanes
            )

    def send(ref, sub_at, stage, device):
        pltpu.make_async_remote_copy(
            src_ref=ref, dst_ref=ref, send_sem=sent.at[stage, sub_at], recv_sem=came.at[stage, sub_at],
            device_id=device, device_id_type=MESH,
        ).start()

    def whole_wait(ref, sub_at, stage):
        return pltpu.make_async_remote_copy(
            src_ref=ref, dst_ref=ref, send_sem=sent.at[stage, sub_at], recv_sem=came.at[stage, sub_at],
            device_id={"tp": other}, device_id_type=MESH,
        )

    def arrived(ref, sub_at, stage):
        whole_wait(ref, sub_at, stage).wait_recv()

    def line(d):
        return lax.rem(z + d, lines)

    side = z // 2
    inner = lax.rem(z + side, 2) == 1
    outer = jnp.logical_not(inner)
    beside = z + 1 - 2 * lax.rem(z, 2)
    across = 2 - side
    to_x = {"groups": 1 - x}
    to_y = {"ctx": z * 2 + 1 - y}
    to_beside = {"ctx": beside * 2 + y}

    def z_blocks(q, many):
        if q in WHOLE_Z:
            return whole.at[0, 0, 0, pl.ds(0, many)]
        return whole.at[pl.ds(0, many), 0, 0, 0, 0]

    def stage0(c, q):
        n = c * QUARTERS + q
        ref = whole.at[c, z, y, q] if q in WHOLE_Z else whole.at[c, z, y, q, x]
        send(ref, n, 0, {"ctx": across * 2 + y})
        send(ref, n, 0, to_beside)

    def stage0b(c, q):
        n = c * QUARTERS + q

        @pl.when(inner)
        def _():
            arrived(z_blocks(q, 3), n, 0)
            far = pl.ds(2 - 2 * side, 2)
            send(whole.at[c, far, y, q] if q in WHOLE_Z else whole.at[c, far, y, q, x], n, 0, to_beside)

    def stage1(c, q):
        n = c * QUARTERS + q
        pl.when(outer)(lambda: arrived(z_blocks(q, 3), n, 0))
        if q not in WHOLE_Z:
            for d in range(1, lines):
                send(whole.at[c, line(d), y, q, x], n, 1, to_x)
        send(whole.at[c, :, y, q, x], n, 1, to_y)

    def stage2(c, q):
        n = c * QUARTERS + q
        arrived(whole.at[pl.ds(0, stage1_blocks(q)), 0, 0, 0, 0], n, 1)
        if q not in HALF_Y:
            send(whole.at[c, :, 1 - y, q, x], n, 2, to_x)
        else:
            half = PIECE // 2
            send(whole.at[c, :, 1 - y, q, x, pl.ds(0, half)], n, 2, to_x)
            send(whole.at[c, :, y, q, 1 - x, pl.ds(half, half)], n, 2, to_y)

    def stage1_blocks(q):
        return lines if q in WHOLE_Z else 2 * lines - 1

    def slot(base, off):
        for stage, back in zip((stage0, stage2, stage1, stage0b), (0, LAGS[2], LAGS[1], LAGS[0])):
            at = off - back
            if at < 0:
                continue
            c, q = base + at // QUARTERS, at % QUARTERS
            if isinstance(base, int):
                stage(c, q)
            else:
                pl.when(c < chunks)(functools.partial(stage, c, q))

    def near(k):
        src, dst, device = (
            (tokens_hbm.at[pl.ds(rows - halo, halo)], tokens_ref.at[pl.ds(0, halo)], to_next),
            (tokens_hbm.at[pl.ds(0, halo)], tokens_ref.at[pl.ds(rows + halo, halo)], to_last),
            (cot_hbm.at[pl.ds(0, halo)], cot_ref.at[pl.ds(rows, halo)], to_last),
        )[k]
        return pltpu.make_async_remote_copy(
            src_ref=src, dst_ref=dst, send_sem=near_send.at[k], recv_sem=near_recv.at[k],
            device_id=device, device_id_type=MESH,
        )

    def edge(k, c):
        src, dst, device = ((hold_g, edge_g, to_next), (hold_f, edge_f, to_last))[k]
        return pltpu.make_async_remote_copy(
            src_ref=src.at[c], dst_ref=dst.at[c], send_sem=edge_send.at[k, c],
            recv_sem=edge_recv.at[k, c], device_id=device, device_id_type=MESH,
        )

    for c in range(chunks):
        for g in range(3):
            up_ref[c, :, g * lanes : (g + 1) * lanes] = wide_ref[g, :, c * lanes : (c + 1) * lanes]
    merge(0)
    pl.semaphore_wait(barrier, count + 1)

    first_slots = LAGS[3] + QUARTERS - 1
    body_rows = pl.ds(halo, rows)
    for n in range(first_slots):
        slot(0, n)
        if n + 1 < chunks:
            merge(n + 1)
        if n == 0:
            pl.when(has_next)(lambda: near(0).start())

            @pl.when(has_last)
            def _():
                near(1).start()
                near(2).start()

            @pl.when(jnp.logical_not(has_last))
            def _():
                tokens_ref[pl.ds(0, halo), :] = jnp.zeros((halo, tokens_ref.shape[1]), bf16)
                edge_g[...] = jnp.zeros_like(edge_g)

            @pl.when(jnp.logical_not(has_next))
            def _():
                tokens_ref[pl.ds(rows + halo, halo), :] = jnp.zeros((halo, tokens_ref.shape[1]), bf16)
                cot_ref[pl.ds(rows, halo), :] = jnp.zeros((halo, channels), bf16)
                edge_f[...] = jnp.zeros_like(edge_f)

            tail = cot_ref.shape[0] - rows - halo
            cot_ref[pl.ds(rows + halo, tail), :] = jnp.zeros((tail, channels), bf16)
            known = rows + halo
            for ref in (query, keyed, valued):
                ref[pl.ds(known, ref.shape[0] - known), :] = jnp.zeros((ref.shape[0] - known, lanes), f32)
            after = gated.shape[0] - known - long_taps
            gated[pl.ds(known + long_taps, after), :] = jnp.zeros((after, lanes), f32)
            after = gradf.shape[0] - rows - edge_f.shape[1]
            gradf[pl.ds(rows + edge_f.shape[1], after), :] = jnp.zeros((after, lanes), f32)
        if n == first_slots - 2:
            for copy in loads:
                copy.wait()
            proj[...] = lax.dot_general(
                down_ref[...], tokens_ref[body_rows, :], (((1,), (1,)), ((), ())),
                preferred_element_type=f32,
            ).astype(bf16)
            through[...] = jnp.zeros_like(through)
        if n == first_slots - 1:
            acc[...] = jnp.zeros_like(acc)

            @pl.when(has_last)
            def _():
                near(0).wait_recv()
                near(1).wait_send()
                near(2).wait_send()

            @pl.when(has_next)
            def _():
                near(0).wait_send()
                near(1).wait_recv()
                near(2).wait_recv()

    def spread(row, count_rows):
        return jnp.broadcast_to(row, (count_rows, lanes))

    def short(ref, g, cols, first, sign, size, stride):
        seen = {}

        def at(k):
            if k not in seen:
                seen[k] = ref[pl.ds(first + k, SUB, stride=stride), :]
            return seen[k]

        result = [None] * size
        for j in range(short_taps):
            tap = spread(short_ref[j * 3 + g : j * 3 + g + 1, cols], SUB)
            for i in range(size):
                term = tap * at(i + sign * j)
                result[i] = term if j == 0 else result[i] + term
        return result

    def packed_grad(c):
        cols = pl.ds(c * lanes if isinstance(c, int) else pl.multiple_of(c * lanes, lanes), lanes)

        @pl.loop(0, OUT_SEG // OUT_STEP)
        def _(b):
            for g, ref in enumerate((gs0, gs1, gs2)):
                value = short(ref, g, cols, b * OUT_STEP, 1, OUT_STEP, OUT_SEG)
                for i in range(OUT_STEP):
                    pk[g][pl.ds(b * OUT_STEP + i, SUB, stride=OUT_SEG), :] = value[i]

        @pl.loop(0, rows // BLOCK)
        def _(i):
            here = pl.ds(pl.multiple_of(i * BLOCK, BLOCK), BLOCK)
            mixed_ref[here, cols] = mix[here, :].astype(bf16)
            for g in range(3):
                gp[here, pl.ds(g * lanes, lanes)] = pk[g][here, :].astype(bf16)

    def adapter_terms(c):
        terms[c, :, pl.ds(terms.shape[2] - 3 * lanes, 3 * lanes)] = jnp.dot(
            proj[...], gp[...], preferred_element_type=f32
        )
        through[...] += lax.dot_general(
            up_ref[c], gp[...], (((1,), (1,)), ((), ())), preferred_element_type=f32
        )

    def token_terms(c, k, pair):
        block = whole[c, k, pair].reshape(-1, 3 * lanes)
        wide = block.shape[0]
        start = (k * 2 + pair) * wide
        at = pl.ds(start if isinstance(start, int) else pl.multiple_of(start, wide), wide)
        value = acc[:, at] + lax.dot_general(
            gp[...], block, (((1,), (1,)), ((), ())), preferred_element_type=f32
        )
        acc[:, at] = value
        return value

    def token_copy(t):
        return pltpu.make_async_remote_copy(
            src_ref=ready.at[t], dst_ref=landed.at[t], send_sem=send_tok.at[t],
            recv_sem=recv_tok.at[t], device_id={"tp": other}, device_id_type=MESH,
        )

    def chunk_step(c):
        cols = pl.ds(pl.multiple_of(c * lanes, lanes), lanes)

        slot(c, first_slots)
        for q in range(QUARTERS):
            arrived(whole.at[pl.ds(0, lines), 0, 0, 0, 0], c * QUARTERS + q, 2)
        ext = tokens_ref.shape[0]
        part = ext // 2

        @pl.loop(0, 2)
        def _(r):
            at = pl.ds(pl.multiple_of(r * part, 16), part)
            value = jnp.dot(
                tokens_ref[at, :], whole[c].reshape(-1, 3 * lanes), preferred_element_type=f32
            )
            for g in range(3):
                pk[g][at, :] = rounded(value[:, g * lanes : (g + 1) * lanes])

        slot(c, first_slots + 1)

        @pl.loop(0, cot.shape[0] // BLOCK)
        def _(i):
            here = pl.ds(pl.multiple_of(i * BLOCK, BLOCK), BLOCK)
            cot[here, :] = cot_ref[here, cols].astype(f32)

        @pl.loop(0, OUT_SEG // OUT_STEP)
        def _(b):
            at = b * OUT_STEP
            key = short(pk1, 1, cols, at + halo, -1, OUT_STEP, OUT_SEG)
            val = short(pk2, 2, cols, at + halo, -1, OUT_STEP, OUT_SEG)
            for i in range(OUT_STEP):
                here = pl.ds(at + i, SUB, stride=OUT_SEG)
                keyed[here, :] = key[i]
                valued[here, :] = val[i]
                gated[pl.ds(at + i + long_taps, SUB, stride=OUT_SEG), :] = rounded(key[i] * val[i])
            que = short(pk0, 0, cols, at + halo, -1, OUT_STEP, OUT_SEG)
            for i in range(OUT_STEP):
                here = pl.ds(at + i, SUB, stride=OUT_SEG)
                query[here, :] = que[i]
                gradf[here, :] = rounded(que[i] * cot[here, :])

        hold_g[c] = gated[pl.ds(rows, long_taps), :].astype(bf16)
        hold_f[c] = gradf[pl.ds(0, edge_f.shape[1]), :].astype(bf16)
        pl.when(has_next)(lambda: edge(0, c).start())
        pl.when(has_last)(lambda: edge(1, c).start())

        @pl.when(c > 0)
        def _():
            packed_grad(c - 1)

        slot(c, first_slots + 2)

        @pl.when(c > 0)
        def _():
            adapter_terms(c - 1)
            for k in range(lines):
                for pair in range(2):
                    token_terms(c - 1, k, pair)

        @pl.loop(0, long_taps // SUB)
        def _(k):
            piece = long_ref[pl.ds(pl.multiple_of(k * SUB, SUB), SUB), cols]
            for h in range(2):
                p = [spread(piece[4 * h + i : 4 * h + i + 1], SUB) for i in range(4)]
                at = pl.ds(pl.multiple_of((2 * k + h) * SUB, SUB), SUB)
                for e, value in enumerate(combine(p)):
                    taps[e, at, :] = value

        pl.when(has_last)(lambda: edge(0, c).wait_recv())
        pl.when(has_next)(lambda: edge(1, c).wait_recv())
        gated[pl.ds(0, long_taps), :] = edge_g[c].astype(f32)
        gradf[pl.ds(rows, edge_f.shape[1]), :] = edge_f[c].astype(f32)

        span = PHASE_TAPS + SEG // 4

        @pl.loop(0, span)
        def _(k):
            at = pl.ds(pl.multiple_of(k * SUB, SUB), SUB)
            ahead = [gated[pl.ds(4 * k + i, SUB, stride=OUT_SEG), :] for i in range(4)]
            last = long_taps + SEG - 1
            back = [gradf[pl.ds(last - 4 * k - i, SUB, stride=OUT_SEG), :] for i in range(4)]
            for e, value in enumerate(combine(ahead) + combine(back)):
                comb[e, at, :] = value

        slot(c, first_slots + 3)

        outs = SEG // 4 + 1

        @pl.loop(0, 2 * COMBOS)
        def _(e):
            te = lax.rem(e, COMBOS)
            sums = [None] * outs
            seen = {}
            for k in range(PHASE_TAPS):
                weight = taps[te, k * SUB : (k + 1) * SUB, :]
                for n in range(outs):
                    at = n + PHASE_TAPS - 1 - k
                    if at not in seen:
                        seen[at] = comb[e, at * SUB : (at + 1) * SUB, :]
                    term = weight * seen[at]
                    sums[n] = term if sums[n] is None else sums[n] + term
            for n in range(outs):
                sub[e, n * SUB : (n + 1) * SUB, :] = sums[n]

        skip = spread(skip_ref[:, cols], SUB)

        def finish_rows(first_n, many):
            jobs = []
            for m in range(many):
                n = first_n + m
                before = pl.ds(n * SUB if isinstance(n, int) else pl.multiple_of(n * SUB, SUB), SUB)
                now = pl.ds((n + 1) * SUB if isinstance(n, int) else pl.multiple_of((n + 1) * SUB, SUB), SUB)
                jobs.append(([sub[e, now, :] for e in range(2 * COMBOS)],
                             {e: sub[e, before, :] for e in (1, 3, 4, 5, 7, 10, 12, 13, 14, 16)}))
            at = lambda ref, start: ref[pl.ds(start, SUB, stride=OUT_SEG), :]
            order = [(4 * (first_n + m) + i) for m in range(many) for i in range(4)]
            ahead = [(at(gated, long_taps + k), at(cot, k), at(query, k)) for k in order]
            back = [
                (at(gradf, SEG - 1 - k), at(valued, SEG - 1 - k), at(keyed, SEG - 1 - k)) for k in order
            ]

            def outputs(now, before, e):
                def pair(p):
                    v0, v1, v2 = now[e + p], now[e + p + 1], now[e + p + 2]
                    return v0 + before[e + p + 1], v2 - v0 - v1

                a_e, a_o = pair(0)
                b_e, b_o = now[e + 3] + before[e + 4], now[e + 5] - now[e + 3] - now[e + 4]
                c_e, c_o = pair(6)
                b_was = before[e + 5] - before[e + 3] - before[e + 4]
                return [a_e + b_was, c_e - a_e - b_e, a_o + b_e, c_o - a_o - b_o]

            forward, backward = [], []
            for now, before in jobs:
                forward += outputs(now, before, 0)
                backward += outputs(now, before, COMBOS)
            stores = []
            for k, value, (gate, ct, que) in zip(order, forward, ahead):
                filtered = value + skip * gate
                stores += [(gs0, k, rounded(ct * filtered)), (mix, k, que * filtered)]
            for k, value, (gf, val, key) in zip(order, backward, back):
                grad_gated = value + skip * gf
                stores += [
                    (gs1, SEG - 1 - k, rounded(grad_gated * val)), (gs2, SEG - 1 - k, rounded(grad_gated * key))
                ]
            for ref, k, value in stores:
                ref[pl.ds(k, SUB, stride=OUT_SEG), :] = value

        pl.loop(0, SEG // 8)(lambda n: finish_rows(2 * n, 2))
        finish_rows(SEG // 4 - 1, 1)

    pl.loop(0, chunks)(chunk_step)

    cols = tokgrad_ref.shape[1]
    tile = ready.shape[2]
    steps = cols // tile
    width = mate.shape[1]
    packed_grad(chunks - 1)
    adapter_terms(chunks - 1)
    part_a = jnp.dot(through[...].astype(bf16), tokens_ref[body_rows, :], preferred_element_type=f32)
    for d in range(count):
        terms[d, :, pl.ds(0, width)] = part_a[:, d * width : (d + 1) * width]

    first = []
    for d in range(1, count):
        peer = lax.rem(me + d, count)
        first.append(
            pltpu.make_async_remote_copy(
                src_ref=terms.at[peer], dst_ref=held.at[d], send_sem=send_one.at[d],
                recv_sem=recv_one.at[d], device_id={"ctx": peer}, device_id_type=MESH,
            )
        )
        first[-1].start()
    half_lines = lines // 2
    for t in range(steps):
        value = token_terms(chunks - 1, other * half_lines + t // 2, t % 2)
        ready[t] = value.astype(bf16)
        token_copy(t).start()
    own = terms[me]
    for d in range(1, count):
        first[d - 1].wait()
        own = own + held[d]
    total[...] = own
    tp_copy = pltpu.make_async_remote_copy(
        src_ref=total.at[:, pl.ds(0, width)], dst_ref=mate, send_sem=send_tp, recv_sem=recv_tp,
        device_id={"tp": other}, device_id_type=MESH,
    )
    tp_copy.start()
    for t in range(steps):
        token_terms(chunks - 1, mine * half_lines + t // 2, t % 2)
    tp_copy.wait()
    total[:, pl.ds(0, width)] = total[:, pl.ds(0, width)] + mate[...]
    summed[me] = total[...]
    second = []
    for d in range(1, count):
        second.append(
            pltpu.make_async_remote_copy(
                src_ref=total, dst_ref=summed.at[me], send_sem=send_two.at[d],
                recv_sem=recv_two.at[d], device_id={"ctx": lax.rem(me + d, count)},
                device_id_type=MESH,
            )
        )
        second[-1].start()

    @pl.loop(0, steps)
    def _(t):
        token_copy(t).wait()
        at = pl.multiple_of(t * tile, tile)
        from_at = pl.multiple_of(mine * cols + t * tile, tile)
        tokgrad_ref[:, pl.ds(at, tile)] = (
            acc[:, pl.ds(from_at, tile)] + landed[t].astype(f32)
        ).astype(bf16)

    @pl.loop(0, chunks)
    def _(c):
        for q in range(QUARTERS):
            n = c * QUARTERS + q
            pl.when(inner)(lambda: whole_wait(z_blocks(q, 4), n, 0).wait_send())
            pl.when(outer)(lambda: whole_wait(z_blocks(q, 2), n, 0).wait_send())
            whole_wait(whole.at[pl.ds(0, stage1_blocks(q)), 0, 0, 0, 0], n, 1).wait_send()
            whole_wait(whole.at[pl.ds(0, lines), 0, 0, 0, 0], n, 2).wait_send()

    @pl.when(has_next)
    def _():
        for c in range(chunks):
            edge(0, c).wait_send()

    @pl.when(has_last)
    def _():
        for c in range(chunks):
            edge(1, c).wait_send()

    for copy in second:
        copy.wait()
    sums_ref[...] = summed[...]


def block(weight, adapter_a, adapter_b, tokens, cotangent, short, long, skip, count):
    rank = adapter_a.shape[1]
    rows, features = tokens.shape
    channels = long.shape[1]
    chunks = channels // CHUNK_LANES
    lanes = CHUNK_LANES
    width = features // count
    cols = features // 2
    tile = 256
    vmem = pl.BlockSpec(memory_space=pltpu.VMEM)
    f32, bf16 = jnp.float32, jnp.bfloat16
    seg_rows = SUB * SEG
    reach = seg_rows + long.shape[0]
    plain = lambda n: pltpu.VMEM((n, lanes), f32)
    dma = pltpu.SemaphoreType.DMA
    subs = chunks * QUARTERS
    terms = (count, rank, width + 3 * lanes)
    reach_back = long.shape[0] + EDGE
    scratch = [
        pltpu.VMEM((chunks, rank, 3 * lanes), bf16),
        pltpu.VMEM((rows + 2 * EDGE, features), bf16),
        pltpu.VMEM((seg_rows, channels), bf16),
        pltpu.VMEM((chunks, long.shape[0], lanes), bf16),
        pltpu.VMEM((chunks, reach_back, lanes), bf16),
        pltpu.VMEM((chunks, long.shape[0], lanes), bf16),
        pltpu.VMEM((chunks, reach_back, lanes), bf16),
        pltpu.VMEM((chunks, count // 2, 2, QUARTERS, 2, PIECE, 3 * lanes), bf16),
        plain(rows + 2 * EDGE), plain(rows + 2 * EDGE), plain(rows + 2 * EDGE),
        plain(seg_rows), plain(seg_rows), plain(seg_rows), plain(reach), plain(seg_rows), plain(reach),
        plain(seg_rows), plain(seg_rows), plain(seg_rows), plain(seg_rows),
        pltpu.VMEM((2 * COMBOS, (PHASE_TAPS + SEG // 4) * SUB, lanes), f32),
        pltpu.VMEM((COMBOS, PHASE_TAPS * SUB, lanes), f32),
        pltpu.VMEM((2 * COMBOS, (SEG // 4 + 1) * SUB, lanes), f32),
        pltpu.VMEM((rows, 3 * lanes), bf16),
        pltpu.VMEM((rows, features), f32),
        pltpu.VMEM((rank, rows), bf16),
        pltpu.VMEM((rank, rows), f32),
        pltpu.VMEM(terms, f32),
        pltpu.VMEM(terms, f32),
        pltpu.VMEM(terms[1:], f32),
        pltpu.VMEM((rank, width), f32),
        pltpu.VMEM(terms, f32),
        pltpu.VMEM((cols // tile, rows, tile), bf16),
        pltpu.VMEM((cols // tile, rows, tile), bf16),
        dma((2,)), dma((3,)), dma((3,)), dma((2, chunks)), dma((2, chunks)),
        dma((3, subs)), dma((3, subs)),
        dma((count,)), dma((count,)), dma((count,)), dma((count,)),
        dma, dma, dma((cols // tile,)), dma((cols // tile,)),
    ]
    mixed, grad_tokens, sums = pl.pallas_call(
        functools.partial(block_kernel, chunks, rows),
        out_shape=(
            jax.ShapeDtypeStruct((rows, channels), bf16),
            jax.ShapeDtypeStruct((rows, cols), bf16),
            jax.ShapeDtypeStruct(terms, f32),
        ),
        in_specs=[vmem] * 3 + [pl.BlockSpec(memory_space=pl.ANY)] * 2 + [vmem] * 3,
        out_specs=(vmem,) * 3,
        scratch_shapes=scratch,
        compiler_params=pltpu.CompilerParams(
            vmem_limit_bytes=58 << 20, collective_id=3, has_side_effects=True
        ),
        cost_estimate=pl.CostEstimate(
            flops=8 * rows * 3 * channels * features, bytes_accessed=20 << 20, transcendentals=0
        ),
    )(weight.transpose(1, 0, 2), adapter_a.T, adapter_b.transpose(1, 0, 2), tokens, cotangent, short, long, skip)
    sum_a = sums[:, :, :width].transpose(1, 0, 2).reshape(rank, features)
    sum_b = sums[:, :, width:].reshape(chunks, rank, 3, lanes).transpose(1, 2, 0, 3)
    return mixed, grad_tokens, sum_a, sum_b.reshape(rank, 3 * channels)


def body(tokens, weight, adapter_a, adapter_b, short_filter, long_filter, skip_gain, cotangent):
    rows, features = tokens.shape
    share = weight.shape[0]
    channels = weight.shape[2]
    rank = adapter_a.shape[1]
    count = lax.axis_size("ctx")
    fits = (
        count == 8
        and lax.axis_size("groups") == 2
        and rows == SUB * (SEG - 4)
        and long_filter.shape[0] == 4 * PHASE_TAPS
        and short_filter.shape[0] <= BLOCK
        and channels == count * CHUNK_LANES
        and share == 2 * QUARTERS * PIECE
        and features == share * count
    )
    if not fits:
        return general_body(
            tokens, weight, adapter_a, adapter_b, short_filter, long_filter, skip_gain, cotangent
        )
    mixed, grad_tokens, sum_a, sum_b = block(
        weight, adapter_a, adapter_b, tokens, cotangent,
        short_filter.reshape(-1, channels), long_filter, skip_gain.reshape(1, channels), count,
    )
    factor = adapter_scale / math.sqrt(rows * count)
    return (mixed, grad_tokens, sum_a.T * factor, (sum_b * factor).reshape(rank, 3, channels))


def solution(mesh):
    return jax.shard_map(
        body,
        mesh=mesh,
        in_specs=(
            P(("groups", "ctx"), None),
            P("ctx", None, "tp"),
            P(),
            P(None, None, "tp"),
            P(None, None, "tp"),
            P(None, "tp"),
            P("tp"),
            P(("groups", "ctx"), "tp"),
        ),
        out_specs=(
            P(("groups", "ctx"), "tp"),
            P(("groups", "ctx"), "tp"),
            P("groups", None),
            P("groups", None, "tp"),
        ),
        check_vma=False,
    )
```

```python
import functools
import math

import jax
import jax.numpy as jnp
from jax import lax
from jax.experimental import pallas as pl
from jax.experimental.pallas import tpu as pltpu
from jax.sharding import PartitionSpec as P

adapter_scale = 0.03125
LANES = 128
SUB = 8
BLOCK = 16
CHUNK = 32


def shifted(value, axis, steps):
    count = lax.axis_size(axis)
    initial, last = (max(0, -steps), min(count, count - steps))
    return lax.ppermute(value, axis, [(source, source + steps) for source in range(initial, last)])


def tiles(ref, first, count):
    start = first * SUB
    if not isinstance(start, int):
        start = pl.multiple_of(start, SUB)
    return ref[pl.ds(start, count * SUB), :].reshape(count, SUB, LANES)


def put(ref, first, value):
    count = value.shape[0]
    ref[pl.ds(pl.multiple_of(first * SUB, SUB), count * SUB), :] = value.reshape(count * SUB, LANES)


def rounded(value):
    return value.astype(jnp.bfloat16).astype(jnp.float32)


def mixer_kernel(
    rows, halo, packed_ref, cot_ref, short_ref, long_ref, skip_ref, mixed_ref, grad_ref,
    p0, p1, p2, cot, query, keyed, valued, gated, gradf,
):
    channels = SUB * LANES
    short_taps = short_ref.shape[0] // 3
    long_taps = long_ref.shape[0]
    spread = (p0, p1, p2)
    front = halo - long_taps

    @pl.loop(0, (rows + 2 * halo) // BLOCK)
    def _(i):
        at = pl.multiple_of(i * BLOCK, BLOCK)
        for g in range(3):
            for s in range(SUB):
                piece = packed_ref[pl.ds(at, BLOCK), pl.ds(g * channels + s * LANES, LANES)]
                spread[g][pl.ds(at * SUB + s, BLOCK, stride=SUB), :] = piece.astype(jnp.float32)

    @pl.loop(0, (rows + halo) // BLOCK)
    def _(i):
        at = pl.multiple_of(i * BLOCK, BLOCK)
        for s in range(SUB):
            piece = cot_ref[pl.ds(at, BLOCK), pl.ds(s * LANES, LANES)]
            cot[pl.ds(at * SUB + s, BLOCK, stride=SUB), :] = piece.astype(jnp.float32)

    def short(ref, g, first, sign):
        total = None
        for j in range(short_taps):
            term = short_ref[j * 3 + g][None] * tiles(ref, first + sign * j, SUB)
            total = term if total is None else total + term
        return total

    @pl.loop(0, (rows + BLOCK + long_taps) // SUB)
    def _(i):
        at = i * SUB
        key = short(p1, 1, at + front, -1)
        val = short(p2, 2, at + front, -1)
        put(keyed, at, key)
        put(valued, at, val)
        put(gated, at, rounded(key * val))

    @pl.loop(0, (rows + halo) // SUB)
    def _(i):
        at = i * SUB
        que = short(p0, 0, at + halo, -1)
        put(query, at, que)
        put(gradf, at, rounded(que * tiles(cot, at, SUB)))

    zero = tuple(jnp.zeros((SUB, LANES), jnp.float32) for _ in range(BLOCK))

    def long_sum(ref, base, sign):
        def chunk(c, acc):
            acc = list(acc)
            tap0 = c * CHUNK
            origin = base + sign * tap0
            low = origin - (CHUNK - 1) if sign < 0 else origin
            seen = {}

            def at(k):
                if k not in seen:
                    seen[k] = ref[pl.ds(pl.multiple_of((low + k) * SUB, SUB), SUB), :]
                return seen[k]

            for j in range(CHUNK):
                tap = long_ref[tap0 + j]
                for i in range(BLOCK):
                    k = i + (CHUNK - 1) - j if sign < 0 else i + j
                    acc[i] = acc[i] + tap * at(k)
            return tuple(acc)

        return lax.fori_loop(0, long_taps // CHUNK, chunk, zero)

    @pl.loop(0, (rows + BLOCK) // BLOCK)
    def _(b):
        at = b * BLOCK
        skip = skip_ref[...]
        ahead = jnp.stack(long_sum(gated, at + long_taps, -1))
        filtered = ahead + skip[None] * tiles(gated, at + long_taps, BLOCK)
        back = jnp.stack(long_sum(gradf, at, 1))
        grad_gated = back + skip[None] * tiles(gradf, at, BLOCK)
        put(p0, at, rounded(tiles(cot, at, BLOCK) * filtered))
        put(p1, at, rounded(grad_gated * tiles(valued, at + long_taps, BLOCK)))
        put(p2, at, rounded(grad_gated * tiles(keyed, at + long_taps, BLOCK)))
        put(gated, at, tiles(query, at, BLOCK) * filtered)

    results = (query, keyed, valued)

    @pl.loop(0, rows // SUB)
    def _(i):
        at = i * SUB
        for g in range(3):
            put(results[g], at, short(spread[g], g, at, 1))

    @pl.loop(0, rows // BLOCK)
    def _(i):
        at = pl.multiple_of(i * BLOCK, BLOCK)
        for s in range(SUB):
            pick = pl.ds(at * SUB + s, BLOCK, stride=SUB)
            mixed_ref[pl.ds(at, BLOCK), pl.ds(s * LANES, LANES)] = gated[pick, :].astype(jnp.bfloat16)
            for g in range(3):
                grad_ref[pl.ds(at, BLOCK), pl.ds(g * channels + s * LANES, LANES)] = results[g][
                    pick, :
                ].astype(jnp.bfloat16)


def mixer(packed, cot, short_filter, long_filter, skip_gain, rows, halo):
    channels = long_filter.shape[1]
    long_taps = long_filter.shape[0]
    full = (rows + 2 * halo) * SUB
    side = (rows + halo) * SUB
    scratch = [pltpu.VMEM((full, LANES), jnp.float32)] * 3 + [
        pltpu.VMEM((side, LANES), jnp.float32)
    ] * 6
    return pl.pallas_call(
        functools.partial(mixer_kernel, rows, halo),
        out_shape=(
            jax.ShapeDtypeStruct((rows, channels), jnp.bfloat16),
            jax.ShapeDtypeStruct((rows, 3 * channels), jnp.bfloat16),
        ),
        in_specs=[pl.BlockSpec(memory_space=pltpu.VMEM)] * 5,
        out_specs=(pl.BlockSpec(memory_space=pltpu.VMEM),) * 2,
        scratch_shapes=scratch,
        compiler_params=pltpu.CompilerParams(vmem_limit_bytes=52 << 20),
        cost_estimate=pl.CostEstimate(
            flops=4 * rows * channels * (long_taps + 42), bytes_accessed=12 << 20, transcendentals=0
        ),
    )(
        packed,
        cot,
        short_filter.reshape(-1, SUB, LANES),
        long_filter.reshape(long_taps, SUB, LANES),
        skip_gain.reshape(SUB, LANES),
    )


def finish_kernel(
    count, grad_ref, whole_ref, terms_ref, tokens_ref, sums_ref,
    held, total, mate, summed, ready, landed,
    send_one, recv_one, send_two, recv_two, send_tp, recv_tp, send_tok, recv_tok,
):
    me = lax.axis_index("ctx")
    mine = lax.axis_index("tp")
    other = 1 - mine
    width = mate.shape[1]
    cols = tokens_ref.shape[1]
    tile = ready.shape[2]
    steps = cols // tile

    barrier = pltpu.get_barrier_semaphore()
    for d in range(1, count):
        pl.semaphore_signal(
            barrier, inc=1, device_id={"ctx": lax.rem(me + d, count)}, device_id_type=pl.DeviceIdType.MESH
        )
    pl.semaphore_signal(barrier, inc=1, device_id={"tp": other}, device_id_type=pl.DeviceIdType.MESH)
    pl.semaphore_wait(barrier, count)

    first = []
    for d in range(1, count):
        peer = lax.rem(me + d, count)
        first.append(
            pltpu.make_async_remote_copy(
                src_ref=terms_ref.at[peer],
                dst_ref=held.at[d],
                send_sem=send_one.at[d],
                recv_sem=recv_one.at[d],
                device_id={"ctx": peer},
                device_id_type=pl.DeviceIdType.MESH,
            )
        )
        first[-1].start()

    def product(half, t):
        at = pl.multiple_of(half * cols + t * tile, tile)
        return lax.dot_general(
            grad_ref[...],
            whole_ref[pl.ds(at, tile), :],
            (((1,), (1,)), ((), ())),
            preferred_element_type=jnp.float32,
        )

    def token_copy(t):
        return pltpu.make_async_remote_copy(
            src_ref=ready.at[t],
            dst_ref=landed.at[t],
            send_sem=send_tok.at[t],
            recv_sem=recv_tok.at[t],
            device_id={"tp": other},
            device_id_type=pl.DeviceIdType.MESH,
        )

    @pl.loop(0, steps)
    def _(t):
        ready[t] = product(other, t).astype(jnp.bfloat16)
        token_copy(t).start()

    own = terms_ref[me]
    for d in range(1, count):
        first[d - 1].wait()
        own = own + held[d]
    total[...] = own
    tp_copy = pltpu.make_async_remote_copy(
        src_ref=total.at[:, pl.ds(0, width)],
        dst_ref=mate,
        send_sem=send_tp,
        recv_sem=recv_tp,
        device_id={"tp": other},
        device_id_type=pl.DeviceIdType.MESH,
    )
    tp_copy.start()

    def own_tile(t):
        value = product(mine, t)
        token_copy(t).wait()
        at = pl.multiple_of(t * tile, tile)
        tokens_ref[:, pl.ds(at, tile)] = (value + landed[t].astype(jnp.float32)).astype(jnp.bfloat16)

    pl.loop(0, steps // 4)(own_tile)
    tp_copy.wait()
    total[:, pl.ds(0, width)] = total[:, pl.ds(0, width)] + mate[...]
    summed[me] = total[...]
    second = []
    for d in range(1, count):
        second.append(
            pltpu.make_async_remote_copy(
                src_ref=total,
                dst_ref=summed.at[me],
                send_sem=send_two.at[d],
                recv_sem=recv_two.at[d],
                device_id={"ctx": lax.rem(me + d, count)},
                device_id_type=pl.DeviceIdType.MESH,
            )
        )
        second[-1].start()
    pl.loop(steps // 4, steps)(own_tile)
    for copy in second:
        copy.wait()
    sums_ref[...] = summed[...]


def finish(grad_packed, whole, part_a, part_b, count):
    rank, features = part_a.shape
    rows, wide = grad_packed.shape
    width, rest = features // count, wide // count
    cols = features // 2
    tile = 256
    terms = jnp.concatenate(
        [part_a.reshape(rank, count, width), part_b.reshape(rank, count, rest)], axis=2
    ).transpose(1, 0, 2)
    vmem = pl.BlockSpec(memory_space=pltpu.VMEM)
    grad_tokens, sums = pl.pallas_call(
        functools.partial(finish_kernel, count),
        out_shape=(
            jax.ShapeDtypeStruct((rows, cols), jnp.bfloat16),
            jax.ShapeDtypeStruct(terms.shape, jnp.float32),
        ),
        in_specs=[vmem] * 3,
        out_specs=(vmem, vmem),
        scratch_shapes=[
            pltpu.VMEM(terms.shape, jnp.float32),
            pltpu.VMEM((rank, width + rest), jnp.float32),
            pltpu.VMEM((rank, width), jnp.float32),
            pltpu.VMEM(terms.shape, jnp.float32),
            pltpu.VMEM((cols // tile, rows, tile), jnp.bfloat16),
            pltpu.VMEM((cols // tile, rows, tile), jnp.bfloat16),
            pltpu.SemaphoreType.DMA((count,)),
            pltpu.SemaphoreType.DMA((count,)),
            pltpu.SemaphoreType.DMA((count,)),
            pltpu.SemaphoreType.DMA((count,)),
            pltpu.SemaphoreType.DMA,
            pltpu.SemaphoreType.DMA,
            pltpu.SemaphoreType.DMA((cols // tile,)),
            pltpu.SemaphoreType.DMA((cols // tile,)),
        ],
        compiler_params=pltpu.CompilerParams(
            vmem_limit_bytes=48 << 20, collective_id=1, has_side_effects=True
        ),
        cost_estimate=pl.CostEstimate(
            flops=2 * rows * wide * features, bytes_accessed=20 << 20, transcendentals=0
        ),
    )(grad_packed, whole, terms)
    flat = sums.transpose(1, 0, 2)
    return (
        grad_tokens,
        flat[:, :, :width].reshape(rank, features),
        flat[:, :, width:].reshape(rank, wide),
    )


MESH = pl.DeviceIdType.MESH
PIECES = 4


def gather_kernel(
    outer, shard_ref, out_ref, z_send, z_recv, y_send, y_recv, x_send, x_recv, local_sem
):
    me = lax.axis_index("ctx")
    x = lax.axis_index("groups")
    z, y = me // 2, lax.rem(me, 2)
    rows = shard_ref.shape[0]
    piece = rows // PIECES
    half = piece // 2
    last = outer - 2
    steps = outer - 1

    def ctx_of(line, pair):
        return {"ctx": line * 2 + pair}

    def span(line, pair, start, size):
        return pl.ds(pl.multiple_of((line * 2 + pair) * rows + start, half), size)

    def part(p, side):
        return p * piece + side * half

    def copy(src, dst, send, recv, device):
        return pltpu.make_async_remote_copy(
            src_ref=src, dst_ref=dst, send_sem=send, recv_sem=recv, device_id=device, device_id_type=MESH
        )

    def z_range(k, p):
        return (part(p, x), half) if k == last else (p * piece, piece)

    def z_out(way, k, p):
        step = 1 - 2 * way
        start, size = z_range(k, p)
        place = span(z - step * k, y, start, size)
        src = out_ref.at[place] if k else shard_ref.at[pl.ds(pl.multiple_of(start, half), size)]
        return copy(
            src, out_ref.at[place], z_send.at[way, k, p], z_recv.at[way, k, p], ctx_of(z + step, y)
        )

    def z_in(way, k, p):
        step = 1 - 2 * way
        start, size = z_range(k, p)
        place = out_ref.at[span(z - step * (k + 1), y, start, size)]
        return copy(place, place, z_send.at[way, k, p], z_recv.at[way, k, p], ctx_of(z - step, y))

    def sends(way, k):
        return (z < steps) & (z >= k) if way == 0 else (z > 0) & (z + k <= steps)

    def receives(way, k):
        return z > k if way == 0 else z + k < steps

    def line_of(i):
        if i == 0:
            return z
        way, k = (i - 1) // steps, (i - 1) % steps
        return z - (1 - 2 * way) * (k + 1)

    def item(way, k):
        return 1 + way * steps + k

    def y_out(i, p):
        start = part(p, x)
        place = span(line_of(i), y, start, half)
        src = out_ref.at[place] if i else shard_ref.at[pl.ds(pl.multiple_of(start, half), half)]
        return copy(src, out_ref.at[place], y_send.at[i, p], y_recv.at[i, p], ctx_of(z, 1 - y))

    def y_in(i, p):
        place = out_ref.at[span(line_of(i), 1 - y, part(p, x), half)]
        return copy(place, place, y_send.at[i, p], y_recv.at[i, p], ctx_of(z, 1 - y))

    def x_copy(i, p, side):
        if i > 2 * steps:
            line, pair = line_of(item(i - 2 * steps - 1, last)), y
        else:
            line, pair = line_of(i), 1 - y
        place = out_ref.at[span(line, pair, part(p, side), half)]
        return copy(place, place, x_send.at[i, p], x_recv.at[i, p], {"groups": 1 - x})

    def extra(way):
        return 2 * steps + 1 + way

    barrier = pltpu.get_barrier_semaphore()
    pl.semaphore_signal(barrier, inc=1, device_id=ctx_of(z, 1 - y), device_id_type=MESH)
    pl.semaphore_signal(barrier, inc=1, device_id={"groups": 1 - x}, device_id_type=MESH)
    for step in (1, outer - 1):
        pl.semaphore_signal(
            barrier, inc=1, device_id=ctx_of(lax.rem(z + step, outer), y), device_id_type=MESH
        )
    pl.semaphore_wait(barrier, 4)

    @pl.loop(0, PIECES)
    def _(p):
        for way in range(2):
            @pl.when(sends(way, 0))
            def _():
                z_out(way, 0, p).start()
        y_out(0, p).start()

    own = pltpu.make_async_copy(
        shard_ref, out_ref.at[pl.ds(pl.multiple_of(me * rows, rows), rows)], local_sem
    )
    own.start()

    def pass_on(k, p):
        for way in range(2):
            @pl.when(receives(way, k))
            def _():
                i = item(way, k)
                y_in(i, p).wait_recv()
                x_copy(i, p, x).start()

    for k in range(steps):
        @pl.loop(0, PIECES)
        def _(p):
            for way in range(2):
                @pl.when(receives(way, k))
                def _():
                    z_in(way, k, p).wait_recv()
                    if k < last:
                        @pl.when(sends(way, k + 1))
                        def _():
                            z_out(way, k + 1, p).start()
                    y_out(item(way, k), p).start()
                    if k == last:
                        x_copy(extra(way), p, x).start()
            if k == 0:
                y_in(0, p).wait_recv()
                x_copy(0, p, x).start()

            @pl.when(p > 0)
            def _():
                pass_on(k, p - 1)

            if k > 0:
                @pl.when(p == 0)
                def _():
                    pass_on(k - 1, PIECES - 1)

    pass_on(last, PIECES - 1)
    own.wait()

    @pl.loop(0, PIECES)
    def _(p):
        x_copy(0, p, 1 - x).wait_recv()
        x_copy(0, p, x).wait_send()
        y_out(0, p).wait_send()
        for way in range(2):
            for k in range(steps):
                @pl.when(sends(way, k))
                def _():
                    z_out(way, k, p).wait_send()

                @pl.when(receives(way, k))
                def _():
                    i = item(way, k)
                    x_copy(i, p, 1 - x).wait_recv()
                    x_copy(i, p, x).wait_send()
                    y_out(i, p).wait_send()
                    if k == last:
                        x_copy(extra(way), p, 1 - x).wait_recv()
                        x_copy(extra(way), p, x).wait_send()


def gather(merged, count):
    rows, wide = merged.shape
    outer = count // 2
    items = 2 * (outer - 1) + 1
    dma = pltpu.SemaphoreType.DMA
    hbm = pl.BlockSpec(memory_space=pl.ANY)
    return pl.pallas_call(
        functools.partial(gather_kernel, outer),
        out_shape=jax.ShapeDtypeStruct((rows * count, wide), merged.dtype),
        in_specs=[hbm],
        out_specs=hbm,
        scratch_shapes=[
            dma((2, outer - 1, PIECES)),
            dma((2, outer - 1, PIECES)),
            dma((items, PIECES)),
            dma((items, PIECES)),
            dma((items + 2, PIECES)),
            dma((items + 2, PIECES)),
            dma,
        ],
        compiler_params=pltpu.CompilerParams(collective_id=2, has_side_effects=True),
        cost_estimate=pl.CostEstimate(flops=0, bytes_accessed=300 << 20, transcendentals=0),
    )(merged)


def general_body(tokens, weight, adapter_a, adapter_b, short_filter, long_filter, skip_gain, cotangent):
    row_count = tokens.shape[0]
    share_rows = weight.shape[0]
    channels = weight.shape[2]
    features = tokens.shape[1]
    adapter_rank = adapter_a.shape[1]
    halo = long_filter.shape[0] + BLOCK
    count = lax.axis_size("ctx")
    seq_total = row_count * count
    first_row = lax.axis_index("ctx") * share_rows
    before = shifted(tokens[row_count - halo :], "ctx", 1)
    after = shifted(tokens[:halo], "ctx", -1)
    cot_after = shifted(cotangent[:halo], "ctx", -1)
    tokens_ext = jnp.concatenate([before, tokens, after], axis=0)
    cot_ext = jnp.concatenate([cotangent, cot_after], axis=0)
    own_rows = lax.dynamic_slice_in_dim(adapter_a, first_row, share_rows, 0)
    flat_b = adapter_b.reshape(adapter_rank, 3 * channels)
    delta_w = jnp.dot(own_rows, flat_b, preferred_element_type=jnp.float32)
    merged = (
        weight.reshape(share_rows, 3 * channels).astype(jnp.float32) + adapter_scale * delta_w
    ).astype(jnp.bfloat16)
    if count == 8 and lax.axis_size("groups") == 2:
        whole = gather(merged, count)
    else:
        whole = lax.all_gather(merged, "ctx", axis=0, tiled=True)
    packed = jnp.dot(tokens_ext, whole, preferred_element_type=jnp.float32).astype(jnp.bfloat16)
    mixed, grad_packed = mixer(
        packed, cot_ext, short_filter, long_filter, skip_gain, row_count, halo
    )
    projected = jnp.dot(tokens, adapter_a, preferred_element_type=jnp.float32).astype(jnp.bfloat16)
    part_b = lax.dot_general(
        projected, grad_packed, (((0,), (0,)), ((), ())), preferred_element_type=jnp.float32
    )
    through = lax.dot_general(
        flat_b, grad_packed, (((1,), (1,)), ((), ())), preferred_element_type=jnp.float32
    ).astype(jnp.bfloat16)
    part_a = jnp.dot(through, tokens, preferred_element_type=jnp.float32)
    if features % (LANES * count) == 0 and (3 * channels) % (LANES * count) == 0:
        grad_tokens, sum_a, sum_b = finish(grad_packed, whole, part_a, part_b, count)
    else:
        sum_a = lax.psum(part_a, ("ctx", "tp"))
        sum_b = lax.psum(part_b, "ctx")
        partial_grad = lax.dot_general(
            grad_packed, whole, (((1,), (1,)), ((), ())), preferred_element_type=jnp.float32
        )
        grad_tokens = lax.psum_scatter(
            partial_grad.astype(jnp.bfloat16), "tp", scatter_dimension=1, tiled=True
        )
    sum_a = sum_a.T
    factor = adapter_scale / math.sqrt(seq_total)
    return (mixed, grad_tokens, sum_a * factor, (sum_b * factor).reshape(adapter_rank, 3, channels))


CHUNK_LANES = 128
QUARTERS = 4
LAGS = (2, 4, 6, 8)
WHOLE_Z = (1, 3)
HALF_Y = (2,)
PIECE = 32
SEG = 68
COMBOS = 9
PHASE_TAPS = 32
OUT_SEG = 66
OUT_STEP = 11
EDGE = 16


def combine(p):
    p02, p13, p01, p23 = p[0] + p[2], p[1] + p[3], p[0] + p[1], p[2] + p[3]
    return (p[0], p[2], p02, p[1], p[3], p13, p01, p23, p01 + p23)


def block_kernel(
    chunks, rows,
    weight_ref, down_ref, wide_ref, tokens_hbm, cot_hbm, short_ref, long_ref, skip_ref,
    mixed_ref, tokgrad_ref, grad_a_ref, grad_b_ref,
    up_ref, tokens_ref, cot_ref, hold_g, hold_f, edge_g, edge_f,
    whole, pk0, pk1, pk2, cot, keyed, valued, gated, query, gradf, gs0, gs1, gs2, mix,
    comb, taps, sub, gp, acc, proj, through, terms_b, held_b, sum_b, terms_a, held_a, sum_a, ready, landed,
    load_sem, near_send, near_recv, edge_send, edge_recv,
    sent, came, send_b, recv_b, back_b, done_b, send_a, recv_a, back_a, done_a, send_tok, recv_tok,
):
    me = lax.axis_index("ctx")
    x = lax.axis_index("groups")
    mine = lax.axis_index("tp")
    other = 1 - mine
    z, y = me // 2, lax.rem(me, 2)
    count = chunks
    lines = count // 2
    subs = chunks * QUARTERS
    lanes = CHUNK_LANES
    f32, bf16 = jnp.float32, jnp.bfloat16
    pk = (pk0, pk1, pk2)
    long_taps = long_ref.shape[0]
    short_taps = short_ref.shape[0] // 3
    channels = chunks * lanes
    halo = EDGE
    has_next, has_last = me < count - 1, me > 0
    to_next = {"ctx": lax.rem(me + 1, count)}
    to_last = {"ctx": lax.rem(me + count - 1, count)}

    loads = (
        pltpu.make_async_copy(tokens_hbm, tokens_ref.at[pl.ds(halo, rows)], load_sem.at[0]),
        pltpu.make_async_copy(cot_hbm, cot_ref.at[pl.ds(0, rows)], load_sem.at[1]),
    )
    for copy in loads:
        copy.start()

    barrier = pltpu.get_barrier_semaphore()
    for d in range(1, count):
        pl.semaphore_signal(
            barrier, inc=1, device_id={"ctx": lax.rem(me + d, count)}, device_id_type=MESH
        )
    pl.semaphore_signal(barrier, inc=1, device_id={"tp": other}, device_id_type=MESH)
    for d in range(1, count):
        pl.semaphore_signal(
            barrier, inc=1, device_id={"ctx": lax.rem(me + d, count), "tp": other}, device_id_type=MESH
        )
    pl.semaphore_signal(barrier, inc=1, device_id={"groups": 1 - x}, device_id_type=MESH)

    def merge(c):
        own = pl.ds(pl.multiple_of(me * weight_ref.shape[1], weight_ref.shape[1]), weight_ref.shape[1])
        delta = lax.dot_general(
            down_ref[:, own], up_ref[c], (((0,), (0,)), ((), ())), preferred_element_type=f32
        )
        for g in range(3):
            value = weight_ref[g, :, c * lanes : (c + 1) * lanes].astype(f32) + adapter_scale * delta[:, g * lanes : (g + 1) * lanes]
            whole[c, z, y, :, :, :, pl.ds(g * lanes, lanes)] = value.astype(bf16).reshape(
                QUARTERS, 2, PIECE, lanes
            )

    def send(ref, sub_at, stage, device):
        pltpu.make_async_remote_copy(
            src_ref=ref, dst_ref=ref, send_sem=sent.at[stage, sub_at], recv_sem=came.at[stage, sub_at],
            device_id=device, device_id_type=MESH,
        ).start()

    def whole_wait(ref, sub_at, stage):
        return pltpu.make_async_remote_copy(
            src_ref=ref, dst_ref=ref, send_sem=sent.at[stage, sub_at], recv_sem=came.at[stage, sub_at],
            device_id={"tp": other}, device_id_type=MESH,
        )

    def arrived(ref, sub_at, stage):
        whole_wait(ref, sub_at, stage).wait_recv()

    def line(d):
        return lax.rem(z + d, lines)

    side = z // 2
    inner = lax.rem(z + side, 2) == 1
    outer = jnp.logical_not(inner)
    beside = z + 1 - 2 * lax.rem(z, 2)
    across = 2 - side
    to_x = {"groups": 1 - x}
    to_y = {"ctx": z * 2 + 1 - y}
    to_beside = {"ctx": beside * 2 + y}

    def z_blocks(q, many):
        if q in WHOLE_Z:
            return whole.at[0, 0, 0, pl.ds(0, many)]
        return whole.at[pl.ds(0, many), 0, 0, 0, 0]

    def stage0(c, q):
        n = c * QUARTERS + q
        ref = whole.at[c, z, y, q] if q in WHOLE_Z else whole.at[c, z, y, q, x]
        send(ref, n, 0, {"ctx": across * 2 + y})
        send(ref, n, 0, to_beside)

    def stage0b(c, q):
        n = c * QUARTERS + q

        @pl.when(inner)
        def _():
            arrived(z_blocks(q, 3), n, 0)
            far = pl.ds(2 - 2 * side, 2)
            send(whole.at[c, far, y, q] if q in WHOLE_Z else whole.at[c, far, y, q, x], n, 0, to_beside)

    def stage1(c, q):
        n = c * QUARTERS + q
        pl.when(outer)(lambda: arrived(z_blocks(q, 3), n, 0))
        if q not in WHOLE_Z:
            for d in range(1, lines):
                send(whole.at[c, line(d), y, q, x], n, 1, to_x)
        send(whole.at[c, :, y, q, x], n, 1, to_y)

    def stage2(c, q):
        n = c * QUARTERS + q
        arrived(whole.at[pl.ds(0, stage1_blocks(q)), 0, 0, 0, 0], n, 1)
        if q not in HALF_Y:
            send(whole.at[c, :, 1 - y, q, x], n, 2, to_x)
        else:
            half = PIECE // 2
            send(whole.at[c, :, 1 - y, q, x, pl.ds(0, half)], n, 2, to_x)
            send(whole.at[c, :, y, q, 1 - x, pl.ds(half, half)], n, 2, to_y)

    def stage1_blocks(q):
        return lines if q in WHOLE_Z else 2 * lines - 1

    def slot(base, off):
        for stage, back in zip((stage0, stage2, stage1, stage0b), (0, LAGS[2], LAGS[1], LAGS[0])):
            at = off - back
            if at < 0:
                continue
            c, q = base + at // QUARTERS, at % QUARTERS
            if isinstance(base, int):
                stage(c, q)
            else:
                pl.when(c < chunks)(functools.partial(stage, c, q))

    def near(k):
        src, dst, device = (
            (tokens_hbm.at[pl.ds(rows - halo, halo)], tokens_ref.at[pl.ds(0, halo)], to_next),
            (tokens_hbm.at[pl.ds(0, halo)], tokens_ref.at[pl.ds(rows + halo, halo)], to_last),
            (cot_hbm.at[pl.ds(0, halo)], cot_ref.at[pl.ds(rows, halo)], to_last),
        )[k]
        return pltpu.make_async_remote_copy(
            src_ref=src, dst_ref=dst, send_sem=near_send.at[k], recv_sem=near_recv.at[k],
            device_id=device, device_id_type=MESH,
        )

    def edge(k, c):
        src, dst, device = ((hold_g, edge_g, to_next), (hold_f, edge_f, to_last))[k]
        return pltpu.make_async_remote_copy(
            src_ref=src.at[c], dst_ref=dst.at[c], send_sem=edge_send.at[k, c],
            recv_sem=edge_recv.at[k, c], device_id=device, device_id_type=MESH,
        )

    for c in range(chunks):
        for g in range(3):
            up_ref[c, :, g * lanes : (g + 1) * lanes] = wide_ref[g, :, c * lanes : (c + 1) * lanes]
    merge(0)
    pl.semaphore_wait(barrier, 2 * count)

    first_slots = LAGS[3] + QUARTERS - 1
    body_rows = pl.ds(halo, rows)
    for n in range(first_slots):
        slot(0, n)
        if n + 1 < chunks:
            merge(n + 1)
        if n == 0:
            pl.when(has_next)(lambda: near(0).start())

            @pl.when(has_last)
            def _():
                near(1).start()
                near(2).start()

            @pl.when(jnp.logical_not(has_last))
            def _():
                tokens_ref[pl.ds(0, halo), :] = jnp.zeros((halo, tokens_ref.shape[1]), bf16)
                edge_g[...] = jnp.zeros_like(edge_g)

            @pl.when(jnp.logical_not(has_next))
            def _():
                tokens_ref[pl.ds(rows + halo, halo), :] = jnp.zeros((halo, tokens_ref.shape[1]), bf16)
                cot_ref[pl.ds(rows, halo), :] = jnp.zeros((halo, channels), bf16)
                edge_f[...] = jnp.zeros_like(edge_f)

            tail = cot_ref.shape[0] - rows - halo
            cot_ref[pl.ds(rows + halo, tail), :] = jnp.zeros((tail, channels), bf16)
            known = rows + halo
            for ref in (query, keyed, valued):
                ref[pl.ds(known, ref.shape[0] - known), :] = jnp.zeros((ref.shape[0] - known, lanes), f32)
            after = gated.shape[0] - known - long_taps
            gated[pl.ds(known + long_taps, after), :] = jnp.zeros((after, lanes), f32)
            after = gradf.shape[0] - rows - edge_f.shape[1]
            gradf[pl.ds(rows + edge_f.shape[1], after), :] = jnp.zeros((after, lanes), f32)
        if n == first_slots - 2:
            for copy in loads:
                copy.wait()
            proj[...] = lax.dot_general(
                down_ref[...], tokens_ref[body_rows, :], (((1,), (1,)), ((), ())),
                preferred_element_type=f32,
            ).astype(bf16)
            through[...] = jnp.zeros_like(through)
        if n == first_slots - 1:
            acc[...] = jnp.zeros_like(acc)

            @pl.when(has_last)
            def _():
                near(0).wait_recv()
                near(1).wait_send()
                near(2).wait_send()

            @pl.when(has_next)
            def _():
                near(0).wait_send()
                near(1).wait_recv()
                near(2).wait_recv()

    def spread(row, count_rows):
        return jnp.broadcast_to(row, (count_rows, lanes))

    def short(ref, g, cols, first, sign, size, stride):
        seen = {}

        def at(k):
            if k not in seen:
                seen[k] = ref[pl.ds(first + k, SUB, stride=stride), :]
            return seen[k]

        result = [None] * size
        for j in range(short_taps):
            tap = spread(short_ref[j * 3 + g : j * 3 + g + 1, cols], SUB)
            for i in range(size):
                term = tap * at(i + sign * j)
                result[i] = term if j == 0 else result[i] + term
        return result

    def packed_grad(c):
        cols = pl.ds(c * lanes if isinstance(c, int) else pl.multiple_of(c * lanes, lanes), lanes)

        @pl.loop(0, OUT_SEG // OUT_STEP)
        def _(b):
            for g, ref in enumerate((gs0, gs1, gs2)):
                value = short(ref, g, cols, b * OUT_STEP, 1, OUT_STEP, OUT_SEG)
                for i in range(OUT_STEP):
                    pk[g][pl.ds(b * OUT_STEP + i, SUB, stride=OUT_SEG), :] = value[i]

        @pl.loop(0, rows // BLOCK)
        def _(i):
            here = pl.ds(pl.multiple_of(i * BLOCK, BLOCK), BLOCK)
            mixed_ref[here, cols] = mix[here, :].astype(bf16)
            for g in range(3):
                gp[here, pl.ds(g * lanes, lanes)] = pk[g][here, :].astype(bf16)

    def to_owner(c):
        return pltpu.make_async_remote_copy(
            src_ref=terms_b.at[c], dst_ref=held_b.at[me], send_sem=send_b.at[c], recv_sem=recv_b.at[me],
            device_id={"ctx": c}, device_id_type=MESH,
        )

    def peer_of(d):
        return lax.rem(me + d, count)

    def sum_share():
        value = terms_b[me].astype(f32)
        for d in range(1, count):
            peer = peer_of(d)
            pltpu.make_async_remote_copy(
                src_ref=held_b.at[peer], dst_ref=held_b.at[peer], send_sem=send_b.at[peer],
                recv_sem=recv_b.at[peer], device_id={"ctx": peer}, device_id_type=MESH,
            ).wait_recv()
            value = value + held_b[peer].astype(f32)
        sum_b[me] = value.astype(bf16)
        for d in range(1, count):
            share_back(d).start()

    def share_back(d):
        return pltpu.make_async_remote_copy(
            src_ref=sum_b.at[me], dst_ref=sum_b.at[me], send_sem=back_b.at[d], recv_sem=done_b.at[me],
            device_id={"ctx": peer_of(d)}, device_id_type=MESH,
        )

    def adapter_terms(c):
        terms_b[c] = jnp.dot(proj[...], gp[...], preferred_element_type=f32).astype(bf16)

        @pl.when(me != c)
        def _():
            to_owner(c).start()

        through[...] += lax.dot_general(
            up_ref[c], gp[...], (((1,), (1,)), ((), ())), preferred_element_type=f32
        )

    def token_terms(c, k, pair):
        block = whole[c, k, pair].reshape(-1, 3 * lanes)
        wide = block.shape[0]
        start = (k * 2 + pair) * wide
        at = pl.ds(start if isinstance(start, int) else pl.multiple_of(start, wide), wide)
        value = acc[:, at] + lax.dot_general(
            gp[...], block, (((1,), (1,)), ((), ())), preferred_element_type=f32
        )
        acc[:, at] = value
        return value

    def token_copy(t):
        return pltpu.make_async_remote_copy(
            src_ref=ready.at[t], dst_ref=landed.at[t], send_sem=send_tok.at[t],
            recv_sem=recv_tok.at[t], device_id={"tp": other}, device_id_type=MESH,
        )

    def chunk_step(c):
        cols = pl.ds(pl.multiple_of(c * lanes, lanes), lanes)

        slot(c, first_slots)
        for q in range(QUARTERS):
            arrived(whole.at[pl.ds(0, lines), 0, 0, 0, 0], c * QUARTERS + q, 2)
        ext = tokens_ref.shape[0]
        part = ext // 2

        @pl.loop(0, 2)
        def _(r):
            at = pl.ds(pl.multiple_of(r * part, 16), part)
            value = jnp.dot(
                tokens_ref[at, :], whole[c].reshape(-1, 3 * lanes), preferred_element_type=f32
            )
            for g in range(3):
                pk[g][at, :] = rounded(value[:, g * lanes : (g + 1) * lanes])

        slot(c, first_slots + 1)

        @pl.loop(0, cot.shape[0] // BLOCK)
        def _(i):
            here = pl.ds(pl.multiple_of(i * BLOCK, BLOCK), BLOCK)
            cot[here, :] = cot_ref[here, cols].astype(f32)

        @pl.loop(0, OUT_SEG // OUT_STEP)
        def _(b):
            at = b * OUT_STEP
            key = short(pk1, 1, cols, at + halo, -1, OUT_STEP, OUT_SEG)
            val = short(pk2, 2, cols, at + halo, -1, OUT_STEP, OUT_SEG)
            for i in range(OUT_STEP):
                here = pl.ds(at + i, SUB, stride=OUT_SEG)
                keyed[here, :] = key[i]
                valued[here, :] = val[i]
                gated[pl.ds(at + i + long_taps, SUB, stride=OUT_SEG), :] = rounded(key[i] * val[i])
            que = short(pk0, 0, cols, at + halo, -1, OUT_STEP, OUT_SEG)
            for i in range(OUT_STEP):
                here = pl.ds(at + i, SUB, stride=OUT_SEG)
                query[here, :] = que[i]
                gradf[here, :] = rounded(que[i] * cot[here, :])

        hold_g[c] = gated[pl.ds(rows, long_taps), :].astype(bf16)
        hold_f[c] = gradf[pl.ds(0, edge_f.shape[1]), :].astype(bf16)
        pl.when(has_next)(lambda: edge(0, c).start())
        pl.when(has_last)(lambda: edge(1, c).start())

        @pl.when(c > 0)
        def _():
            packed_grad(c - 1)

        slot(c, first_slots + 2)

        @pl.when(c > 0)
        def _():
            adapter_terms(c - 1)
            pl.when(c - 2 == me)(sum_share)
            for k in range(lines):
                for pair in range(2):
                    token_terms(c - 1, k, pair)

        @pl.loop(0, long_taps // SUB)
        def _(k):
            piece = long_ref[pl.ds(pl.multiple_of(k * SUB, SUB), SUB), cols]
            for h in range(2):
                p = [spread(piece[4 * h + i : 4 * h + i + 1], SUB) for i in range(4)]
                at = pl.ds(pl.multiple_of((2 * k + h) * SUB, SUB), SUB)
                for e, value in enumerate(combine(p)):
                    taps[e, at, :] = value

        pl.when(has_last)(lambda: edge(0, c).wait_recv())
        pl.when(has_next)(lambda: edge(1, c).wait_recv())
        gated[pl.ds(0, long_taps), :] = edge_g[c].astype(f32)
        gradf[pl.ds(rows, edge_f.shape[1]), :] = edge_f[c].astype(f32)

        span = PHASE_TAPS + SEG // 4

        @pl.loop(0, span)
        def _(k):
            at = pl.ds(pl.multiple_of(k * SUB, SUB), SUB)
            ahead = [gated[pl.ds(4 * k + i, SUB, stride=OUT_SEG), :] for i in range(4)]
            last = long_taps + SEG - 1
            back = [gradf[pl.ds(last - 4 * k - i, SUB, stride=OUT_SEG), :] for i in range(4)]
            for e, value in enumerate(combine(ahead) + combine(back)):
                comb[e, at, :] = value

        slot(c, first_slots + 3)

        outs = SEG // 4 + 1

        @pl.loop(0, 2 * COMBOS)
        def _(e):
            te = lax.rem(e, COMBOS)
            sums = [None] * outs
            seen = {}
            for k in range(PHASE_TAPS):
                weight = taps[te, k * SUB : (k + 1) * SUB, :]
                for n in range(outs):
                    at = n + PHASE_TAPS - 1 - k
                    if at not in seen:
                        seen[at] = comb[e, at * SUB : (at + 1) * SUB, :]
                    term = weight * seen[at]
                    sums[n] = term if sums[n] is None else sums[n] + term
            for n in range(outs):
                sub[e, n * SUB : (n + 1) * SUB, :] = sums[n]

        skip = spread(skip_ref[:, cols], SUB)

        def finish_rows(first_n, many):
            jobs = []
            for m in range(many):
                n = first_n + m
                before = pl.ds(n * SUB if isinstance(n, int) else pl.multiple_of(n * SUB, SUB), SUB)
                now = pl.ds((n + 1) * SUB if isinstance(n, int) else pl.multiple_of((n + 1) * SUB, SUB), SUB)
                jobs.append(([sub[e, now, :] for e in range(2 * COMBOS)],
                             {e: sub[e, before, :] for e in (1, 3, 4, 5, 7, 10, 12, 13, 14, 16)}))
            at = lambda ref, start: ref[pl.ds(start, SUB, stride=OUT_SEG), :]
            order = [(4 * (first_n + m) + i) for m in range(many) for i in range(4)]
            ahead = [(at(gated, long_taps + k), at(cot, k), at(query, k)) for k in order]
            back = [
                (at(gradf, SEG - 1 - k), at(valued, SEG - 1 - k), at(keyed, SEG - 1 - k)) for k in order
            ]

            def outputs(now, before, e):
                def pair(p):
                    v0, v1, v2 = now[e + p], now[e + p + 1], now[e + p + 2]
                    return v0 + before[e + p + 1], v2 - v0 - v1

                a_e, a_o = pair(0)
                b_e, b_o = now[e + 3] + before[e + 4], now[e + 5] - now[e + 3] - now[e + 4]
                c_e, c_o = pair(6)
                b_was = before[e + 5] - before[e + 3] - before[e + 4]
                return [a_e + b_was, c_e - a_e - b_e, a_o + b_e, c_o - a_o - b_o]

            forward, backward = [], []
            for now, before in jobs:
                forward += outputs(now, before, 0)
                backward += outputs(now, before, COMBOS)
            stores = []
            for k, value, (gate, ct, que) in zip(order, forward, ahead):
                filtered = value + skip * gate
                stores += [(gs0, k, rounded(ct * filtered)), (mix, k, que * filtered)]
            for k, value, (gf, val, key) in zip(order, backward, back):
                grad_gated = value + skip * gf
                stores += [
                    (gs1, SEG - 1 - k, rounded(grad_gated * val)), (gs2, SEG - 1 - k, rounded(grad_gated * key))
                ]
            for ref, k, value in stores:
                ref[pl.ds(k, SUB, stride=OUT_SEG), :] = value

        pl.loop(0, SEG // 8)(lambda n: finish_rows(2 * n, 2))
        finish_rows(SEG // 4 - 1, 1)

    pl.loop(0, chunks)(chunk_step)

    cols = tokgrad_ref.shape[1]
    tile = ready.shape[2]
    steps = cols // tile
    width = 2 * lanes
    packed_grad(chunks - 1)
    adapter_terms(chunks - 1)
    part_a = jnp.dot(through[...].astype(bf16), tokens_ref[body_rows, :], preferred_element_type=f32)
    for p in range(count):
        for t in range(2):
            at = p * width + t * lanes
            terms_a[p, t] = part_a[:, at : at + lanes].astype(bf16)

    pairs = [(d, h) for h in range(2) for d in range(count) if (d, h) != (0, 0)]

    def a_copy(src, dst, k, d, h, send, recv):
        return pltpu.make_async_remote_copy(
            src_ref=src, dst_ref=dst, send_sem=send.at[k], recv_sem=recv.at[k],
            device_id={"ctx": peer_of(d), "tp": other if h else mine}, device_id_type=MESH,
        )

    first = [
        a_copy(terms_a.at[peer_of(d), other if h else mine], held_a.at[k], k, d, h, send_a, recv_a)
        for k, (d, h) in enumerate(pairs)
    ]
    for copy in first:
        copy.start()
    half_lines = lines // 2
    for t in range(steps):
        value = token_terms(chunks - 1, other * half_lines + t // 2, t % 2)
        ready[t] = value.astype(bf16)
        token_copy(t).start()
    pl.when(me >= chunks - 2)(sum_share)
    own = terms_a[me, mine].astype(f32)
    for k, copy in enumerate(first):
        copy.wait()
        own = own + held_a[k].astype(f32)
    sum_a[me, mine] = own.astype(bf16)
    second = [
        a_copy(sum_a.at[me, mine], sum_a.at[me, mine], k, d, h, back_a, done_a)
        for k, (d, h) in enumerate(pairs)
    ]
    for copy in second:
        copy.start()
    for t in range(steps):
        token_terms(chunks - 1, mine * half_lines + t // 2, t % 2)

    @pl.loop(0, steps)
    def _(t):
        token_copy(t).wait()
        at = pl.multiple_of(t * tile, tile)
        from_at = pl.multiple_of(mine * cols + t * tile, tile)
        tokgrad_ref[:, pl.ds(at, tile)] = (
            acc[:, pl.ds(from_at, tile)] + landed[t].astype(f32)
        ).astype(bf16)

    @pl.loop(0, chunks)
    def _(c):
        for q in range(QUARTERS):
            n = c * QUARTERS + q
            pl.when(inner)(lambda: whole_wait(z_blocks(q, 4), n, 0).wait_send())
            pl.when(outer)(lambda: whole_wait(z_blocks(q, 2), n, 0).wait_send())
            whole_wait(whole.at[pl.ds(0, stage1_blocks(q)), 0, 0, 0, 0], n, 1).wait_send()
            whole_wait(whole.at[pl.ds(0, lines), 0, 0, 0, 0], n, 2).wait_send()

    @pl.when(has_next)
    def _():
        for c in range(chunks):
            edge(0, c).wait_send()

    @pl.when(has_last)
    def _():
        for c in range(chunks):
            edge(1, c).wait_send()

    for c in range(chunks):
        @pl.when(me != c)
        def _():
            to_owner(c).wait_send()
            pltpu.make_async_remote_copy(
                src_ref=sum_b.at[c], dst_ref=sum_b.at[c], send_sem=back_b.at[0], recv_sem=done_b.at[c],
                device_id={"ctx": c}, device_id_type=MESH,
            ).wait_recv()

    for d in range(1, count):
        share_back(d).wait_send()
    for copy in second:
        copy.wait()
    factor = adapter_scale / math.sqrt(rows * count)
    for p in range(count):
        for t in range(2):
            at = p * width + t * lanes
            grad_a_ref[:, at : at + lanes] = sum_a[p, t].astype(f32) * factor
        for g in range(3):
            grad_b_ref[g, :, p * lanes : (p + 1) * lanes] = (
                sum_b[p, :, g * lanes : (g + 1) * lanes].astype(f32) * factor
            )


def block(weight, adapter_a, adapter_b, tokens, cotangent, short, long, skip, count):
    rank = adapter_a.shape[1]
    rows, features = tokens.shape
    channels = long.shape[1]
    chunks = channels // CHUNK_LANES
    lanes = CHUNK_LANES
    cols = features // 2
    tile = 256
    vmem = pl.BlockSpec(memory_space=pltpu.VMEM)
    f32, bf16 = jnp.float32, jnp.bfloat16
    seg_rows = SUB * SEG
    reach = seg_rows + long.shape[0]
    plain = lambda n: pltpu.VMEM((n, lanes), f32)
    dma = pltpu.SemaphoreType.DMA
    subs = chunks * QUARTERS
    share_b, share_a = (count, rank, 3 * lanes), (count, 2, rank, lanes)
    reach_back = long.shape[0] + EDGE
    scratch = [
        pltpu.VMEM((chunks, rank, 3 * lanes), bf16),
        pltpu.VMEM((rows + 2 * EDGE, features), bf16),
        pltpu.VMEM((seg_rows, channels), bf16),
        pltpu.VMEM((chunks, long.shape[0], lanes), bf16),
        pltpu.VMEM((chunks, reach_back, lanes), bf16),
        pltpu.VMEM((chunks, long.shape[0], lanes), bf16),
        pltpu.VMEM((chunks, reach_back, lanes), bf16),
        pltpu.VMEM((chunks, count // 2, 2, QUARTERS, 2, PIECE, 3 * lanes), bf16),
        plain(rows + 2 * EDGE), plain(rows + 2 * EDGE), plain(rows + 2 * EDGE),
        plain(seg_rows), plain(seg_rows), plain(seg_rows), plain(reach), plain(seg_rows), plain(reach),
        plain(seg_rows), plain(seg_rows), plain(seg_rows), plain(seg_rows),
        pltpu.VMEM((2 * COMBOS, (PHASE_TAPS + SEG // 4) * SUB, lanes), f32),
        pltpu.VMEM((COMBOS, PHASE_TAPS * SUB, lanes), f32),
        pltpu.VMEM((2 * COMBOS, (SEG // 4 + 1) * SUB, lanes), f32),
        pltpu.VMEM((rows, 3 * lanes), bf16),
        pltpu.VMEM((rows, features), f32),
        pltpu.VMEM((rank, rows), bf16),
        pltpu.VMEM((rank, rows), f32),
        pltpu.VMEM(share_b, bf16), pltpu.VMEM(share_b, bf16), pltpu.VMEM(share_b, bf16),
        pltpu.VMEM(share_a, bf16), pltpu.VMEM((2 * count - 1, rank, lanes), bf16), pltpu.VMEM(share_a, bf16),
        pltpu.VMEM((cols // tile, rows, tile), bf16),
        pltpu.VMEM((cols // tile, rows, tile), bf16),
        dma((2,)), dma((3,)), dma((3,)), dma((2, chunks)), dma((2, chunks)),
        dma((3, subs)), dma((3, subs)),
        dma((count,)), dma((count,)), dma((count,)), dma((count,)),
        dma((2 * count - 1,)), dma((2 * count - 1,)), dma((2 * count - 1,)), dma((2 * count - 1,)),
        dma((cols // tile,)), dma((cols // tile,)),
    ]
    return pl.pallas_call(
        functools.partial(block_kernel, chunks, rows),
        out_shape=(
            jax.ShapeDtypeStruct((rows, channels), bf16),
            jax.ShapeDtypeStruct((rows, cols), bf16),
            jax.ShapeDtypeStruct((rank, features), f32),
            jax.ShapeDtypeStruct((3, rank, channels), f32),
        ),
        in_specs=[vmem] * 3 + [pl.BlockSpec(memory_space=pl.ANY)] * 2 + [vmem] * 3,
        out_specs=(vmem,) * 4,
        scratch_shapes=scratch,
        compiler_params=pltpu.CompilerParams(
            vmem_limit_bytes=58 << 20, collective_id=3, has_side_effects=True
        ),
        cost_estimate=pl.CostEstimate(
            flops=8 * rows * 3 * channels * features, bytes_accessed=20 << 20, transcendentals=0
        ),
    )(weight.transpose(1, 0, 2), adapter_a.T, adapter_b.transpose(1, 0, 2), tokens, cotangent, short, long, skip)


def body(tokens, weight, adapter_a, adapter_b, short_filter, long_filter, skip_gain, cotangent):
    rows, features = tokens.shape
    share = weight.shape[0]
    channels = weight.shape[2]
    rank = adapter_a.shape[1]
    count = lax.axis_size("ctx")
    fits = (
        count == 8
        and lax.axis_size("groups") == 2
        and rows == SUB * (SEG - 4)
        and long_filter.shape[0] == 4 * PHASE_TAPS
        and short_filter.shape[0] <= BLOCK
        and channels == count * CHUNK_LANES
        and share == 2 * QUARTERS * PIECE
        and features == share * count
    )
    if not fits:
        return general_body(
            tokens, weight, adapter_a, adapter_b, short_filter, long_filter, skip_gain, cotangent
        )
    mixed, grad_tokens, grad_a, grad_b = block(
        weight, adapter_a, adapter_b, tokens, cotangent,
        short_filter.reshape(-1, channels), long_filter, skip_gain.reshape(1, channels), count,
    )
    return mixed, grad_tokens, grad_a.T, grad_b.transpose(1, 0, 2)


def solution(mesh):
    return jax.shard_map(
        body,
        mesh=mesh,
        in_specs=(
            P(("groups", "ctx"), None),
            P("ctx", None, "tp"),
            P(),
            P(None, None, "tp"),
            P(None, None, "tp"),
            P(None, "tp"),
            P("tp"),
            P(("groups", "ctx"), "tp"),
        ),
        out_specs=(
            P(("groups", "ctx"), "tp"),
            P(("groups", "ctx"), "tp"),
            P("groups", None),
            P("groups", None, "tp"),
        ),
        check_vma=False,
    )
```

```python
import functools
import math

import jax
import jax.numpy as jnp
from jax import lax
from jax.experimental import pallas as pl
from jax.experimental.pallas import tpu as pltpu
from jax.sharding import PartitionSpec as P

adapter_scale = 0.03125
LANES = 128
SUB = 8
BLOCK = 16
CHUNK = 32


def shifted(value, axis, steps):
    count = lax.axis_size(axis)
    initial, last = (max(0, -steps), min(count, count - steps))
    return lax.ppermute(value, axis, [(source, source + steps) for source in range(initial, last)])


def tiles(ref, first, count):
    start = first * SUB
    if not isinstance(start, int):
        start = pl.multiple_of(start, SUB)
    return ref[pl.ds(start, count * SUB), :].reshape(count, SUB, LANES)


def put(ref, first, value):
    count = value.shape[0]
    ref[pl.ds(pl.multiple_of(first * SUB, SUB), count * SUB), :] = value.reshape(count * SUB, LANES)


def rounded(value):
    return value.astype(jnp.bfloat16).astype(jnp.float32)


def mixer_kernel(
    rows, halo, packed_ref, cot_ref, short_ref, long_ref, skip_ref, mixed_ref, grad_ref,
    p0, p1, p2, cot, query, keyed, valued, gated, gradf,
):
    channels = SUB * LANES
    short_taps = short_ref.shape[0] // 3
    long_taps = long_ref.shape[0]
    spread = (p0, p1, p2)
    front = halo - long_taps

    @pl.loop(0, (rows + 2 * halo) // BLOCK)
    def _(i):
        at = pl.multiple_of(i * BLOCK, BLOCK)
        for g in range(3):
            for s in range(SUB):
                piece = packed_ref[pl.ds(at, BLOCK), pl.ds(g * channels + s * LANES, LANES)]
                spread[g][pl.ds(at * SUB + s, BLOCK, stride=SUB), :] = piece.astype(jnp.float32)

    @pl.loop(0, (rows + halo) // BLOCK)
    def _(i):
        at = pl.multiple_of(i * BLOCK, BLOCK)
        for s in range(SUB):
            piece = cot_ref[pl.ds(at, BLOCK), pl.ds(s * LANES, LANES)]
            cot[pl.ds(at * SUB + s, BLOCK, stride=SUB), :] = piece.astype(jnp.float32)

    def short(ref, g, first, sign):
        total = None
        for j in range(short_taps):
            term = short_ref[j * 3 + g][None] * tiles(ref, first + sign * j, SUB)
            total = term if total is None else total + term
        return total

    @pl.loop(0, (rows + BLOCK + long_taps) // SUB)
    def _(i):
        at = i * SUB
        key = short(p1, 1, at + front, -1)
        val = short(p2, 2, at + front, -1)
        put(keyed, at, key)
        put(valued, at, val)
        put(gated, at, rounded(key * val))

    @pl.loop(0, (rows + halo) // SUB)
    def _(i):
        at = i * SUB
        que = short(p0, 0, at + halo, -1)
        put(query, at, que)
        put(gradf, at, rounded(que * tiles(cot, at, SUB)))

    zero = tuple(jnp.zeros((SUB, LANES), jnp.float32) for _ in range(BLOCK))

    def long_sum(ref, base, sign):
        def chunk(c, acc):
            acc = list(acc)
            tap0 = c * CHUNK
            origin = base + sign * tap0
            low = origin - (CHUNK - 1) if sign < 0 else origin
            seen = {}

            def at(k):
                if k not in seen:
                    seen[k] = ref[pl.ds(pl.multiple_of((low + k) * SUB, SUB), SUB), :]
                return seen[k]

            for j in range(CHUNK):
                tap = long_ref[tap0 + j]
                for i in range(BLOCK):
                    k = i + (CHUNK - 1) - j if sign < 0 else i + j
                    acc[i] = acc[i] + tap * at(k)
            return tuple(acc)

        return lax.fori_loop(0, long_taps // CHUNK, chunk, zero)

    @pl.loop(0, (rows + BLOCK) // BLOCK)
    def _(b):
        at = b * BLOCK
        skip = skip_ref[...]
        ahead = jnp.stack(long_sum(gated, at + long_taps, -1))
        filtered = ahead + skip[None] * tiles(gated, at + long_taps, BLOCK)
        back = jnp.stack(long_sum(gradf, at, 1))
        grad_gated = back + skip[None] * tiles(gradf, at, BLOCK)
        put(p0, at, rounded(tiles(cot, at, BLOCK) * filtered))
        put(p1, at, rounded(grad_gated * tiles(valued, at + long_taps, BLOCK)))
        put(p2, at, rounded(grad_gated * tiles(keyed, at + long_taps, BLOCK)))
        put(gated, at, tiles(query, at, BLOCK) * filtered)

    results = (query, keyed, valued)

    @pl.loop(0, rows // SUB)
    def _(i):
        at = i * SUB
        for g in range(3):
            put(results[g], at, short(spread[g], g, at, 1))

    @pl.loop(0, rows // BLOCK)
    def _(i):
        at = pl.multiple_of(i * BLOCK, BLOCK)
        for s in range(SUB):
            pick = pl.ds(at * SUB + s, BLOCK, stride=SUB)
            mixed_ref[pl.ds(at, BLOCK), pl.ds(s * LANES, LANES)] = gated[pick, :].astype(jnp.bfloat16)
            for g in range(3):
                grad_ref[pl.ds(at, BLOCK), pl.ds(g * channels + s * LANES, LANES)] = results[g][
                    pick, :
                ].astype(jnp.bfloat16)


def mixer(packed, cot, short_filter, long_filter, skip_gain, rows, halo):
    channels = long_filter.shape[1]
    long_taps = long_filter.shape[0]
    full = (rows + 2 * halo) * SUB
    side = (rows + halo) * SUB
    scratch = [pltpu.VMEM((full, LANES), jnp.float32)] * 3 + [
        pltpu.VMEM((side, LANES), jnp.float32)
    ] * 6
    return pl.pallas_call(
        functools.partial(mixer_kernel, rows, halo),
        out_shape=(
            jax.ShapeDtypeStruct((rows, channels), jnp.bfloat16),
            jax.ShapeDtypeStruct((rows, 3 * channels), jnp.bfloat16),
        ),
        in_specs=[pl.BlockSpec(memory_space=pltpu.VMEM)] * 5,
        out_specs=(pl.BlockSpec(memory_space=pltpu.VMEM),) * 2,
        scratch_shapes=scratch,
        compiler_params=pltpu.CompilerParams(vmem_limit_bytes=52 << 20),
        cost_estimate=pl.CostEstimate(
            flops=4 * rows * channels * (long_taps + 42), bytes_accessed=12 << 20, transcendentals=0
        ),
    )(
        packed,
        cot,
        short_filter.reshape(-1, SUB, LANES),
        long_filter.reshape(long_taps, SUB, LANES),
        skip_gain.reshape(SUB, LANES),
    )


def finish_kernel(
    count, grad_ref, whole_ref, terms_ref, tokens_ref, sums_ref,
    held, total, mate, summed, ready, landed,
    send_one, recv_one, send_two, recv_two, send_tp, recv_tp, send_tok, recv_tok,
):
    me = lax.axis_index("ctx")
    mine = lax.axis_index("tp")
    other = 1 - mine
    width = mate.shape[1]
    cols = tokens_ref.shape[1]
    tile = ready.shape[2]
    steps = cols // tile

    barrier = pltpu.get_barrier_semaphore()
    for d in range(1, count):
        pl.semaphore_signal(
            barrier, inc=1, device_id={"ctx": lax.rem(me + d, count)}, device_id_type=pl.DeviceIdType.MESH
        )
    pl.semaphore_signal(barrier, inc=1, device_id={"tp": other}, device_id_type=pl.DeviceIdType.MESH)
    pl.semaphore_wait(barrier, count)

    first = []
    for d in range(1, count):
        peer = lax.rem(me + d, count)
        first.append(
            pltpu.make_async_remote_copy(
                src_ref=terms_ref.at[peer],
                dst_ref=held.at[d],
                send_sem=send_one.at[d],
                recv_sem=recv_one.at[d],
                device_id={"ctx": peer},
                device_id_type=pl.DeviceIdType.MESH,
            )
        )
        first[-1].start()

    def product(half, t):
        at = pl.multiple_of(half * cols + t * tile, tile)
        return lax.dot_general(
            grad_ref[...],
            whole_ref[pl.ds(at, tile), :],
            (((1,), (1,)), ((), ())),
            preferred_element_type=jnp.float32,
        )

    def token_copy(t):
        return pltpu.make_async_remote_copy(
            src_ref=ready.at[t],
            dst_ref=landed.at[t],
            send_sem=send_tok.at[t],
            recv_sem=recv_tok.at[t],
            device_id={"tp": other},
            device_id_type=pl.DeviceIdType.MESH,
        )

    @pl.loop(0, steps)
    def _(t):
        ready[t] = product(other, t).astype(jnp.bfloat16)
        token_copy(t).start()

    own = terms_ref[me]
    for d in range(1, count):
        first[d - 1].wait()
        own = own + held[d]
    total[...] = own
    tp_copy = pltpu.make_async_remote_copy(
        src_ref=total.at[:, pl.ds(0, width)],
        dst_ref=mate,
        send_sem=send_tp,
        recv_sem=recv_tp,
        device_id={"tp": other},
        device_id_type=pl.DeviceIdType.MESH,
    )
    tp_copy.start()

    def own_tile(t):
        value = product(mine, t)
        token_copy(t).wait()
        at = pl.multiple_of(t * tile, tile)
        tokens_ref[:, pl.ds(at, tile)] = (value + landed[t].astype(jnp.float32)).astype(jnp.bfloat16)

    pl.loop(0, steps // 4)(own_tile)
    tp_copy.wait()
    total[:, pl.ds(0, width)] = total[:, pl.ds(0, width)] + mate[...]
    summed[me] = total[...]
    second = []
    for d in range(1, count):
        second.append(
            pltpu.make_async_remote_copy(
                src_ref=total,
                dst_ref=summed.at[me],
                send_sem=send_two.at[d],
                recv_sem=recv_two.at[d],
                device_id={"ctx": lax.rem(me + d, count)},
                device_id_type=pl.DeviceIdType.MESH,
            )
        )
        second[-1].start()
    pl.loop(steps // 4, steps)(own_tile)
    for copy in second:
        copy.wait()
    sums_ref[...] = summed[...]


def finish(grad_packed, whole, part_a, part_b, count):
    rank, features = part_a.shape
    rows, wide = grad_packed.shape
    width, rest = features // count, wide // count
    cols = features // 2
    tile = 256
    terms = jnp.concatenate(
        [part_a.reshape(rank, count, width), part_b.reshape(rank, count, rest)], axis=2
    ).transpose(1, 0, 2)
    vmem = pl.BlockSpec(memory_space=pltpu.VMEM)
    grad_tokens, sums = pl.pallas_call(
        functools.partial(finish_kernel, count),
        out_shape=(
            jax.ShapeDtypeStruct((rows, cols), jnp.bfloat16),
            jax.ShapeDtypeStruct(terms.shape, jnp.float32),
        ),
        in_specs=[vmem] * 3,
        out_specs=(vmem, vmem),
        scratch_shapes=[
            pltpu.VMEM(terms.shape, jnp.float32),
            pltpu.VMEM((rank, width + rest), jnp.float32),
            pltpu.VMEM((rank, width), jnp.float32),
            pltpu.VMEM(terms.shape, jnp.float32),
            pltpu.VMEM((cols // tile, rows, tile), jnp.bfloat16),
            pltpu.VMEM((cols // tile, rows, tile), jnp.bfloat16),
            pltpu.SemaphoreType.DMA((count,)),
            pltpu.SemaphoreType.DMA((count,)),
            pltpu.SemaphoreType.DMA((count,)),
            pltpu.SemaphoreType.DMA((count,)),
            pltpu.SemaphoreType.DMA,
            pltpu.SemaphoreType.DMA,
            pltpu.SemaphoreType.DMA((cols // tile,)),
            pltpu.SemaphoreType.DMA((cols // tile,)),
        ],
        compiler_params=pltpu.CompilerParams(
            vmem_limit_bytes=48 << 20, collective_id=1, has_side_effects=True
        ),
        cost_estimate=pl.CostEstimate(
            flops=2 * rows * wide * features, bytes_accessed=20 << 20, transcendentals=0
        ),
    )(grad_packed, whole, terms)
    flat = sums.transpose(1, 0, 2)
    return (
        grad_tokens,
        flat[:, :, :width].reshape(rank, features),
        flat[:, :, width:].reshape(rank, wide),
    )


MESH = pl.DeviceIdType.MESH
PIECES = 4


def gather_kernel(
    outer, shard_ref, out_ref, z_send, z_recv, y_send, y_recv, x_send, x_recv, local_sem
):
    me = lax.axis_index("ctx")
    x = lax.axis_index("groups")
    z, y = me // 2, lax.rem(me, 2)
    rows = shard_ref.shape[0]
    piece = rows // PIECES
    half = piece // 2
    last = outer - 2
    steps = outer - 1

    def ctx_of(line, pair):
        return {"ctx": line * 2 + pair}

    def span(line, pair, start, size):
        return pl.ds(pl.multiple_of((line * 2 + pair) * rows + start, half), size)

    def part(p, side):
        return p * piece + side * half

    def copy(src, dst, send, recv, device):
        return pltpu.make_async_remote_copy(
            src_ref=src, dst_ref=dst, send_sem=send, recv_sem=recv, device_id=device, device_id_type=MESH
        )

    def z_range(k, p):
        return (part(p, x), half) if k == last else (p * piece, piece)

    def z_out(way, k, p):
        step = 1 - 2 * way
        start, size = z_range(k, p)
        place = span(z - step * k, y, start, size)
        src = out_ref.at[place] if k else shard_ref.at[pl.ds(pl.multiple_of(start, half), size)]
        return copy(
            src, out_ref.at[place], z_send.at[way, k, p], z_recv.at[way, k, p], ctx_of(z + step, y)
        )

    def z_in(way, k, p):
        step = 1 - 2 * way
        start, size = z_range(k, p)
        place = out_ref.at[span(z - step * (k + 1), y, start, size)]
        return copy(place, place, z_send.at[way, k, p], z_recv.at[way, k, p], ctx_of(z - step, y))

    def sends(way, k):
        return (z < steps) & (z >= k) if way == 0 else (z > 0) & (z + k <= steps)

    def receives(way, k):
        return z > k if way == 0 else z + k < steps

    def line_of(i):
        if i == 0:
            return z
        way, k = (i - 1) // steps, (i - 1) % steps
        return z - (1 - 2 * way) * (k + 1)

    def item(way, k):
        return 1 + way * steps + k

    def y_out(i, p):
        start = part(p, x)
        place = span(line_of(i), y, start, half)
        src = out_ref.at[place] if i else shard_ref.at[pl.ds(pl.multiple_of(start, half), half)]
        return copy(src, out_ref.at[place], y_send.at[i, p], y_recv.at[i, p], ctx_of(z, 1 - y))

    def y_in(i, p):
        place = out_ref.at[span(line_of(i), 1 - y, part(p, x), half)]
        return copy(place, place, y_send.at[i, p], y_recv.at[i, p], ctx_of(z, 1 - y))

    def x_copy(i, p, side):
        if i > 2 * steps:
            line, pair = line_of(item(i - 2 * steps - 1, last)), y
        else:
            line, pair = line_of(i), 1 - y
        place = out_ref.at[span(line, pair, part(p, side), half)]
        return copy(place, place, x_send.at[i, p], x_recv.at[i, p], {"groups": 1 - x})

    def extra(way):
        return 2 * steps + 1 + way

    barrier = pltpu.get_barrier_semaphore()
    pl.semaphore_signal(barrier, inc=1, device_id=ctx_of(z, 1 - y), device_id_type=MESH)
    pl.semaphore_signal(barrier, inc=1, device_id={"groups": 1 - x}, device_id_type=MESH)
    for step in (1, outer - 1):
        pl.semaphore_signal(
            barrier, inc=1, device_id=ctx_of(lax.rem(z + step, outer), y), device_id_type=MESH
        )
    pl.semaphore_wait(barrier, 4)

    @pl.loop(0, PIECES)
    def _(p):
        for way in range(2):
            @pl.when(sends(way, 0))
            def _():
                z_out(way, 0, p).start()
        y_out(0, p).start()

    own = pltpu.make_async_copy(
        shard_ref, out_ref.at[pl.ds(pl.multiple_of(me * rows, rows), rows)], local_sem
    )
    own.start()

    def pass_on(k, p):
        for way in range(2):
            @pl.when(receives(way, k))
            def _():
                i = item(way, k)
                y_in(i, p).wait_recv()
                x_copy(i, p, x).start()

    for k in range(steps):
        @pl.loop(0, PIECES)
        def _(p):
            for way in range(2):
                @pl.when(receives(way, k))
                def _():
                    z_in(way, k, p).wait_recv()
                    if k < last:
                        @pl.when(sends(way, k + 1))
                        def _():
                            z_out(way, k + 1, p).start()
                    y_out(item(way, k), p).start()
                    if k == last:
                        x_copy(extra(way), p, x).start()
            if k == 0:
                y_in(0, p).wait_recv()
                x_copy(0, p, x).start()

            @pl.when(p > 0)
            def _():
                pass_on(k, p - 1)

            if k > 0:
                @pl.when(p == 0)
                def _():
                    pass_on(k - 1, PIECES - 1)

    pass_on(last, PIECES - 1)
    own.wait()

    @pl.loop(0, PIECES)
    def _(p):
        x_copy(0, p, 1 - x).wait_recv()
        x_copy(0, p, x).wait_send()
        y_out(0, p).wait_send()
        for way in range(2):
            for k in range(steps):
                @pl.when(sends(way, k))
                def _():
                    z_out(way, k, p).wait_send()

                @pl.when(receives(way, k))
                def _():
                    i = item(way, k)
                    x_copy(i, p, 1 - x).wait_recv()
                    x_copy(i, p, x).wait_send()
                    y_out(i, p).wait_send()
                    if k == last:
                        x_copy(extra(way), p, 1 - x).wait_recv()
                        x_copy(extra(way), p, x).wait_send()


def gather(merged, count):
    rows, wide = merged.shape
    outer = count // 2
    items = 2 * (outer - 1) + 1
    dma = pltpu.SemaphoreType.DMA
    hbm = pl.BlockSpec(memory_space=pl.ANY)
    return pl.pallas_call(
        functools.partial(gather_kernel, outer),
        out_shape=jax.ShapeDtypeStruct((rows * count, wide), merged.dtype),
        in_specs=[hbm],
        out_specs=hbm,
        scratch_shapes=[
            dma((2, outer - 1, PIECES)),
            dma((2, outer - 1, PIECES)),
            dma((items, PIECES)),
            dma((items, PIECES)),
            dma((items + 2, PIECES)),
            dma((items + 2, PIECES)),
            dma,
        ],
        compiler_params=pltpu.CompilerParams(collective_id=2, has_side_effects=True),
        cost_estimate=pl.CostEstimate(flops=0, bytes_accessed=300 << 20, transcendentals=0),
    )(merged)


def general_body(tokens, weight, adapter_a, adapter_b, short_filter, long_filter, skip_gain, cotangent):
    row_count = tokens.shape[0]
    share_rows = weight.shape[0]
    channels = weight.shape[2]
    features = tokens.shape[1]
    adapter_rank = adapter_a.shape[1]
    halo = long_filter.shape[0] + BLOCK
    count = lax.axis_size("ctx")
    seq_total = row_count * count
    first_row = lax.axis_index("ctx") * share_rows
    before = shifted(tokens[row_count - halo :], "ctx", 1)
    after = shifted(tokens[:halo], "ctx", -1)
    cot_after = shifted(cotangent[:halo], "ctx", -1)
    tokens_ext = jnp.concatenate([before, tokens, after], axis=0)
    cot_ext = jnp.concatenate([cotangent, cot_after], axis=0)
    own_rows = lax.dynamic_slice_in_dim(adapter_a, first_row, share_rows, 0)
    flat_b = adapter_b.reshape(adapter_rank, 3 * channels)
    delta_w = jnp.dot(own_rows, flat_b, preferred_element_type=jnp.float32)
    merged = (
        weight.reshape(share_rows, 3 * channels).astype(jnp.float32) + adapter_scale * delta_w
    ).astype(jnp.bfloat16)
    if count == 8 and lax.axis_size("groups") == 2:
        whole = gather(merged, count)
    else:
        whole = lax.all_gather(merged, "ctx", axis=0, tiled=True)
    packed = jnp.dot(tokens_ext, whole, preferred_element_type=jnp.float32).astype(jnp.bfloat16)
    mixed, grad_packed = mixer(
        packed, cot_ext, short_filter, long_filter, skip_gain, row_count, halo
    )
    projected = jnp.dot(tokens, adapter_a, preferred_element_type=jnp.float32).astype(jnp.bfloat16)
    part_b = lax.dot_general(
        projected, grad_packed, (((0,), (0,)), ((), ())), preferred_element_type=jnp.float32
    )
    through = lax.dot_general(
        flat_b, grad_packed, (((1,), (1,)), ((), ())), preferred_element_type=jnp.float32
    ).astype(jnp.bfloat16)
    part_a = jnp.dot(through, tokens, preferred_element_type=jnp.float32)
    if features % (LANES * count) == 0 and (3 * channels) % (LANES * count) == 0:
        grad_tokens, sum_a, sum_b = finish(grad_packed, whole, part_a, part_b, count)
    else:
        sum_a = lax.psum(part_a, ("ctx", "tp"))
        sum_b = lax.psum(part_b, "ctx")
        partial_grad = lax.dot_general(
            grad_packed, whole, (((1,), (1,)), ((), ())), preferred_element_type=jnp.float32
        )
        grad_tokens = lax.psum_scatter(
            partial_grad.astype(jnp.bfloat16), "tp", scatter_dimension=1, tiled=True
        )
    sum_a = sum_a.T
    factor = adapter_scale / math.sqrt(seq_total)
    return (mixed, grad_tokens, sum_a * factor, (sum_b * factor).reshape(adapter_rank, 3, channels))


CHUNK_LANES = 128
QUARTERS = 4
LAGS = (2, 4, 6, 8)
WHOLE_Z = (1, 3)
HALF_Y = (2,)
PIECE = 32
SEG = 68
COMBOS = 9
PHASE_TAPS = 32
OUT_SEG = 66
OUT_STEP = 11
EDGE = 16


def combine(p):
    p02, p13, p01, p23 = p[0] + p[2], p[1] + p[3], p[0] + p[1], p[2] + p[3]
    return (p[0], p[2], p02, p[1], p[3], p13, p01, p23, p01 + p23)


def block_kernel(
    chunks, rows,
    weight_ref, down_ref, wide_ref, tokens_hbm, cot_hbm, short_ref, long_ref, skip_ref,
    mixed_ref, tokgrad_ref, grad_a_ref, grad_b_ref,
    up_ref, tokens_ref, cot_ref, hold_g, hold_f, edge_g, edge_f,
    whole, pk0, pk1, pk2, cot, keyed, valued, gated, query, gradf, gs0, gs1, gs2, mix,
    comb, taps, sub, gp, acc, proj, through, terms_b, held_b, sum_b, terms_a, held_a, sum_a, ready, landed,
    load_sem, near_send, near_recv, edge_send, edge_recv,
    sent, came, send_b, recv_b, back_b, done_b, send_a, recv_a, back_a, done_a, send_tok, recv_tok,
):
    me = lax.axis_index("ctx")
    x = lax.axis_index("groups")
    mine = lax.axis_index("tp")
    other = 1 - mine
    z, y = me // 2, lax.rem(me, 2)
    count = chunks
    lines = count // 2
    subs = chunks * QUARTERS
    lanes = CHUNK_LANES
    f32, bf16 = jnp.float32, jnp.bfloat16
    pk = (pk0, pk1, pk2)
    long_taps = long_ref.shape[0]
    short_taps = short_ref.shape[0] // 3
    channels = chunks * lanes
    halo = EDGE
    has_next, has_last = me < count - 1, me > 0
    to_next = {"ctx": lax.rem(me + 1, count)}
    to_last = {"ctx": lax.rem(me + count - 1, count)}

    loads = (
        pltpu.make_async_copy(tokens_hbm, tokens_ref.at[pl.ds(halo, rows)], load_sem.at[0]),
        pltpu.make_async_copy(cot_hbm, cot_ref.at[pl.ds(0, rows)], load_sem.at[1]),
    )
    for copy in loads:
        copy.start()

    barrier = pltpu.get_barrier_semaphore()
    for d in range(1, count):
        pl.semaphore_signal(
            barrier, inc=1, device_id={"ctx": lax.rem(me + d, count)}, device_id_type=MESH
        )
    pl.semaphore_signal(barrier, inc=1, device_id={"tp": other}, device_id_type=MESH)
    for d in range(1, count):
        pl.semaphore_signal(
            barrier, inc=1, device_id={"ctx": lax.rem(me + d, count), "tp": other}, device_id_type=MESH
        )
    pl.semaphore_signal(barrier, inc=1, device_id={"groups": 1 - x}, device_id_type=MESH)

    def merge(c):
        own = pl.ds(pl.multiple_of(me * weight_ref.shape[1], weight_ref.shape[1]), weight_ref.shape[1])
        delta = lax.dot_general(
            down_ref[:, own], up_ref[c], (((0,), (0,)), ((), ())), preferred_element_type=f32
        )
        for g in range(3):
            value = weight_ref[g, :, c * lanes : (c + 1) * lanes].astype(f32) + adapter_scale * delta[:, g * lanes : (g + 1) * lanes]
            whole[c, z, y, :, :, :, pl.ds(g * lanes, lanes)] = value.astype(bf16).reshape(
                QUARTERS, 2, PIECE, lanes
            )

    def send(ref, sub_at, stage, device):
        pltpu.make_async_remote_copy(
            src_ref=ref, dst_ref=ref, send_sem=sent.at[stage, sub_at], recv_sem=came.at[stage, sub_at],
            device_id=device, device_id_type=MESH,
        ).start()

    def whole_wait(ref, sub_at, stage):
        return pltpu.make_async_remote_copy(
            src_ref=ref, dst_ref=ref, send_sem=sent.at[stage, sub_at], recv_sem=came.at[stage, sub_at],
            device_id={"tp": other}, device_id_type=MESH,
        )

    def arrived(ref, sub_at, stage):
        whole_wait(ref, sub_at, stage).wait_recv()

    def line(d):
        return lax.rem(z + d, lines)

    side = z // 2
    inner = lax.rem(z + side, 2) == 1
    outer = jnp.logical_not(inner)
    beside = z + 1 - 2 * lax.rem(z, 2)
    across = 2 - side
    to_x = {"groups": 1 - x}
    to_y = {"ctx": z * 2 + 1 - y}
    to_beside = {"ctx": beside * 2 + y}

    def z_blocks(q, many):
        if q in WHOLE_Z:
            return whole.at[0, 0, 0, pl.ds(0, many)]
        return whole.at[pl.ds(0, many), 0, 0, 0, 0]

    def stage0(c, q):
        n = c * QUARTERS + q
        ref = whole.at[c, z, y, q] if q in WHOLE_Z else whole.at[c, z, y, q, x]
        send(ref, n, 0, {"ctx": across * 2 + y})
        send(ref, n, 0, to_beside)

    def stage0b(c, q):
        n = c * QUARTERS + q

        @pl.when(inner)
        def _():
            arrived(z_blocks(q, 3), n, 0)
            far = pl.ds(2 - 2 * side, 2)
            send(whole.at[c, far, y, q] if q in WHOLE_Z else whole.at[c, far, y, q, x], n, 0, to_beside)

    def stage1(c, q):
        n = c * QUARTERS + q
        pl.when(outer)(lambda: arrived(z_blocks(q, 3), n, 0))
        if q not in WHOLE_Z:
            for d in range(1, lines):
                send(whole.at[c, line(d), y, q, x], n, 1, to_x)
        send(whole.at[c, :, y, q, x], n, 1, to_y)

    def stage2(c, q):
        n = c * QUARTERS + q
        arrived(whole.at[pl.ds(0, stage1_blocks(q)), 0, 0, 0, 0], n, 1)
        if q not in HALF_Y:
            send(whole.at[c, :, 1 - y, q, x], n, 2, to_x)
        else:
            half = PIECE // 2
            send(whole.at[c, :, 1 - y, q, x, pl.ds(0, half)], n, 2, to_x)
            send(whole.at[c, :, y, q, 1 - x, pl.ds(half, half)], n, 2, to_y)

    def stage1_blocks(q):
        return lines if q in WHOLE_Z else 2 * lines - 1

    def slot(base, off):
        for stage, back in zip((stage0, stage2, stage1, stage0b), (0, LAGS[2], LAGS[1], LAGS[0])):
            at = off - back
            if at < 0:
                continue
            c, q = base + at // QUARTERS, at % QUARTERS
            if isinstance(base, int):
                stage(c, q)
            else:
                pl.when(c < chunks)(functools.partial(stage, c, q))

    def near(k):
        src, dst, device = (
            (tokens_hbm.at[pl.ds(rows - halo, halo)], tokens_ref.at[pl.ds(0, halo)], to_next),
            (tokens_hbm.at[pl.ds(0, halo)], tokens_ref.at[pl.ds(rows + halo, halo)], to_last),
            (cot_hbm.at[pl.ds(0, halo)], cot_ref.at[pl.ds(rows, halo)], to_last),
        )[k]
        return pltpu.make_async_remote_copy(
            src_ref=src, dst_ref=dst, send_sem=near_send.at[k], recv_sem=near_recv.at[k],
            device_id=device, device_id_type=MESH,
        )

    def edge(k, c):
        src, dst, device = ((hold_g, edge_g, to_next), (hold_f, edge_f, to_last))[k]
        return pltpu.make_async_remote_copy(
            src_ref=src.at[c], dst_ref=dst.at[c], send_sem=edge_send.at[k, c],
            recv_sem=edge_recv.at[k, c], device_id=device, device_id_type=MESH,
        )

    for c in range(chunks):
        for g in range(3):
            up_ref[c, :, g * lanes : (g + 1) * lanes] = wide_ref[g, :, c * lanes : (c + 1) * lanes]
    merge(0)
    pl.semaphore_wait(barrier, 2 * count)

    first_slots = LAGS[3] + QUARTERS - 1
    body_rows = pl.ds(halo, rows)
    for n in range(first_slots):
        slot(0, n)
        if n + 1 < chunks:
            merge(n + 1)
        if n == 0:
            pl.when(has_next)(lambda: near(0).start())

            @pl.when(has_last)
            def _():
                near(1).start()
                near(2).start()

            @pl.when(jnp.logical_not(has_last))
            def _():
                tokens_ref[pl.ds(0, halo), :] = jnp.zeros((halo, tokens_ref.shape[1]), bf16)
                edge_g[...] = jnp.zeros_like(edge_g)

            @pl.when(jnp.logical_not(has_next))
            def _():
                tokens_ref[pl.ds(rows + halo, halo), :] = jnp.zeros((halo, tokens_ref.shape[1]), bf16)
                cot_ref[pl.ds(rows, halo), :] = jnp.zeros((halo, channels), bf16)
                edge_f[...] = jnp.zeros_like(edge_f)

            tail = cot_ref.shape[0] - rows - halo
            cot_ref[pl.ds(rows + halo, tail), :] = jnp.zeros((tail, channels), bf16)
            known = rows + halo
            for ref in (query, keyed, valued):
                ref[pl.ds(known, ref.shape[0] - known), :] = jnp.zeros((ref.shape[0] - known, lanes), f32)
            after = gated.shape[0] - known - long_taps
            gated[pl.ds(known + long_taps, after), :] = jnp.zeros((after, lanes), f32)
            after = gradf.shape[0] - rows - edge_f.shape[1]
            gradf[pl.ds(rows + edge_f.shape[1], after), :] = jnp.zeros((after, lanes), f32)
        if n == first_slots - 2:
            for copy in loads:
                copy.wait()
            proj[...] = lax.dot_general(
                down_ref[...], tokens_ref[body_rows, :], (((1,), (1,)), ((), ())),
                preferred_element_type=f32,
            ).astype(bf16)
            through[...] = jnp.zeros_like(through)
        if n == first_slots - 1:
            acc[...] = jnp.zeros_like(acc)

            @pl.when(has_last)
            def _():
                near(0).wait_recv()
                near(1).wait_send()
                near(2).wait_send()

            @pl.when(has_next)
            def _():
                near(0).wait_send()
                near(1).wait_recv()
                near(2).wait_recv()

    def spread(row, count_rows):
        return jnp.broadcast_to(row, (count_rows, lanes))

    def short(ref, g, cols, first, sign, size, stride):
        seen = {}

        def at(k):
            if k not in seen:
                seen[k] = ref[pl.ds(first + k, SUB, stride=stride), :]
            return seen[k]

        result = [None] * size
        for j in range(short_taps):
            tap = spread(short_ref[j * 3 + g : j * 3 + g + 1, cols], SUB)
            for i in range(size):
                term = tap * at(i + sign * j)
                result[i] = term if j == 0 else result[i] + term
        return result

    def packed_grad(c):
        cols = pl.ds(c * lanes if isinstance(c, int) else pl.multiple_of(c * lanes, lanes), lanes)

        @pl.loop(0, OUT_SEG // OUT_STEP)
        def _(b):
            for g, ref in enumerate((gs0, gs1, gs2)):
                value = short(ref, g, cols, b * OUT_STEP, 1, OUT_STEP, OUT_SEG)
                for i in range(OUT_STEP):
                    pk[g][pl.ds(b * OUT_STEP + i, SUB, stride=OUT_SEG), :] = value[i]

        @pl.loop(0, rows // BLOCK)
        def _(i):
            here = pl.ds(pl.multiple_of(i * BLOCK, BLOCK), BLOCK)
            mixed_ref[here, cols] = mix[here, :].astype(bf16)
            for g in range(3):
                gp[here, pl.ds(g * lanes, lanes)] = pk[g][here, :].astype(bf16)

    def to_owner(c):
        return pltpu.make_async_remote_copy(
            src_ref=terms_b.at[c], dst_ref=held_b.at[me], send_sem=send_b.at[c], recv_sem=recv_b.at[me],
            device_id={"ctx": c}, device_id_type=MESH,
        )

    def peer_of(d):
        return lax.rem(me + d, count)

    def sum_share():
        value = terms_b[me].astype(f32)
        for d in range(1, count):
            peer = peer_of(d)
            pltpu.make_async_remote_copy(
                src_ref=held_b.at[peer], dst_ref=held_b.at[peer], send_sem=send_b.at[peer],
                recv_sem=recv_b.at[peer], device_id={"ctx": peer}, device_id_type=MESH,
            ).wait_recv()
            value = value + held_b[peer].astype(f32)
        sum_b[me] = value.astype(bf16)
        for d in range(1, count):
            share_back(d).start()

    def share_back(d):
        return pltpu.make_async_remote_copy(
            src_ref=sum_b.at[me], dst_ref=sum_b.at[me], send_sem=back_b.at[d], recv_sem=done_b.at[me],
            device_id={"ctx": peer_of(d)}, device_id_type=MESH,
        )

    def adapter_terms(c):
        terms_b[c] = jnp.dot(proj[...], gp[...], preferred_element_type=f32).astype(bf16)

        @pl.when(me != c)
        def _():
            to_owner(c).start()

        through[...] += lax.dot_general(
            up_ref[c], gp[...], (((1,), (1,)), ((), ())), preferred_element_type=f32
        )

    def token_terms(c, k, pair):
        block = whole[c, k, pair].reshape(-1, 3 * lanes)
        wide = block.shape[0]
        start = (k * 2 + pair) * wide
        at = pl.ds(start if isinstance(start, int) else pl.multiple_of(start, wide), wide)
        value = acc[:, at] + lax.dot_general(
            gp[...], block, (((1,), (1,)), ((), ())), preferred_element_type=f32
        )
        acc[:, at] = value
        return value

    def token_copy(t):
        return pltpu.make_async_remote_copy(
            src_ref=ready.at[t], dst_ref=landed.at[t], send_sem=send_tok.at[t],
            recv_sem=recv_tok.at[t], device_id={"tp": other}, device_id_type=MESH,
        )

    def chunk_step(c):
        cols = pl.ds(pl.multiple_of(c * lanes, lanes), lanes)

        slot(c, first_slots)
        for q in range(QUARTERS):
            arrived(whole.at[pl.ds(0, lines), 0, 0, 0, 0], c * QUARTERS + q, 2)
        ext = tokens_ref.shape[0]
        part = ext // 2

        @pl.loop(0, 2)
        def _(r):
            at = pl.ds(pl.multiple_of(r * part, 16), part)
            value = jnp.dot(
                tokens_ref[at, :], whole[c].reshape(-1, 3 * lanes), preferred_element_type=f32
            )
            for g in range(3):
                pk[g][at, :] = rounded(value[:, g * lanes : (g + 1) * lanes])

        slot(c, first_slots + 1)

        @pl.loop(0, cot.shape[0] // BLOCK)
        def _(i):
            here = pl.ds(pl.multiple_of(i * BLOCK, BLOCK), BLOCK)
            cot[here, :] = cot_ref[here, cols].astype(f32)

        @pl.loop(0, OUT_SEG // OUT_STEP)
        def _(b):
            at = b * OUT_STEP
            key = short(pk1, 1, cols, at + halo, -1, OUT_STEP, OUT_SEG)
            val = short(pk2, 2, cols, at + halo, -1, OUT_STEP, OUT_SEG)
            for i in range(OUT_STEP):
                here = pl.ds(at + i, SUB, stride=OUT_SEG)
                keyed[here, :] = key[i]
                valued[here, :] = val[i]
                gated[pl.ds(at + i + long_taps, SUB, stride=OUT_SEG), :] = rounded(key[i] * val[i])
            que = short(pk0, 0, cols, at + halo, -1, OUT_STEP, OUT_SEG)
            for i in range(OUT_STEP):
                here = pl.ds(at + i, SUB, stride=OUT_SEG)
                query[here, :] = que[i]
                gradf[here, :] = rounded(que[i] * cot[here, :])

        hold_g[c] = gated[pl.ds(rows, long_taps), :].astype(bf16)
        hold_f[c] = gradf[pl.ds(0, edge_f.shape[1]), :].astype(bf16)
        pl.when(has_next)(lambda: edge(0, c).start())
        pl.when(has_last)(lambda: edge(1, c).start())

        @pl.when(c > 0)
        def _():
            packed_grad(c - 1)

        slot(c, first_slots + 2)

        @pl.when(c > 0)
        def _():
            adapter_terms(c - 1)
            pl.when(c - 2 == me)(sum_share)
            for k in range(lines):
                for pair in range(2):
                    token_terms(c - 1, k, pair)

        slot(c, first_slots + 3)

        @pl.loop(0, long_taps // SUB)
        def _(k):
            piece = long_ref[pl.ds(pl.multiple_of(k * SUB, SUB), SUB), cols]
            for h in range(2):
                p = [spread(piece[4 * h + i : 4 * h + i + 1], SUB) for i in range(4)]
                at = pl.ds(pl.multiple_of((2 * k + h) * SUB, SUB), SUB)
                for e, value in enumerate(combine(p)):
                    taps[e, at, :] = value

        pl.when(has_last)(lambda: edge(0, c).wait_recv())
        pl.when(has_next)(lambda: edge(1, c).wait_recv())
        gated[pl.ds(0, long_taps), :] = edge_g[c].astype(f32)
        gradf[pl.ds(rows, edge_f.shape[1]), :] = edge_f[c].astype(f32)

        span = PHASE_TAPS + SEG // 4

        @pl.loop(0, span)
        def _(k):
            at = pl.ds(pl.multiple_of(k * SUB, SUB), SUB)
            ahead = [gated[pl.ds(4 * k + i, SUB, stride=OUT_SEG), :] for i in range(4)]
            last = long_taps + SEG - 1
            back = [gradf[pl.ds(last - 4 * k - i, SUB, stride=OUT_SEG), :] for i in range(4)]
            for e, value in enumerate(combine(ahead) + combine(back)):
                comb[e, at, :] = value

        outs = SEG // 4 + 1

        @pl.loop(0, 2 * COMBOS)
        def _(e):
            te = lax.rem(e, COMBOS)
            sums = [None] * outs
            seen = {}
            for k in range(PHASE_TAPS):
                weight = taps[te, k * SUB : (k + 1) * SUB, :]
                for n in range(outs):
                    at = n + PHASE_TAPS - 1 - k
                    if at not in seen:
                        seen[at] = comb[e, at * SUB : (at + 1) * SUB, :]
                    term = weight * seen[at]
                    sums[n] = term if sums[n] is None else sums[n] + term
            for n in range(outs):
                sub[e, n * SUB : (n + 1) * SUB, :] = sums[n]

        skip = spread(skip_ref[:, cols], SUB)

        def finish_rows(first_n, many):
            jobs = []
            for m in range(many):
                n = first_n + m
                before = pl.ds(n * SUB if isinstance(n, int) else pl.multiple_of(n * SUB, SUB), SUB)
                now = pl.ds((n + 1) * SUB if isinstance(n, int) else pl.multiple_of((n + 1) * SUB, SUB), SUB)
                jobs.append(([sub[e, now, :] for e in range(2 * COMBOS)],
                             {e: sub[e, before, :] for e in (1, 3, 4, 5, 7, 10, 12, 13, 14, 16)}))
            at = lambda ref, start: ref[pl.ds(start, SUB, stride=OUT_SEG), :]
            order = [(4 * (first_n + m) + i) for m in range(many) for i in range(4)]
            ahead = [(at(gated, long_taps + k), at(cot, k), at(query, k)) for k in order]
            back = [
                (at(gradf, SEG - 1 - k), at(valued, SEG - 1 - k), at(keyed, SEG - 1 - k)) for k in order
            ]

            def outputs(now, before, e):
                def pair(p):
                    v0, v1, v2 = now[e + p], now[e + p + 1], now[e + p + 2]
                    return v0 + before[e + p + 1], v2 - v0 - v1

                a_e, a_o = pair(0)
                b_e, b_o = now[e + 3] + before[e + 4], now[e + 5] - now[e + 3] - now[e + 4]
                c_e, c_o = pair(6)
                b_was = before[e + 5] - before[e + 3] - before[e + 4]
                return [a_e + b_was, c_e - a_e - b_e, a_o + b_e, c_o - a_o - b_o]

            forward, backward = [], []
            for now, before in jobs:
                forward += outputs(now, before, 0)
                backward += outputs(now, before, COMBOS)
            stores = []
            for k, value, (gate, ct, que) in zip(order, forward, ahead):
                filtered = value + skip * gate
                stores += [(gs0, k, rounded(ct * filtered)), (mix, k, que * filtered)]
            for k, value, (gf, val, key) in zip(order, backward, back):
                grad_gated = value + skip * gf
                stores += [
                    (gs1, SEG - 1 - k, rounded(grad_gated * val)), (gs2, SEG - 1 - k, rounded(grad_gated * key))
                ]
            for ref, k, value in stores:
                ref[pl.ds(k, SUB, stride=OUT_SEG), :] = value

        pl.loop(0, SEG // 8)(lambda n: finish_rows(2 * n, 2))
        finish_rows(SEG // 4 - 1, 1)

    pl.loop(0, chunks)(chunk_step)

    cols = tokgrad_ref.shape[1]
    tile = ready.shape[2]
    steps = cols // tile
    width = 2 * lanes
    packed_grad(chunks - 1)
    adapter_terms(chunks - 1)
    part_a = jnp.dot(through[...].astype(bf16), tokens_ref[body_rows, :], preferred_element_type=f32)
    for p in range(count):
        for t in range(2):
            at = p * width + t * lanes
            terms_a[p, t] = part_a[:, at : at + lanes].astype(bf16)

    pairs = [(d, h) for h in range(2) for d in range(count) if (d, h) != (0, 0)]

    def a_copy(src, dst, k, d, h, send, recv):
        return pltpu.make_async_remote_copy(
            src_ref=src, dst_ref=dst, send_sem=send.at[k], recv_sem=recv.at[k],
            device_id={"ctx": peer_of(d), "tp": other if h else mine}, device_id_type=MESH,
        )

    first = [
        a_copy(terms_a.at[peer_of(d), other if h else mine], held_a.at[k], k, d, h, send_a, recv_a)
        for k, (d, h) in enumerate(pairs)
    ]
    for copy in first:
        copy.start()
    half_lines = lines // 2
    for t in range(steps):
        value = token_terms(chunks - 1, other * half_lines + t // 2, t % 2)
        ready[t] = value.astype(bf16)
        token_copy(t).start()
    pl.when(me >= chunks - 2)(sum_share)
    own = terms_a[me, mine].astype(f32)
    for k, copy in enumerate(first):
        copy.wait()
        own = own + held_a[k].astype(f32)
    sum_a[me, mine] = own.astype(bf16)
    second = [
        a_copy(sum_a.at[me, mine], sum_a.at[me, mine], k, d, h, back_a, done_a)
        for k, (d, h) in enumerate(pairs)
    ]
    for copy in second:
        copy.start()
    for t in range(steps):
        token_terms(chunks - 1, mine * half_lines + t // 2, t % 2)

    @pl.loop(0, steps)
    def _(t):
        token_copy(t).wait()
        at = pl.multiple_of(t * tile, tile)
        from_at = pl.multiple_of(mine * cols + t * tile, tile)
        tokgrad_ref[:, pl.ds(at, tile)] = (
            acc[:, pl.ds(from_at, tile)] + landed[t].astype(f32)
        ).astype(bf16)

    @pl.loop(0, chunks)
    def _(c):
        for q in range(QUARTERS):
            n = c * QUARTERS + q
            pl.when(inner)(lambda: whole_wait(z_blocks(q, 4), n, 0).wait_send())
            pl.when(outer)(lambda: whole_wait(z_blocks(q, 2), n, 0).wait_send())
            whole_wait(whole.at[pl.ds(0, stage1_blocks(q)), 0, 0, 0, 0], n, 1).wait_send()
            whole_wait(whole.at[pl.ds(0, lines), 0, 0, 0, 0], n, 2).wait_send()

    @pl.when(has_next)
    def _():
        for c in range(chunks):
            edge(0, c).wait_send()

    @pl.when(has_last)
    def _():
        for c in range(chunks):
            edge(1, c).wait_send()

    for c in range(chunks):
        @pl.when(me != c)
        def _():
            to_owner(c).wait_send()
            pltpu.make_async_remote_copy(
                src_ref=sum_b.at[c], dst_ref=sum_b.at[c], send_sem=back_b.at[0], recv_sem=done_b.at[c],
                device_id={"ctx": c}, device_id_type=MESH,
            ).wait_recv()

    for d in range(1, count):
        share_back(d).wait_send()
    for copy in second:
        copy.wait()
    factor = adapter_scale / math.sqrt(rows * count)
    for p in range(count):
        for t in range(2):
            at = p * width + t * lanes
            grad_a_ref[:, at : at + lanes] = sum_a[p, t].astype(f32) * factor
        for g in range(3):
            grad_b_ref[g, :, p * lanes : (p + 1) * lanes] = (
                sum_b[p, :, g * lanes : (g + 1) * lanes].astype(f32) * factor
            )


def block(weight, adapter_a, adapter_b, tokens, cotangent, short, long, skip, count):
    rank = adapter_a.shape[1]
    rows, features = tokens.shape
    channels = long.shape[1]
    chunks = channels // CHUNK_LANES
    lanes = CHUNK_LANES
    cols = features // 2
    tile = 256
    vmem = pl.BlockSpec(memory_space=pltpu.VMEM)
    f32, bf16 = jnp.float32, jnp.bfloat16
    seg_rows = SUB * SEG
    reach = seg_rows + long.shape[0]
    plain = lambda n: pltpu.VMEM((n, lanes), f32)
    dma = pltpu.SemaphoreType.DMA
    subs = chunks * QUARTERS
    share_b, share_a = (count, rank, 3 * lanes), (count, 2, rank, lanes)
    reach_back = long.shape[0] + EDGE
    scratch = [
        pltpu.VMEM((chunks, rank, 3 * lanes), bf16),
        pltpu.VMEM((rows + 2 * EDGE, features), bf16),
        pltpu.VMEM((seg_rows, channels), bf16),
        pltpu.VMEM((chunks, long.shape[0], lanes), bf16),
        pltpu.VMEM((chunks, reach_back, lanes), bf16),
        pltpu.VMEM((chunks, long.shape[0], lanes), bf16),
        pltpu.VMEM((chunks, reach_back, lanes), bf16),
        pltpu.VMEM((chunks, count // 2, 2, QUARTERS, 2, PIECE, 3 * lanes), bf16),
        plain(rows + 2 * EDGE), plain(rows + 2 * EDGE), plain(rows + 2 * EDGE),
        plain(seg_rows), plain(seg_rows), plain(seg_rows), plain(reach), plain(seg_rows), plain(reach),
        plain(seg_rows), plain(seg_rows), plain(seg_rows), plain(seg_rows),
        pltpu.VMEM((2 * COMBOS, (PHASE_TAPS + SEG // 4) * SUB, lanes), f32),
        pltpu.VMEM((COMBOS, PHASE_TAPS * SUB, lanes), f32),
        pltpu.VMEM((2 * COMBOS, (SEG // 4 + 1) * SUB, lanes), f32),
        pltpu.VMEM((rows, 3 * lanes), bf16),
        pltpu.VMEM((rows, features), f32),
        pltpu.VMEM((rank, rows), bf16),
        pltpu.VMEM((rank, rows), f32),
        pltpu.VMEM(share_b, bf16), pltpu.VMEM(share_b, bf16), pltpu.VMEM(share_b, bf16),
        pltpu.VMEM(share_a, bf16), pltpu.VMEM((2 * count - 1, rank, lanes), bf16), pltpu.VMEM(share_a, bf16),
        pltpu.VMEM((cols // tile, rows, tile), bf16),
        pltpu.VMEM((cols // tile, rows, tile), bf16),
        dma((2,)), dma((3,)), dma((3,)), dma((2, chunks)), dma((2, chunks)),
        dma((3, subs)), dma((3, subs)),
        dma((count,)), dma((count,)), dma((count,)), dma((count,)),
        dma((2 * count - 1,)), dma((2 * count - 1,)), dma((2 * count - 1,)), dma((2 * count - 1,)),
        dma((cols // tile,)), dma((cols // tile,)),
    ]
    return pl.pallas_call(
        functools.partial(block_kernel, chunks, rows),
        out_shape=(
            jax.ShapeDtypeStruct((rows, channels), bf16),
            jax.ShapeDtypeStruct((rows, cols), bf16),
            jax.ShapeDtypeStruct((rank, features), f32),
            jax.ShapeDtypeStruct((3, rank, channels), f32),
        ),
        in_specs=[vmem] * 3 + [pl.BlockSpec(memory_space=pl.ANY)] * 2 + [vmem] * 3,
        out_specs=(vmem,) * 4,
        scratch_shapes=scratch,
        compiler_params=pltpu.CompilerParams(
            vmem_limit_bytes=58 << 20, collective_id=3, has_side_effects=True
        ),
        cost_estimate=pl.CostEstimate(
            flops=8 * rows * 3 * channels * features, bytes_accessed=20 << 20, transcendentals=0
        ),
    )(weight.transpose(1, 0, 2), adapter_a.T, adapter_b.transpose(1, 0, 2), tokens, cotangent, short, long, skip)


def body(tokens, weight, adapter_a, adapter_b, short_filter, long_filter, skip_gain, cotangent):
    rows, features = tokens.shape
    share = weight.shape[0]
    channels = weight.shape[2]
    rank = adapter_a.shape[1]
    count = lax.axis_size("ctx")
    fits = (
        count == 8
        and lax.axis_size("groups") == 2
        and rows == SUB * (SEG - 4)
        and long_filter.shape[0] == 4 * PHASE_TAPS
        and short_filter.shape[0] <= BLOCK
        and channels == count * CHUNK_LANES
        and share == 2 * QUARTERS * PIECE
        and features == share * count
    )
    if not fits:
        return general_body(
            tokens, weight, adapter_a, adapter_b, short_filter, long_filter, skip_gain, cotangent
        )
    mixed, grad_tokens, grad_a, grad_b = block(
        weight, adapter_a, adapter_b, tokens, cotangent,
        short_filter.reshape(-1, channels), long_filter, skip_gain.reshape(1, channels), count,
    )
    return mixed, grad_tokens, grad_a.T, grad_b.transpose(1, 0, 2)


def solution(mesh):
    return jax.shard_map(
        body,
        mesh=mesh,
        in_specs=(
            P(("groups", "ctx"), None),
            P("ctx", None, "tp"),
            P(),
            P(None, None, "tp"),
            P(None, None, "tp"),
            P(None, "tp"),
            P("tp"),
            P(("groups", "ctx"), "tp"),
        ),
        out_specs=(
            P(("groups", "ctx"), "tp"),
            P(("groups", "ctx"), "tp"),
            P("groups", None),
            P("groups", None, "tp"),
        ),
        check_vma=False,
    )
```
